32 devices in a mesh: pp: 4 (over y, x), cp: 2 (over core), tp: 4 (over z).
Axes of the slice: x: 2, y: 2, z: 4, core: 2. Of those that a mesh axis runs over, the one named last changes fastest.
Arguments:
- query: bfloat16 [4, 384, 8192], P('pp', 'cp', 'tp'), may hold values from -125 to 125
- keys: bfloat16 [4, 384, 512], P('pp', 'cp', 'tp'), may hold values from -5 to 5
- values: bfloat16 [4, 384, 512], P('pp', 'cp', 'tp'), may hold values from -6 to 6
- attn_out: bfloat16 [4, 384, 8192], P('pp', 'cp', 'tp'), may hold values from -6 to 6
- grad_out: bfloat16 [4, 384, 8192], P('pp', 'cp', 'tp'), may hold values from -192 to 192
- span_pairs: int32 [2, 2], replicated, may hold values from 0 to 3, as said below
Outputs:
- key_grad: bfloat16 [4, 384, 512], P('pp', 'cp', 'tp')
- value_grad: bfloat16 [4, 384, 512], P('pp', 'cp', 'tp')
- upstream_grad: bfloat16 [4, 384, 8192], P('pp', 'cp', 'tp')
The draws below stay inside these ranges and needn't reach their ends.
Inputs may be any that keep to these rules, and one draw needn't show every extreme that they name: `span_pairs`: row r names the two spans of 96 positions held by context rank r, in either order; every span is named once.
All inputs are finite; a program needn't handle non-finite values.
Results may differ from the reference program's by a relative error of at most 0.0052.
Values may be sent and summed in bfloat16 or wider, within the bound.
A program may use at most 64 MiB of HBM per device.

```python
import math
import jax
import jax.numpy as jnp
from jax import lax

HEAD_DIM = 128
GROUP = 16
TOK_DEV = 192
SPAN = 96
TOKENS = 384
SPANS = 4
SECTIONS = 4
KV_HEADS = 4
Q_HEADS = 64


def draw_both(key):
    base = jax.random.fold_in(key, 4242)
    first, second = jax.random.split(base, 2)
    query_all = jnp.clip(jax.random.normal(first, (SECTIONS, TOKENS, Q_HEADS, HEAD_DIM), jnp.float32), -5.0, 5.0)
    key_all = jnp.clip(jax.random.normal(second, (SECTIONS, TOKENS, KV_HEADS, HEAD_DIM), jnp.float32), -5.0, 5.0)
    return (query_all, key_all)


def draw_query(key, part):
    query_all, key_all = draw_both(key)
    return query_all.reshape(SECTIONS, TOKENS, Q_HEADS * HEAD_DIM).astype(jnp.bfloat16)


def draw_keys(key, part):
    query_all, key_all = draw_both(key)
    return key_all.reshape(SECTIONS, TOKENS, KV_HEADS * HEAD_DIM).astype(jnp.bfloat16)


def draw_span_pairs(key, part):
    order = jax.random.permutation(jax.random.fold_in(key, 99), SPANS).astype(jnp.int32)
    return order.reshape(SPANS // 2, 2).astype(jnp.int32)


def steps_of(stream_key, shape, cuts, least, largest):
    factor_of, own = 1.0, jax.random.fold_in(stream_key, 6)
    for dim, shards_of in cuts:
        steps = jnp.exp(jax.random.uniform(jax.random.fold_in(own, dim), (shards_of,), jnp.float32, least / len(cuts), largest / len(cuts)))
        factor_of = factor_of * jnp.repeat(steps, shape[dim] // shards_of).reshape([-1 if axis == dim else 1 for axis in range(len(shape))])
    return factor_of


def scatter_about(own_key, extent, scale, reach, pieces=(), kind=jnp.bfloat16):
    gain = steps_of(own_key, extent, pieces, -0.22, 0.18) if pieces else 1.0
    entries = jax.random.normal(own_key, extent, jnp.float32) * scale * gain
    return jnp.minimum(jnp.maximum(entries, -reach), reach).astype(kind)


def setup_inputs(seed: int = 0) -> dict:
    splits = jax.random.split(jax.random.key(seed), 7)
    query = draw_query(jax.random.fold_in(splits[6], 71), 0)
    keys = draw_keys(jax.random.fold_in(splits[6], 71), 0)
    values = scatter_about(splits[2], (SECTIONS, TOKENS, KV_HEADS * HEAD_DIM), 1.0, 6.0, ((0, 4), (1, 2), (2, 4)))
    attn_out = scatter_about(splits[3], (SECTIONS, TOKENS, Q_HEADS * HEAD_DIM), 1.0, 6.0, ((0, 4), (1, 2), (2, 4)))
    grad_out = scatter_about(splits[4], (SECTIONS, TOKENS, Q_HEADS * HEAD_DIM), 32.0, 192.0, ((0, 4), (1, 2), (2, 4)))
    span_pairs = draw_span_pairs(jax.random.fold_in(splits[6], 71), 0)
    return {"query": query, "keys": keys, "values": values, "attn_out": attn_out, "grad_out": grad_out, "span_pairs": span_pairs}


def positions_of(span_pairs, tok_dev, span_len):
    row_ids = jnp.arange(span_pairs.shape[0] * tok_dev, dtype=jnp.int32)
    owners = row_ids // tok_dev
    halves = row_ids % tok_dev // span_len
    return (span_pairs[owners, halves] * span_len + row_ids % span_len).astype(jnp.int32)

def group_backward(query_group, key_rows, value_rows, output_group, grad_group, position):
    scale_factor = 1.0 / math.sqrt(HEAD_DIM)
    block_rows = min(512, TOKENS)
    block_count = TOKENS // block_rows

    def one_block(carry, block_index):
        start = block_index * block_rows
        query_block = lax.dynamic_slice_in_dim(query_group, start, block_rows, 0)
        grad_block = lax.dynamic_slice_in_dim(grad_group, start, block_rows, 0)
        output_block = lax.dynamic_slice_in_dim(output_group, start, block_rows, 0)
        query_pos = lax.dynamic_slice_in_dim(position, start, block_rows, 0)
        kept = (position[None, :] <= query_pos[:, None])[None]
        score = jnp.einsum('qhd,kd->hqk', query_block, key_rows) * scale_factor
        masked = jnp.where(kept, score, -jnp.inf)
        row_top = lax.optimization_barrier(jnp.max(masked, axis=-1, keepdims=True))
        log_mass = row_top + jnp.log(lax.optimization_barrier(jnp.sum(jnp.exp(masked - row_top), axis=-1, keepdims=True)))
        prob = jnp.exp(masked - log_mass)
        prob_low = lax.optimization_barrier(prob.astype(jnp.bfloat16)).astype(jnp.float32)
        dprob = jnp.einsum('qhd,kd->hqk', grad_block, value_rows)
        delta = jnp.einsum('qhd,qhd->hq', grad_block, output_block)
        dscore = prob * (dprob - delta[:, :, None]) * scale_factor
        dscore = lax.optimization_barrier(dscore.astype(jnp.bfloat16)).astype(jnp.float32)
        query_term = jnp.einsum('hqk,kd->qhd', dscore, key_rows)
        key_term = jnp.einsum('hqk,qhd->kd', dscore, query_block)
        value_term = jnp.einsum('hqk,qhd->kd', prob_low, grad_block)
        return ((carry[0] + key_term, carry[1] + value_term), query_term)
    zeros_init = jnp.zeros((TOKENS, HEAD_DIM), jnp.float32)
    (key_grad, value_grad), query_blocks = lax.scan(one_block, (zeros_init, zeros_init), jnp.arange(block_count, dtype=jnp.int32))
    return (query_blocks.reshape(TOKENS, GROUP * HEAD_DIM), key_grad, value_grad)

def reference(query, keys, values, attn_out, grad_out, span_pairs):
    position = positions_of(span_pairs, TOK_DEV, SPAN)
    width_q = GROUP * HEAD_DIM
    upstream_rows = []
    key_sections = []
    value_sections = []
    for section in range(SECTIONS):
        query_heads = []
        key_heads = []
        value_heads = []
        for group_id in range(KV_HEADS):
            key_rows = keys[section, :, group_id * HEAD_DIM:(group_id + 1) * HEAD_DIM].astype(jnp.float32)
            value_rows = values[section, :, group_id * HEAD_DIM:(group_id + 1) * HEAD_DIM].astype(jnp.float32)
            query_group = query[section, :, group_id * width_q:(group_id + 1) * width_q].astype(jnp.float32).reshape(TOKENS, GROUP, HEAD_DIM)
            output_group = attn_out[section, :, group_id * width_q:(group_id + 1) * width_q].astype(jnp.float32).reshape(TOKENS, GROUP, HEAD_DIM)
            grad_group = grad_out[section, :, group_id * width_q:(group_id + 1) * width_q].astype(jnp.float32).reshape(TOKENS, GROUP, HEAD_DIM)
            query_grad, key_grad, value_grad = group_backward(query_group, key_rows, value_rows, output_group, grad_group, position)
            query_heads.append(query_grad)
            key_heads.append(key_grad)
            value_heads.append(value_grad)
        upstream_rows.append(jnp.concatenate(query_heads, axis=1).astype(jnp.bfloat16))
        key_sections.append(jnp.concatenate(key_heads, axis=1).astype(jnp.bfloat16))
        value_sections.append(jnp.concatenate(value_heads, axis=1).astype(jnp.bfloat16))
    shifted = upstream_rows[1:] + [jnp.zeros_like(upstream_rows[0])]
    return (jnp.stack(key_sections), jnp.stack(value_sections), jnp.stack(shifted))
```

```python
import functools
import math

import jax
import jax.numpy as jnp
from jax import lax
from jax.experimental import pallas as pl
from jax.experimental.pallas import tpu as pltpu
from jax.sharding import PartitionSpec as P

MESH = pl.DeviceIdType.MESH
NEG = -1e30
LOG2E = math.log2(math.e)


def kernel(
    ranks, sections, block_len,
    pairs_hbm, query, keys, values, attn_out, grad_out,
    key_grad, value_grad, upstream,
    q_buf, o_buf, g_buf, k_buf, v_buf, dq_buf, bias, stats, dq_acc, pair_acc, pair_recv,
    pairs, in_sem, kv_send, kv_recv, dq_send, dq_recv, pair_send, pair_got,
):
    rows, width = q_buf.shape
    dim = k_buf.shape[1]
    heads = width // dim
    span = rows // 2
    seq = ranks * rows
    blocks = seq // block_len
    scale = 1.0 / math.sqrt(dim)
    me = lax.axis_index("cp")
    sec = lax.axis_index("pp")
    mine = pl.ds(0, rows)

    barrier = pltpu.get_barrier_semaphore()
    for off in range(1, ranks):
        pl.semaphore_signal(
            barrier, inc=1, device_id={"cp": lax.rem(me + off, ranks)}, device_id_type=MESH
        )

    @pl.when(sec < sections - 1)
    def _():
        pl.semaphore_signal(barrier, inc=1, device_id={"pp": sec + 1}, device_id_type=MESH)

    own = [
        pltpu.make_async_copy(keys, k_buf.at[mine, :], in_sem.at[0]),
        pltpu.make_async_copy(values, v_buf.at[mine, :], in_sem.at[1]),
    ]
    first, rest = pl.ds(0, dim), pl.ds(dim, width - dim)
    wide = ((query, q_buf), (grad_out, g_buf), (attn_out, o_buf))
    begin = [
        pltpu.make_async_copy(src.at[:, first], dst.at[:, first], in_sem.at[2 + i])
        for i, (src, dst) in enumerate(wide)
    ]
    later = [
        pltpu.make_async_copy(src.at[:, rest], dst.at[:, rest], in_sem.at[5 + i])
        for i, (src, dst) in enumerate(wide)
    ]
    table = pltpu.make_async_copy(pairs_hbm, pairs, in_sem.at[8])
    for copy in [table] + own + begin:
        copy.start()

    pl.semaphore_wait(barrier, ranks - 1 + (sec > 0).astype(jnp.int32))
    sent = []
    for off in range(1, ranks):
        for which, (src, buf) in enumerate(((keys, k_buf), (values, v_buf))):
            sent.append(
                pltpu.make_async_remote_copy(
                    src_ref=src,
                    dst_ref=buf.at[pl.ds((ranks - off) * rows, rows), :],
                    send_sem=kv_send.at[which, off - 1],
                    recv_sem=kv_recv.at[which, off - 1],
                    device_id={"cp": lax.rem(me + off, ranks)},
                    device_id_type=MESH,
                )
            )
    for copy in sent + later:
        copy.start()

    table.wait()
    row = lax.broadcasted_iota(jnp.int32, (rows, rows), 0)
    col = lax.broadcasted_iota(jnp.int32, (rows, rows), 1)
    q_pos = jnp.where(row < span, pairs[me, 0] * span, pairs[me, 1] * span - span) + row
    for r in range(ranks):
        rank = lax.rem(me + r, ranks)
        k_pos = jnp.where(col < span, pairs[rank, 0] * span, pairs[rank, 1] * span - span) + col
        bias[:, r * rows:(r + 1) * rows] = jnp.where(k_pos <= q_pos, 0.0, NEG)
    pair_acc[...] = jnp.zeros_like(pair_acc)

    for copy in own + begin:
        copy.wait()
    for copy in sent:
        copy.wait_recv()

    def dot(a, b, da, db):
        return lax.dot_general(a, b, (((da,), (db,)), ((), ())), preferred_element_type=jnp.float32)

    def lanes_of(h):
        return pl.ds(h * dim if isinstance(h, int) else pl.multiple_of(h * dim, dim), dim)

    def send_dq(h, lines, slot):
        return pltpu.make_async_remote_copy(
            src_ref=dq_buf.at[lines, lanes_of(h)],
            dst_ref=upstream.at[lines, lanes_of(h)],
            send_sem=dq_send.at[slot],
            recv_sem=dq_recv.at[slot],
            device_id={"pp": jnp.maximum(sec - 1, 0)},
            device_id_type=MESH,
        )

    def rows_of_head(h, lines, slot):
        lanes = lanes_of(h)
        q = q_buf[lines, lanes]
        g = g_buf[lines, lanes]
        delta = jnp.sum(
            g.astype(jnp.float32) * o_buf[lines, lanes].astype(jnp.float32), axis=1, keepdims=True
        )

        def scores(b):
            at = b * block_len if isinstance(b, int) else pl.multiple_of(b * block_len, block_len)
            part = pl.ds(at, block_len)
            return part, dot(q, k_buf[part, :], 1, 1) * (scale * LOG2E) + bias[lines, part]

        def terms(part, prob):
            dprob = dot(g, v_buf[part, :], 1, 1)
            dscore = (prob * (dprob - delta) * scale).astype(jnp.bfloat16)
            return prob.astype(jnp.bfloat16), dscore, dot(dscore, k_buf[part, :], 1, 0)

        def pair_terms(part, prob_low, dscore):
            pair_acc[part, :dim] += dot(dscore, q, 0, 0)
            pair_acc[part, dim:] += dot(prob_low, g, 0, 0)

        def start_dq(dq):
            dq_buf[lines, lanes] = dq.astype(jnp.bfloat16)

            @pl.when(sec > 0)
            def _():
                send_dq(h, lines, slot).start()

        if blocks == 1:
            part, score = scores(0)
            top = jnp.max(score, axis=1, keepdims=True)
            prob = jnp.exp2(score - top)
            prob = prob * (1.0 / jnp.sum(prob, axis=1, keepdims=True))
            prob_low, dscore, dq = terms(part, prob)
            start_dq(dq)
            pair_terms(part, prob_low, dscore)
        else:
            stats[0, lines] = jnp.full((lines.size, 1), NEG, jnp.float32)
            stats[1, lines] = jnp.zeros((lines.size, 1), jnp.float32)
            dq_acc[lines] = jnp.zeros((lines.size, dim), jnp.float32)

            def gather_stats(b, _):
                _, score = scores(b)
                before = stats[0, lines]
                top = jnp.maximum(before, jnp.max(score, axis=1, keepdims=True))
                mass = jnp.sum(jnp.exp2(score - top), axis=1, keepdims=True)
                stats[1, lines] = stats[1, lines] * jnp.exp2(before - top) + mass
                stats[0, lines] = top
                return 0

            def gather_terms(b, _):
                part, score = scores(b)
                prob = jnp.exp2(score - stats[0, lines]) * (1.0 / stats[1, lines])
                prob_low, dscore, dq = terms(part, prob)
                dq_acc[lines] += dq
                pair_terms(part, prob_low, dscore)
                return 0

            lax.fori_loop(0, blocks, gather_stats, 0)
            lax.fori_loop(0, blocks, gather_terms, 0)
            start_dq(dq_acc[lines])

    pieces = [(h, pl.ds(0, rows), h) for h in range(heads)]
    for piece in pieces[:1]:
        rows_of_head(*piece)

    @pl.when(sec == sections - 1)
    def _():
        upstream[...] = jnp.zeros_like(upstream)

    for copy in later:
        copy.wait()

    def one_head(h, _):
        rows_of_head(h, pl.ds(0, rows), h)
        return 0

    lax.fori_loop(1, heads, one_head, 0)

    pair_sent = []
    for off in range(1, ranks):
        dst = lax.rem(me + off, ranks)
        pair_sent.append(
            pltpu.make_async_remote_copy(
                src_ref=pair_acc.at[pl.ds(off * rows, rows), :],
                dst_ref=pair_recv.at[off - 1],
                send_sem=pair_send.at[off - 1],
                recv_sem=pair_got.at[off - 1],
                device_id={"cp": dst},
                device_id_type=MESH,
            )
        )
    for copy in pair_sent:
        copy.start()
    for copy in sent:
        copy.wait_send()
    for copy in pair_sent:
        copy.wait_recv()
    total = pair_acc[mine, :]
    for off in range(1, ranks):
        total = total + pair_recv[off - 1]
    key_grad[...] = total[:, :dim].astype(jnp.bfloat16)
    value_grad[...] = total[:, dim:].astype(jnp.bfloat16)
    for copy in pair_sent:
        copy.wait_send()

    @pl.when(sec > 0)
    def _():
        for piece in pieces:
            send_dq(*piece).wait_send()

    @pl.when(sec < sections - 1)
    def _():
        for piece in pieces:
            send_dq(*piece).wait_recv()


def pair_kernel(
    sections, first, last, roles,
    pairs_hbm, query, keys, values, attn_out, grad_out,
    key_grad, value_grad, upstream,
    q_buf, o_buf, g_buf, k_raw, v_raw, k_buf, v_buf, d_buf, y_got, s_buf, p_own, p_got, p_out,
    r_one, r_two, r_pack, key_low, key_wide, ds_buf, pr_buf, bias, pair_acc, pair_out, pair_recv, pairs,
    in_sem, kv_sem, low_send, low_recv, dq_sem, one_send, one_recv, block_send, pack_send, give_recv,
    two_recv, pack_recv, swap_sem, met, may_send,
):
    rows, width = q_buf.shape
    dim = k_buf.shape[1]
    heads = width // dim
    span = rows // 2
    seq = 2 * rows
    part = span // 6
    packed = 3 * part
    units = (last - first) // 2
    lag = 2
    scale = 1.0 / math.sqrt(dim)
    low, full = jnp.bfloat16, jnp.float32
    me = lax.axis_index("cp")
    sec = lax.axis_index("pp")
    peer = {"cp": 1 - me}
    below = {"pp": jnp.maximum(sec - 1, 0)}
    sends, gets = sec > 0, sec < sections - 1
    upper, lower, every = pl.ds(0, span), pl.ds(span, span), pl.ds(0, rows)

    def remote(src, dst, send, recv, device):
        return pltpu.make_async_remote_copy(
            src_ref=src, dst_ref=dst, send_sem=send, recv_sem=recv, device_id=device, device_id_type=MESH
        )

    def take(ref, sem):
        pltpu.make_async_copy(ref, ref, sem).wait()

    barrier = pltpu.get_barrier_semaphore()

    @pl.when(me == 1)
    def _():
        pl.semaphore_signal(barrier, inc=1, device_id=peer, device_id_type=MESH)

    own = [
        pltpu.make_async_copy(keys, k_raw.at[every, :], in_sem.at[0]),
        pltpu.make_async_copy(values, v_raw.at[every, :], in_sem.at[0]),
    ]
    head, rest = pl.ds(0, dim), pl.ds(dim, width - dim)
    wide = ((query, q_buf), (grad_out, g_buf), (attn_out, o_buf))
    begin = [pltpu.make_async_copy(src.at[:, head], dst.at[:, head], in_sem.at[1]) for src, dst in wide]
    later = [pltpu.make_async_copy(src.at[:, rest], dst.at[:, rest], in_sem.at[2 + i]) for i, (src, dst) in enumerate(wide)]
    table = pltpu.make_async_copy(pairs_hbm, pairs, in_sem.at[5])
    for copy in own + [table] + begin:
        copy.start()

    @pl.when(me == 0)
    def _():
        pl.semaphore_wait(barrier, 1)
        pl.semaphore_signal(met, inc=1, device_id=peer, device_id_type=MESH)

    @pl.when(me == 1)
    def _():
        pl.semaphore_wait(met, 1)

    other = pl.ds(rows, rows)
    for src, dst in ((keys, k_raw), (values, v_raw)):
        remote(src, dst.at[other, :], kv_sem.at[0], kv_sem.at[1], peer).start()

    @pl.when((me == 1) & gets)
    def _():
        pl.semaphore_signal(barrier, inc=1, device_id={"pp": sec + 1}, device_id_type=MESH)

    for copy in later:
        copy.start()

    table.wait()
    row = lax.broadcasted_iota(jnp.int32, (rows, seq), 0)
    col = lax.broadcasted_iota(jnp.int32, (rows, seq), 1)
    spans = [pairs[me, 0], pairs[me, 1], pairs[1 - me, 0], pairs[1 - me, 1]]
    q_pos = jnp.where(row < span, spans[0] * span, spans[1] * span - span) + row
    bias[...] = jnp.where(col <= q_pos, 0.0, NEG)
    pair_acc[...] = jnp.zeros_like(pair_acc)
    low_here = spans[0] == 0
    high_here = spans[1] == 0
    here = low_here | high_here

    def block_of(ref, n):
        return ref[n * span:(n + 1) * span, :]

    def of_span(ref, s):
        block = block_of(ref, 0)
        for n in range(1, 4):
            block = jnp.where(spans[n] == s, block_of(ref, n), block)
        return block

    def at_span(ref, s):
        block = block_of(ref, 0)
        for n in range(1, 4):
            block = jnp.where(s == n, block_of(ref, n), block)
        return block

    take(k_raw, in_sem.at[0])
    take(k_raw, kv_sem.at[1])
    for s in range(4):
        k_buf[pl.ds(s * span, span), :] = of_span(k_raw, s)

    half = pl.ds(pl.multiple_of(me * (span // 2), span // 2), span // 2)
    rest_half = pl.ds(pl.multiple_of((1 - me) * (span // 2), span // 2), span // 2)
    send_low = remote(k_buf.at[half, :], key_low.at[half, :], low_send.at[0], low_recv.at[0], below)
    pass_low = remote(key_low.at[half, :], key_low.at[half, :], low_send.at[1], low_recv.at[1], peer)

    @pl.when(sends)
    def _():
        @pl.when(me == 1)
        def _():
            pl.semaphore_wait(barrier, 1)
            pl.semaphore_signal(may_send, inc=1, device_id=peer, device_id_type=MESH)

        @pl.when(me == 0)
        def _():
            pl.semaphore_wait(may_send, 1)

        send_low.start()

    for s in range(4):
        v_buf[pl.ds(s * span, span), :] = of_span(v_raw, s)
    take(q_buf.at[:, pl.ds(0, 3 * dim)], in_sem.at[1])

    def dot(a, b, da, db):
        return lax.dot_general(a, b, (((da,), (db,)), ((), ())), preferred_element_type=full)

    def lanes_of(h, count=1):
        return pl.ds(h * dim if isinstance(h, int) else pl.multiple_of(h * dim, dim), count * dim)

    def lines_of(n, size, count=1):
        return pl.ds(n * size if isinstance(n, int) else pl.multiple_of(n * size, size), count * size)

    def two_blocks(group):
        role = jnp.int32(roles[0])
        for g in range(1, len(roles)):
            role = jnp.where(group >= g, roles[g], role)
        return me == role

    def by_role(group, if_two, if_one):
        pl.when(two_blocks(group))(if_two)
        pl.when(jnp.logical_not(two_blocks(group)))(if_one)

    def send_dq(h, lines):
        return remote(
            d_buf.at[lines, lanes_of(h)], upstream.at[lines, lanes_of(h)], dq_sem.at[0], dq_sem.at[1], below
        )

    def unit_lanes(i):
        return lanes_of(first + 2 * i, 2)

    def unit_lines(i):
        return lines_of(i, 2 * packed)

    def group_of(i):
        return i // 2 if isinstance(i, int) else lax.div(i, 2)

    def send_one(i):
        at = unit_lanes(i)
        return remote(d_buf.at[upper, at], r_one.at[:, at], one_send.at[0], one_recv.at[group_of(i)], below)

    def send_two(i):
        at = unit_lanes(i)
        return remote(s_buf.at[:, at], r_two.at[:, at], block_send.at[1], two_recv.at[group_of(i)], below)

    def send_pack(i):
        at = unit_lines(i)
        return remote(p_out.at[at, :], r_pack.at[at, :], pack_send.at[1], pack_recv.at[group_of(i)], below)

    def give_block(i):
        at = unit_lanes(i)
        return remote(d_buf.at[lower, at], y_got.at[:, at], block_send.at[0], give_recv.at[i], peer)

    def give_pack(i):
        at = unit_lines(i)
        return remote(p_own.at[at, :], p_got.at[at, :], pack_send.at[0], give_recv.at[i], peer)

    def pass_two(g):
        at = lanes_of(first + 4 * g, 4)
        return remote(r_two.at[:, at], r_two.at[:, at], block_send.at[2], two_recv.at[g], peer)

    def pass_pack(g):
        at = lines_of(g, 4 * packed)
        return remote(r_pack.at[at, :], r_pack.at[at, :], pack_send.at[2], pack_recv.at[g], peer)

    def gradients(h, lines):
        lanes = lanes_of(h)
        q = q_buf[lines, lanes]
        g = g_buf[lines, lanes]
        delta = jnp.sum(g.astype(full) * o_buf[lines, lanes].astype(full), axis=1, keepdims=True)
        score = dot(q, k_buf[...], 1, 1) * (scale * LOG2E) + bias[lines, :]
        top = jnp.max(score, axis=1, keepdims=True)
        prob = jnp.exp2(score - top)
        prob = prob * (1.0 / jnp.sum(prob, axis=1, keepdims=True))
        dprob = dot(g, v_buf[...], 1, 1)
        dscore = (prob * (dprob - delta) * scale).astype(low)
        place = pl.ds(
            h * rows + lines.start if isinstance(h, int) else pl.multiple_of(h * rows + lines.start, span), lines.size
        )
        pr_buf[place, :] = prob.astype(low)
        ds_buf[place, :] = dscore
        return dscore, dot(dscore, k_buf[...], 1, 0)

    def pair_terms(h, _):
        place = lines_of(h, rows)
        pair_acc[:, :dim] += dot(ds_buf[place, :], q_buf[:, lanes_of(h)], 0, 0)
        pair_acc[:, dim:] += dot(pr_buf[place, :], g_buf[:, lanes_of(h)], 0, 0)
        return 0

    def plain_pieces(pieces, before=None):
        for h, lines in pieces:
            d_buf[lines, lanes_of(h)] = gradients(h, lines)[1].astype(low)

        @pl.when(sends)
        def _():
            if before is not None:
                before()
            for piece in pieces:
                send_dq(*piece).start()

    def pack_head(h):
        lanes = lanes_of(h)
        dscore, dq = gradients(h, every)
        block = jnp.where(high_here, dscore[span:, :dim].astype(full), dscore[:span, :dim].astype(full))
        wide_rows = block[4 * part:] + pltpu.roll(block[:2 * part], 6 * part, 1)
        short_rows = block[3 * part:4 * part] + pltpu.roll(block[2 * part:3 * part], 4 * part, 1)
        p_own[lines_of(h - first, packed), :] = jnp.concatenate([wide_rows, short_rows], axis=0).astype(low)
        d_buf[upper, lanes] = jnp.where(low_here, dq[span:], dq[:span]).astype(low)
        d_buf[lower, lanes] = dq[span:].astype(low)

    def first_sends(i):
        send_one(i).start()
        by_role(group_of(i), lambda: give_pack(i).start(), lambda: give_block(i).start())

    def second_sends(i):
        def two():
            at = unit_lanes(i)
            give_block(i).wait_recv()
            s_buf[:, at] = jnp.where(here, y_got[:, at], d_buf[lower, at])
            send_two(i).start()

        def one():
            at = unit_lines(i)
            give_pack(i).wait_recv()
            p_out[at, :] = jnp.where(here, p_own[at, :], p_got[at, :])
            send_pack(i).start()

        by_role(group_of(i), two, one)

    def packed_unit(i, _):
        pack_head(first + 2 * i)
        pack_head(first + 2 * i + 1)

        @pl.when(sends)
        def _():
            first_sends(i)

            @pl.when(i >= lag)
            def _():
                second_sends(i - lag)

        return 0

    plain_pieces([(0, upper)])
    plain_pieces([(0, lower)])
    for copy in later:
        copy.wait()
    plain_pieces([(h, every) for h in range(1, first)])
    lax.fori_loop(0, units, packed_unit, 0)

    def waiting():
        for i in range(units - lag, units):
            second_sends(i)

    plain_pieces([(h, every) for h in range(last, heads)], waiting)
    lax.fori_loop(0, heads, pair_terms, 0, unroll=2)

    for n in range(2):
        pair_out[lines_of(n, span), :] = at_span(pair_acc, spans[2 + n])
    swap = remote(pair_out, pair_recv, swap_sem.at[0], swap_sem.at[1], peer)
    swap.start()

    def group_two(g):
        return r_two.at[:, lanes_of(first + 4 * g, 4)]

    def group_pack(g):
        return r_pack.at[lines_of(g, 4 * packed), :]

    def pass_on(g):
        def two():
            take(group_two(g), two_recv.at[g])
            pass_two(g).start()

        def one():
            take(group_pack(g), pack_recv.at[g])
            pass_pack(g).start()

        by_role(g, two, one)

    def assemble(g):
        at = lanes_of(first + 4 * g, 4)
        take(r_one.at[:, at], one_recv.at[g])
        by_role(g, lambda: pass_pack(g).wait_recv(), lambda: pass_two(g).wait_recv())
        for h in range(first + 4 * g, first + 4 * g + 4):
            lanes = lanes_of(h)
            terms = dot(r_pack[lines_of(h - first, packed), :], key_wide[...], 1, 0)
            opened = jnp.concatenate(
                [
                    terms[:2 * part, dim:2 * dim],
                    terms[2 * part:, 3 * dim:],
                    terms[2 * part:, 2 * dim:3 * dim],
                    terms[:2 * part, :dim],
                ],
                axis=0,
            ).astype(low)
            one = r_one[:, lanes]
            upstream[upper, lanes] = jnp.where(low_here, opened, one)
            upstream[lower, lanes] = jnp.where(low_here, one, jnp.where(high_here, opened, r_two[:, lanes]))

    @pl.when(gets)
    def _():
        send_low.wait_recv()
        pass_low.start()
        pass_on(0)

    swap.wait_recv()
    for n in range(2):
        lines = lines_of(n, span)
        total = at_span(pair_acc, spans[n]) + pair_recv[lines, :]
        key_grad[lines, :] = total[:, :dim].astype(low)
        value_grad[lines, :] = total[:, dim:].astype(low)

    plain = heads - (last - first)

    @pl.when(gets)
    def _():
        take(key_low.at[rest_half, :], low_recv.at[1])
        key_wide[...] = jnp.zeros_like(key_wide)
        key_wide[:6 * part, :dim] = key_low[...]
        key_wide[6 * part:, dim:2 * dim] = key_low[:2 * part, :]
        key_wide[:4 * part, 2 * dim:3 * dim] = key_low[:4 * part, :]
        key_wide[4 * part:7 * part, 3 * dim:] = key_low[:3 * part, :]
        for g in range(1, len(roles)):
            pass_on(g)
            assemble(g - 1)
        assemble(len(roles) - 1)
        pass_low.wait_send()

    @pl.when(jnp.logical_not(gets))
    def _():
        upstream[...] = jnp.zeros_like(upstream)

    take(k_raw, kv_sem.at[0])
    swap.wait_send()

    @pl.when(sends)
    def _():
        send_low.wait_send()
        take(d_buf.at[upper, lanes_of(first, last - first)], one_send.at[0])
        take(d_buf.at[:, lanes_of(0, plain)], dq_sem.at[0])

    def drain(core):
        double = 2 * sum(role == core for role in roles)
        single = 2 * len(roles) - double

        def sent(step):
            def blocks(n, at):
                if n:
                    take(s_buf.at[:, lanes_of(0, 2 * n)], block_send.at[at])

            def packs(n, at):
                if n:
                    take(p_out.at[lines_of(0, 2 * packed, n), :], pack_send.at[at])

            blocks(single if step == 0 else double, step)
            packs(double if step == 0 else single, step)

        @pl.when(sends)
        def _():
            sent(0)
            sent(1)

        @pl.when(gets)
        def _():
            sent(2)

    pl.when(me == 0)(lambda: drain(0))
    pl.when(me == 1)(lambda: drain(1))

    @pl.when(gets)
    def _():
        take(upstream.at[:, lanes_of(0, plain)], dq_sem.at[1])


def store(key_grad, value_grad, upstream, key_out, value_out, upstream_out, sem):
    copies = [
        pltpu.make_async_copy(src, dst, sem.at[i])
        for i, (src, dst) in enumerate(
            ((upstream, upstream_out), (key_grad, key_out), (value_grad, value_out))
        )
    ]
    for copy in copies:
        copy.start()
    for copy in copies:
        copy.wait()


def body(query, keys, values, attn_out, grad_out, span_pairs):
    _, rows, width = query.shape
    dim = keys.shape[2]
    heads = width // dim
    ranks = lax.axis_size("cp")
    sections = lax.axis_size("pp")
    seq = ranks * rows
    low, full = jnp.bfloat16, jnp.float32
    dma = pltpu.SemaphoreType.DMA
    vmem = pl.BlockSpec(memory_space=pltpu.VMEM)
    hbm = pl.BlockSpec(memory_space=pltpu.HBM)

    def spaces(*shapes):
        return [pltpu.VMEM(shape, low) for shape in shapes]

    tall, flat, block = (rows, width), (seq, dim), (rows // 2, width)
    if ranks == 2 and sections > 1 and dim == 128 and rows == 192 and heads % 4 == 0 and heads >= 16:
        groups, packs = (heads - 4) // 4, ((heads - 4) * (rows // 4), dim)
        run = functools.partial(pair_kernel, sections, 2, heads - 2, (1, 0, 1) + (1,) * (groups - 3))
        scratch = (
            spaces(tall, tall, tall, flat, flat, flat, flat, tall, block, block, packs, packs, packs)
            + spaces(block, block, packs, (rows // 2, dim), (dim, 4 * dim))
            + spaces((heads * rows, seq), (heads * rows, seq))
            + [
                pltpu.VMEM((rows, seq), full),
                pltpu.VMEM((seq, 2 * dim), full),
                pltpu.VMEM((rows, 2 * dim), full),
                pltpu.VMEM((rows, 2 * dim), full),
                pltpu.SMEM((ranks, 2), jnp.int32),
            ]
            + [dma((n,)) for n in (6, 2, 2, 2, 2, 1, groups, 3, 3, 2 * groups, groups, groups, 2)]
            + [pltpu.SemaphoreType.REGULAR] * 2
        )
    else:
        others = max(ranks - 1, 1)
        run = functools.partial(kernel, ranks, sections, 2 * rows if ranks % 2 == 0 else rows)
        scratch = (
            spaces(tall, tall, tall, flat, flat, tall)
            + [
                pltpu.VMEM((rows, seq), full),
                pltpu.VMEM((2, rows, 1), full),
                pltpu.VMEM((rows, dim), full),
                pltpu.VMEM((seq, 2 * dim), full),
                pltpu.VMEM((others, rows, 2 * dim), full),
                pltpu.SMEM((ranks, 2), jnp.int32),
            ]
            + [dma((9,)), dma((2, others)), dma((2, others)), dma((heads + 1,)), dma((heads + 1,))]
            + [dma((others,)), dma((others,))]
        )
    key_grad, value_grad, upstream = pl.pallas_call(
        run,
        out_shape=(
            pltpu.VMEM((rows, dim), low),
            pltpu.VMEM((rows, dim), low),
            pltpu.VMEM((rows, width), low),
        ),
        in_specs=[hbm] * 6,
        out_specs=(vmem, vmem, vmem),
        scratch_shapes=scratch,
        compiler_params=pltpu.CompilerParams(
            collective_id=0, has_side_effects=True, vmem_limit_bytes=64 * 1024 * 1024 - 1200 * 1024
        ),
        name="backward",
    )(span_pairs, query[0], keys[0], values[0], attn_out[0], grad_out[0])
    anywhere = pl.BlockSpec(memory_space=pl.ANY)
    key_grad, value_grad, upstream = pl.pallas_call(
        store,
        out_shape=(
            jax.ShapeDtypeStruct((rows, dim), low),
            jax.ShapeDtypeStruct((rows, dim), low),
            jax.ShapeDtypeStruct((rows, width), low),
        ),
        in_specs=[anywhere] * 3,
        out_specs=(anywhere,) * 3,
        scratch_shapes=[dma((3,))],
        compiler_params=pltpu.CompilerParams(vmem_limit_bytes=1024 * 1024),
        name="store",
    )(key_grad, value_grad, upstream)
    return key_grad[None], value_grad[None], upstream[None]


def solution(mesh):
    spec = P("pp", "cp", "tp")
    return jax.shard_map(
        body,
        mesh=mesh,
        in_specs=(spec, spec, spec, spec, spec, P()),
        out_specs=(spec, spec, spec),
        check_vma=False,
    )
```

```python
import functools
import math

import jax
import jax.numpy as jnp
from jax import lax
from jax.experimental import pallas as pl
from jax.experimental.pallas import tpu as pltpu
from jax.sharding import PartitionSpec as P

MESH = pl.DeviceIdType.MESH
NEG = -1e30
LOG2E = math.log2(math.e)


def kernel(
    ranks, sections, block_len,
    pairs_hbm, query, keys, values, attn_out, grad_out,
    key_grad, value_grad, upstream,
    q_buf, o_buf, g_buf, k_buf, v_buf, dq_buf, bias, stats, dq_acc, pair_acc, pair_recv,
    pairs, in_sem, kv_send, kv_recv, dq_send, dq_recv, pair_send, pair_got,
):
    rows, width = q_buf.shape
    dim = k_buf.shape[1]
    heads = width // dim
    span = rows // 2
    seq = ranks * rows
    blocks = seq // block_len
    scale = 1.0 / math.sqrt(dim)
    me = lax.axis_index("cp")
    sec = lax.axis_index("pp")
    mine = pl.ds(0, rows)

    barrier = pltpu.get_barrier_semaphore()
    for off in range(1, ranks):
        pl.semaphore_signal(
            barrier, inc=1, device_id={"cp": lax.rem(me + off, ranks)}, device_id_type=MESH
        )

    @pl.when(sec < sections - 1)
    def _():
        pl.semaphore_signal(barrier, inc=1, device_id={"pp": sec + 1}, device_id_type=MESH)

    own = [
        pltpu.make_async_copy(keys, k_buf.at[mine, :], in_sem.at[0]),
        pltpu.make_async_copy(values, v_buf.at[mine, :], in_sem.at[1]),
    ]
    first, rest = pl.ds(0, dim), pl.ds(dim, width - dim)
    wide = ((query, q_buf), (grad_out, g_buf), (attn_out, o_buf))
    begin = [
        pltpu.make_async_copy(src.at[:, first], dst.at[:, first], in_sem.at[2 + i])
        for i, (src, dst) in enumerate(wide)
    ]
    later = [
        pltpu.make_async_copy(src.at[:, rest], dst.at[:, rest], in_sem.at[5 + i])
        for i, (src, dst) in enumerate(wide)
    ]
    table = pltpu.make_async_copy(pairs_hbm, pairs, in_sem.at[8])
    for copy in [table] + own + begin:
        copy.start()

    pl.semaphore_wait(barrier, ranks - 1 + (sec > 0).astype(jnp.int32))
    sent = []
    for off in range(1, ranks):
        for which, (src, buf) in enumerate(((keys, k_buf), (values, v_buf))):
            sent.append(
                pltpu.make_async_remote_copy(
                    src_ref=src,
                    dst_ref=buf.at[pl.ds((ranks - off) * rows, rows), :],
                    send_sem=kv_send.at[which, off - 1],
                    recv_sem=kv_recv.at[which, off - 1],
                    device_id={"cp": lax.rem(me + off, ranks)},
                    device_id_type=MESH,
                )
            )
    for copy in sent + later:
        copy.start()

    table.wait()
    row = lax.broadcasted_iota(jnp.int32, (rows, rows), 0)
    col = lax.broadcasted_iota(jnp.int32, (rows, rows), 1)
    q_pos = jnp.where(row < span, pairs[me, 0] * span, pairs[me, 1] * span - span) + row
    for r in range(ranks):
        rank = lax.rem(me + r, ranks)
        k_pos = jnp.where(col < span, pairs[rank, 0] * span, pairs[rank, 1] * span - span) + col
        bias[:, r * rows:(r + 1) * rows] = jnp.where(k_pos <= q_pos, 0.0, NEG)
    pair_acc[...] = jnp.zeros_like(pair_acc)

    for copy in own + begin:
        copy.wait()
    for copy in sent:
        copy.wait_recv()

    def dot(a, b, da, db):
        return lax.dot_general(a, b, (((da,), (db,)), ((), ())), preferred_element_type=jnp.float32)

    def lanes_of(h):
        return pl.ds(h * dim if isinstance(h, int) else pl.multiple_of(h * dim, dim), dim)

    def send_dq(h, lines, slot):
        return pltpu.make_async_remote_copy(
            src_ref=dq_buf.at[lines, lanes_of(h)],
            dst_ref=upstream.at[lines, lanes_of(h)],
            send_sem=dq_send.at[slot],
            recv_sem=dq_recv.at[slot],
            device_id={"pp": jnp.maximum(sec - 1, 0)},
            device_id_type=MESH,
        )

    def rows_of_head(h, lines, slot):
        lanes = lanes_of(h)
        q = q_buf[lines, lanes]
        g = g_buf[lines, lanes]
        delta = jnp.sum(
            g.astype(jnp.float32) * o_buf[lines, lanes].astype(jnp.float32), axis=1, keepdims=True
        )

        def scores(b):
            at = b * block_len if isinstance(b, int) else pl.multiple_of(b * block_len, block_len)
            part = pl.ds(at, block_len)
            return part, dot(q, k_buf[part, :], 1, 1) * (scale * LOG2E) + bias[lines, part]

        def terms(part, prob):
            dprob = dot(g, v_buf[part, :], 1, 1)
            dscore = (prob * (dprob - delta) * scale).astype(jnp.bfloat16)
            return prob.astype(jnp.bfloat16), dscore, dot(dscore, k_buf[part, :], 1, 0)

        def pair_terms(part, prob_low, dscore):
            pair_acc[part, :dim] += dot(dscore, q, 0, 0)
            pair_acc[part, dim:] += dot(prob_low, g, 0, 0)

        def start_dq(dq):
            dq_buf[lines, lanes] = dq.astype(jnp.bfloat16)

            @pl.when(sec > 0)
            def _():
                send_dq(h, lines, slot).start()

        if blocks == 1:
            part, score = scores(0)
            top = jnp.max(score, axis=1, keepdims=True)
            prob = jnp.exp2(score - top)
            prob = prob * (1.0 / jnp.sum(prob, axis=1, keepdims=True))
            prob_low, dscore, dq = terms(part, prob)
            start_dq(dq)
            pair_terms(part, prob_low, dscore)
        else:
            stats[0, lines] = jnp.full((lines.size, 1), NEG, jnp.float32)
            stats[1, lines] = jnp.zeros((lines.size, 1), jnp.float32)
            dq_acc[lines] = jnp.zeros((lines.size, dim), jnp.float32)

            def gather_stats(b, _):
                _, score = scores(b)
                before = stats[0, lines]
                top = jnp.maximum(before, jnp.max(score, axis=1, keepdims=True))
                mass = jnp.sum(jnp.exp2(score - top), axis=1, keepdims=True)
                stats[1, lines] = stats[1, lines] * jnp.exp2(before - top) + mass
                stats[0, lines] = top
                return 0

            def gather_terms(b, _):
                part, score = scores(b)
                prob = jnp.exp2(score - stats[0, lines]) * (1.0 / stats[1, lines])
                prob_low, dscore, dq = terms(part, prob)
                dq_acc[lines] += dq
                pair_terms(part, prob_low, dscore)
                return 0

            lax.fori_loop(0, blocks, gather_stats, 0)
            lax.fori_loop(0, blocks, gather_terms, 0)
            start_dq(dq_acc[lines])

    pieces = [(h, pl.ds(0, rows), h) for h in range(heads)]
    for piece in pieces[:1]:
        rows_of_head(*piece)

    @pl.when(sec == sections - 1)
    def _():
        upstream[...] = jnp.zeros_like(upstream)

    for copy in later:
        copy.wait()

    def one_head(h, _):
        rows_of_head(h, pl.ds(0, rows), h)
        return 0

    lax.fori_loop(1, heads, one_head, 0)

    pair_sent = []
    for off in range(1, ranks):
        dst = lax.rem(me + off, ranks)
        pair_sent.append(
            pltpu.make_async_remote_copy(
                src_ref=pair_acc.at[pl.ds(off * rows, rows), :],
                dst_ref=pair_recv.at[off - 1],
                send_sem=pair_send.at[off - 1],
                recv_sem=pair_got.at[off - 1],
                device_id={"cp": dst},
                device_id_type=MESH,
            )
        )
    for copy in pair_sent:
        copy.start()
    for copy in sent:
        copy.wait_send()
    for copy in pair_sent:
        copy.wait_recv()
    total = pair_acc[mine, :]
    for off in range(1, ranks):
        total = total + pair_recv[off - 1]
    key_grad[...] = total[:, :dim].astype(jnp.bfloat16)
    value_grad[...] = total[:, dim:].astype(jnp.bfloat16)
    for copy in pair_sent:
        copy.wait_send()

    @pl.when(sec > 0)
    def _():
        for piece in pieces:
            send_dq(*piece).wait_send()

    @pl.when(sec < sections - 1)
    def _():
        for piece in pieces:
            send_dq(*piece).wait_recv()


def pair_kernel(
    sections, first, last, roles,
    pairs_hbm, query, keys, values, attn_out, grad_out,
    key_grad, value_grad, upstream,
    q_buf, o_buf, g_buf, k_raw, v_raw, k_buf, v_buf, d_buf, y_got, s_buf, p_own, p_got, p_out,
    r_one, r_two, r_pack, key_low, key_wide, ds_buf, pr_buf, bias, pair_acc, pair_out, pair_recv, pairs,
    in_sem, kv_sem, low_send, low_recv, dq_sem, one_send, one_recv, block_send, pack_send, give_recv,
    two_recv, pack_recv, swap_sem, met, may_send,
):
    rows, width = q_buf.shape
    dim = k_buf.shape[1]
    heads = width // dim
    span = rows // 2
    seq = 2 * rows
    part = span // 6
    packed = 3 * part
    units = (last - first) // 2
    lag, held = 2, 2
    scale = 1.0 / math.sqrt(dim)
    low, full = jnp.bfloat16, jnp.float32
    me = lax.axis_index("cp")
    sec = lax.axis_index("pp")
    peer = {"cp": 1 - me}
    below = {"pp": jnp.maximum(sec - 1, 0)}
    sends, gets = sec > 0, sec < sections - 1
    upper, lower, every = pl.ds(0, span), pl.ds(span, span), pl.ds(0, rows)

    def remote(src, dst, send, recv, device):
        return pltpu.make_async_remote_copy(
            src_ref=src, dst_ref=dst, send_sem=send, recv_sem=recv, device_id=device, device_id_type=MESH
        )

    def take(ref, sem):
        pltpu.make_async_copy(ref, ref, sem).wait()

    own = [
        pltpu.make_async_copy(keys, k_raw.at[every, :], in_sem.at[0]),
        pltpu.make_async_copy(values, v_raw.at[every, :], in_sem.at[0]),
    ]
    head, rest = pl.ds(0, dim), pl.ds(dim, width - dim)
    wide = ((query, q_buf), (grad_out, g_buf), (attn_out, o_buf))
    begin = [pltpu.make_async_copy(src.at[:, head], dst.at[:, head], in_sem.at[1]) for src, dst in wide]
    later = [pltpu.make_async_copy(src.at[:, rest], dst.at[:, rest], in_sem.at[2 + i]) for i, (src, dst) in enumerate(wide)]
    table = pltpu.make_async_copy(pairs_hbm, pairs, in_sem.at[5])
    other = pl.ds(rows, rows)

    barrier = pltpu.get_barrier_semaphore()

    @pl.when(me == 1)
    def _():
        pl.semaphore_signal(barrier, inc=1, device_id=peer, device_id_type=MESH)

    @pl.when(me == 0)
    def _():
        pl.semaphore_wait(barrier, 1)
        pl.semaphore_signal(met, inc=1, device_id=peer, device_id_type=MESH)
        for src, dst in ((keys, k_raw), (values, v_raw)):
            remote(src, dst.at[other, :], kv_sem.at[0], kv_sem.at[1], peer).start()

    for copy in own + [table] + begin:
        copy.start()

    @pl.when(me == 1)
    def _():
        take(k_raw, in_sem.at[0])
        pl.semaphore_wait(met, 1)
        for buf in (k_raw, v_raw):
            remote(buf.at[every, :], buf.at[other, :], kv_sem.at[0], kv_sem.at[1], peer).start()

        @pl.when(gets)
        def _():
            pl.semaphore_signal(barrier, inc=1, device_id={"pp": sec + 1}, device_id_type=MESH)

    for copy in later:
        copy.start()

    table.wait()
    row = lax.broadcasted_iota(jnp.int32, (rows, seq), 0)
    col = lax.broadcasted_iota(jnp.int32, (rows, seq), 1)
    spans = [pairs[me, 0], pairs[me, 1], pairs[1 - me, 0], pairs[1 - me, 1]]
    q_pos = jnp.where(row < span, spans[0] * span, spans[1] * span - span) + row
    bias[...] = jnp.where(col <= q_pos, 0.0, NEG)
    pair_acc[...] = jnp.zeros_like(pair_acc)
    low_here = spans[0] == 0
    high_here = spans[1] == 0
    here = low_here | high_here

    def block_of(ref, n):
        return ref[n * span:(n + 1) * span, :]

    def of_span(ref, s):
        block = block_of(ref, 0)
        for n in range(1, 4):
            block = jnp.where(spans[n] == s, block_of(ref, n), block)
        return block

    def at_span(ref, s):
        block = block_of(ref, 0)
        for n in range(1, 4):
            block = jnp.where(s == n, block_of(ref, n), block)
        return block

    @pl.when(me == 0)
    def _():
        take(k_raw, in_sem.at[0])

    take(k_raw, kv_sem.at[1])
    for s in range(4):
        k_buf[pl.ds(s * span, span), :] = of_span(k_raw, s)

    half = pl.ds(pl.multiple_of(me * (span // 2), span // 2), span // 2)
    rest_half = pl.ds(pl.multiple_of((1 - me) * (span // 2), span // 2), span // 2)
    send_low = remote(k_buf.at[half, :], key_low.at[half, :], low_send.at[0], low_recv.at[0], below)
    pass_low = remote(key_low.at[half, :], key_low.at[half, :], low_send.at[1], low_recv.at[1], peer)

    @pl.when(sends)
    def _():
        @pl.when(me == 1)
        def _():
            pl.semaphore_wait(barrier, 1)
            pl.semaphore_signal(may_send, inc=1, device_id=peer, device_id_type=MESH)

        @pl.when(me == 0)
        def _():
            pl.semaphore_wait(may_send, 1)

        send_low.start()

    for s in range(4):
        v_buf[pl.ds(s * span, span), :] = of_span(v_raw, s)
    take(q_buf.at[:, pl.ds(0, 3 * dim)], in_sem.at[1])

    def dot(a, b, da, db):
        return lax.dot_general(a, b, (((da,), (db,)), ((), ())), preferred_element_type=full)

    def lanes_of(h, count=1):
        return pl.ds(h * dim if isinstance(h, int) else pl.multiple_of(h * dim, dim), count * dim)

    def lines_of(n, size, count=1):
        return pl.ds(n * size if isinstance(n, int) else pl.multiple_of(n * size, size), count * size)

    def two_blocks(group):
        role = jnp.int32(roles[0])
        for g in range(1, len(roles)):
            role = jnp.where(group >= g, roles[g], role)
        return me == role

    def by_role(group, if_two, if_one):
        pl.when(two_blocks(group))(if_two)
        pl.when(jnp.logical_not(two_blocks(group)))(if_one)

    def send_dq(h, lines):
        return remote(
            d_buf.at[lines, lanes_of(h)], upstream.at[lines, lanes_of(h)], dq_sem.at[0], dq_sem.at[1], below
        )

    def unit_lanes(i):
        return lanes_of(first + 2 * i, 2)

    def unit_lines(i):
        return lines_of(i, 2 * packed)

    def group_of(i):
        return i // 2 if isinstance(i, int) else lax.div(i, 2)

    def send_one(i):
        at = unit_lanes(i)
        return remote(d_buf.at[upper, at], r_one.at[:, at], one_send.at[0], one_recv.at[group_of(i)], below)

    def send_two(i):
        at = unit_lanes(i)
        return remote(s_buf.at[:, at], r_two.at[:, at], block_send.at[1], two_recv.at[group_of(i)], below)

    def send_pack(i):
        at = unit_lines(i)
        return remote(p_out.at[at, :], r_pack.at[at, :], pack_send.at[1], pack_recv.at[group_of(i)], below)

    def give_block(i):
        at = unit_lanes(i)
        return remote(d_buf.at[lower, at], y_got.at[:, at], block_send.at[0], give_recv.at[i], peer)

    def give_pack(i):
        at = unit_lines(i)
        return remote(p_own.at[at, :], p_got.at[at, :], pack_send.at[0], give_recv.at[i], peer)

    def heads_of(g):
        return range(first + 4 * g, min(first + 4 * g + 4, last))

    def group_lanes(g):
        return lanes_of(first + 4 * g, len(heads_of(g)))

    def group_lines(g):
        return pl.ds(4 * g * packed, len(heads_of(g)) * packed)

    def pass_two(g):
        at = group_lanes(g)
        return remote(r_two.at[:, at], r_two.at[:, at], block_send.at[2], two_recv.at[g], peer)

    def pass_pack(g):
        at = group_lines(g)
        return remote(r_pack.at[at, :], r_pack.at[at, :], pack_send.at[2], pack_recv.at[g], peer)

    def gradients(h, lines):
        lanes = lanes_of(h)
        q = q_buf[lines, lanes]
        g = g_buf[lines, lanes]
        delta = jnp.sum(g.astype(full) * o_buf[lines, lanes].astype(full), axis=1, keepdims=True)
        score = dot(q, k_buf[...], 1, 1) * (scale * LOG2E) + bias[lines, :]
        top = jnp.max(score, axis=1, keepdims=True)
        prob = jnp.exp2(score - top)
        prob = prob * (1.0 / jnp.sum(prob, axis=1, keepdims=True))
        dprob = dot(g, v_buf[...], 1, 1)
        dscore = (prob * (dprob - delta) * scale).astype(low)
        place = pl.ds(
            h * rows + lines.start if isinstance(h, int) else pl.multiple_of(h * rows + lines.start, span), lines.size
        )
        pr_buf[place, :] = prob.astype(low)
        ds_buf[place, :] = dscore
        return dscore, dot(dscore, k_buf[...], 1, 0)

    def pair_terms(h, _):
        place = lines_of(h, rows)
        pair_acc[:, :dim] += dot(ds_buf[place, :], q_buf[:, lanes_of(h)], 0, 0)
        pair_acc[:, dim:] += dot(pr_buf[place, :], g_buf[:, lanes_of(h)], 0, 0)
        return 0

    def plain_pieces(pieces, before=None):
        for h, lines in pieces:
            d_buf[lines, lanes_of(h)] = gradients(h, lines)[1].astype(low)

        @pl.when(sends)
        def _():
            if before is not None:
                before()
            for piece in pieces:
                send_dq(*piece).start()

    def pack_head(h):
        lanes = lanes_of(h)
        dscore, dq = gradients(h, every)
        block = jnp.where(high_here, dscore[span:, :dim].astype(full), dscore[:span, :dim].astype(full))
        wide_rows = block[4 * part:] + pltpu.roll(block[:2 * part], 6 * part, 1)
        short_rows = block[3 * part:4 * part] + pltpu.roll(block[2 * part:3 * part], 4 * part, 1)
        p_own[lines_of(h - first, packed), :] = jnp.concatenate([wide_rows, short_rows], axis=0).astype(low)
        d_buf[upper, lanes] = jnp.where(low_here, dq[span:], dq[:span]).astype(low)
        d_buf[lower, lanes] = dq[span:].astype(low)

    def gives(i):
        by_role(group_of(i), lambda: give_pack(i).start(), lambda: give_block(i).start())

    def second_sends(i):
        def two():
            at = unit_lanes(i)
            give_block(i).wait_recv()
            s_buf[:, at] = jnp.where(here, y_got[:, at], d_buf[lower, at])
            send_two(i).start()

        def one():
            at = unit_lines(i)
            give_pack(i).wait_recv()
            p_out[at, :] = jnp.where(here, p_own[at, :], p_got[at, :])
            send_pack(i).start()

        by_role(group_of(i), two, one)

    def packed_unit(i, _):
        pack_head(first + 2 * i)
        pack_head(first + 2 * i + 1)

        @pl.when(sends)
        def _():
            gives(i)

            @pl.when(i < units - held)
            def _():
                send_one(i).start()

            @pl.when(i >= lag)
            def _():
                second_sends(i - lag)

        return 0

    plain_pieces([(0, every)])
    for copy in later:
        copy.wait()
    lax.fori_loop(0, units, packed_unit, 0)

    def waiting():
        for i in range(units - lag, units):
            second_sends(i)
        for i in range(units - held, units):
            send_one(i).start()

    plain_pieces([(h, every) for h in range(last, heads)], waiting)
    lax.fori_loop(0, heads, pair_terms, 0, unroll=2)

    for n in range(2):
        pair_out[lines_of(n, span), :] = at_span(pair_acc, spans[2 + n])
    swap = remote(pair_out, pair_recv, swap_sem.at[0], swap_sem.at[1], peer)
    swap.start()

    def pass_on(g):
        def two():
            take(r_two.at[:, group_lanes(g)], two_recv.at[g])
            pass_two(g).start()

        def one():
            take(r_pack.at[group_lines(g), :], pack_recv.at[g])
            pass_pack(g).start()

        by_role(g, two, one)

    def assemble(g):
        take(r_one.at[:, group_lanes(g)], one_recv.at[g])
        by_role(g, lambda: pass_pack(g).wait_recv(), lambda: pass_two(g).wait_recv())
        for h in heads_of(g):
            lanes = lanes_of(h)
            terms = dot(r_pack[lines_of(h - first, packed), :], key_wide[...], 1, 0)
            opened = jnp.concatenate(
                [
                    terms[:2 * part, dim:2 * dim],
                    terms[2 * part:, 3 * dim:],
                    terms[2 * part:, 2 * dim:3 * dim],
                    terms[:2 * part, :dim],
                ],
                axis=0,
            ).astype(low)
            one = r_one[:, lanes]
            upstream[upper, lanes] = jnp.where(low_here, opened, one)
            upstream[lower, lanes] = jnp.where(low_here, one, jnp.where(high_here, opened, r_two[:, lanes]))

    @pl.when(gets)
    def _():
        send_low.wait_recv()
        pass_low.start()
        pass_on(0)

    swap.wait_recv()
    for n in range(2):
        lines = lines_of(n, span)
        total = at_span(pair_acc, spans[n]) + pair_recv[lines, :]
        key_grad[lines, :] = total[:, :dim].astype(low)
        value_grad[lines, :] = total[:, dim:].astype(low)

    plain = heads - (last - first)

    @pl.when(gets)
    def _():
        take(key_low.at[rest_half, :], low_recv.at[1])
        key_wide[...] = jnp.zeros_like(key_wide)
        key_wide[:6 * part, :dim] = key_low[...]
        key_wide[6 * part:, dim:2 * dim] = key_low[:2 * part, :]
        key_wide[:4 * part, 2 * dim:3 * dim] = key_low[:4 * part, :]
        key_wide[4 * part:7 * part, 3 * dim:] = key_low[:3 * part, :]
        for g in range(1, len(roles)):
            pass_on(g)
            assemble(g - 1)
        assemble(len(roles) - 1)
        pass_low.wait_send()

    @pl.when(jnp.logical_not(gets))
    def _():
        upstream[...] = jnp.zeros_like(upstream)

    take(k_raw, kv_sem.at[0])
    swap.wait_send()

    @pl.when(sends)
    def _():
        send_low.wait_send()
        take(d_buf.at[upper, lanes_of(first, last - first)], one_send.at[0])
        take(d_buf.at[:, lanes_of(0, plain)], dq_sem.at[0])

    def drain(core):
        double = sum(len(heads_of(g)) // 2 for g, role in enumerate(roles) if role == core)
        single = units - double

        def sent(step):
            def blocks(n, at):
                if n:
                    take(s_buf.at[:, lanes_of(0, 2 * n)], block_send.at[at])

            def packs(n, at):
                if n:
                    take(p_out.at[lines_of(0, 2 * packed, n), :], pack_send.at[at])

            blocks(single if step == 0 else double, step)
            packs(double if step == 0 else single, step)

        @pl.when(sends)
        def _():
            sent(0)
            sent(1)

        @pl.when(gets)
        def _():
            sent(2)

    pl.when(me == 0)(lambda: drain(0))
    pl.when(me == 1)(lambda: drain(1))

    @pl.when(gets)
    def _():
        take(upstream.at[:, lanes_of(0, plain)], dq_sem.at[1])


def store(key_grad, value_grad, upstream, key_out, value_out, upstream_out, sem):
    copies = [
        pltpu.make_async_copy(src, dst, sem.at[i])
        for i, (src, dst) in enumerate(
            ((upstream, upstream_out), (key_grad, key_out), (value_grad, value_out))
        )
    ]
    for copy in copies:
        copy.start()
    for copy in copies:
        copy.wait()


def body(query, keys, values, attn_out, grad_out, span_pairs):
    _, rows, width = query.shape
    dim = keys.shape[2]
    heads = width // dim
    ranks = lax.axis_size("cp")
    sections = lax.axis_size("pp")
    seq = ranks * rows
    low, full = jnp.bfloat16, jnp.float32
    dma = pltpu.SemaphoreType.DMA
    vmem = pl.BlockSpec(memory_space=pltpu.VMEM)
    hbm = pl.BlockSpec(memory_space=pltpu.HBM)

    def spaces(*shapes):
        return [pltpu.VMEM(shape, low) for shape in shapes]

    tall, flat, block = (rows, width), (seq, dim), (rows // 2, width)
    if ranks == 2 and sections > 1 and dim == 128 and rows == 192 and heads == 16:
        roles = (1, 1, 1, 1)
        groups, packs = len(roles), ((heads - 2) * (rows // 4), dim)
        run = functools.partial(pair_kernel, sections, 1, heads - 1, roles)
        scratch = (
            spaces(tall, tall, tall, flat, flat, flat, flat, tall, block, block, packs, packs, packs)
            + spaces(block, block, packs, (rows // 2, dim), (dim, 4 * dim))
            + spaces((heads * rows, seq), (heads * rows, seq))
            + [
                pltpu.VMEM((rows, seq), full),
                pltpu.VMEM((seq, 2 * dim), full),
                pltpu.VMEM((rows, 2 * dim), full),
                pltpu.VMEM((rows, 2 * dim), full),
                pltpu.SMEM((ranks, 2), jnp.int32),
            ]
            + [dma((n,)) for n in (6, 2, 2, 2, 2, 1, groups, 3, 3, heads // 2, groups, groups, 2)]
            + [pltpu.SemaphoreType.REGULAR] * 2
        )
    else:
        others = max(ranks - 1, 1)
        run = functools.partial(kernel, ranks, sections, 2 * rows if ranks % 2 == 0 else rows)
        scratch = (
            spaces(tall, tall, tall, flat, flat, tall)
            + [
                pltpu.VMEM((rows, seq), full),
                pltpu.VMEM((2, rows, 1), full),
                pltpu.VMEM((rows, dim), full),
                pltpu.VMEM((seq, 2 * dim), full),
                pltpu.VMEM((others, rows, 2 * dim), full),
                pltpu.SMEM((ranks, 2), jnp.int32),
            ]
            + [dma((9,)), dma((2, others)), dma((2, others)), dma((heads + 1,)), dma((heads + 1,))]
            + [dma((others,)), dma((others,))]
        )
    key_grad, value_grad, upstream = pl.pallas_call(
        run,
        out_shape=(
            pltpu.VMEM((rows, dim), low),
            pltpu.VMEM((rows, dim), low),
            pltpu.VMEM((rows, width), low),
        ),
        in_specs=[hbm] * 6,
        out_specs=(vmem, vmem, vmem),
        scratch_shapes=scratch,
        compiler_params=pltpu.CompilerParams(
            collective_id=0, has_side_effects=True, vmem_limit_bytes=64 * 1024 * 1024 - 1200 * 1024
        ),
        name="backward",
    )(span_pairs, query[0], keys[0], values[0], attn_out[0], grad_out[0])
    anywhere = pl.BlockSpec(memory_space=pl.ANY)
    key_grad, value_grad, upstream = pl.pallas_call(
        store,
        out_shape=(
            jax.ShapeDtypeStruct((rows, dim), low),
            jax.ShapeDtypeStruct((rows, dim), low),
            jax.ShapeDtypeStruct((rows, width), low),
        ),
        in_specs=[anywhere] * 3,
        out_specs=(anywhere,) * 3,
        scratch_shapes=[dma((3,))],
        compiler_params=pltpu.CompilerParams(vmem_limit_bytes=1024 * 1024),
        name="store",
    )(key_grad, value_grad, upstream)
    return key_grad[None], value_grad[None], upstream[None]


def solution(mesh):
    spec = P("pp", "cp", "tp")
    return jax.shard_map(
        body,
        mesh=mesh,
        in_specs=(spec, spec, spec, spec, spec, P()),
        out_specs=(spec, spec, spec),
        check_vma=False,
    )
```

```python
import functools
import math

import jax
import jax.numpy as jnp
from jax import lax
from jax.experimental import pallas as pl
from jax.experimental.pallas import tpu as pltpu
from jax.sharding import PartitionSpec as P

MESH = pl.DeviceIdType.MESH
NEG = -1e30
LOG2E = math.log2(math.e)


def kernel(
    ranks, sections, block_len,
    pairs_hbm, query, keys, values, attn_out, grad_out,
    key_grad, value_grad, upstream,
    q_buf, o_buf, g_buf, k_buf, v_buf, dq_buf, bias, stats, dq_acc, pair_acc, pair_recv,
    pairs, in_sem, kv_send, kv_recv, dq_send, dq_recv, pair_send, pair_got,
):
    rows, width = q_buf.shape
    dim = k_buf.shape[1]
    heads = width // dim
    span = rows // 2
    seq = ranks * rows
    blocks = seq // block_len
    scale = 1.0 / math.sqrt(dim)
    me = lax.axis_index("cp")
    sec = lax.axis_index("pp")
    mine = pl.ds(0, rows)

    barrier = pltpu.get_barrier_semaphore()
    for off in range(1, ranks):
        pl.semaphore_signal(
            barrier, inc=1, device_id={"cp": lax.rem(me + off, ranks)}, device_id_type=MESH
        )

    @pl.when(sec < sections - 1)
    def _():
        pl.semaphore_signal(barrier, inc=1, device_id={"pp": sec + 1}, device_id_type=MESH)

    own = [
        pltpu.make_async_copy(keys, k_buf.at[mine, :], in_sem.at[0]),
        pltpu.make_async_copy(values, v_buf.at[mine, :], in_sem.at[1]),
    ]
    first, rest = pl.ds(0, dim), pl.ds(dim, width - dim)
    wide = ((query, q_buf), (grad_out, g_buf), (attn_out, o_buf))
    begin = [
        pltpu.make_async_copy(src.at[:, first], dst.at[:, first], in_sem.at[2 + i])
        for i, (src, dst) in enumerate(wide)
    ]
    later = [
        pltpu.make_async_copy(src.at[:, rest], dst.at[:, rest], in_sem.at[5 + i])
        for i, (src, dst) in enumerate(wide)
    ]
    table = pltpu.make_async_copy(pairs_hbm, pairs, in_sem.at[8])
    for copy in [table] + own + begin:
        copy.start()

    pl.semaphore_wait(barrier, ranks - 1 + (sec > 0).astype(jnp.int32))
    sent = []
    for off in range(1, ranks):
        for which, (src, buf) in enumerate(((keys, k_buf), (values, v_buf))):
            sent.append(
                pltpu.make_async_remote_copy(
                    src_ref=src,
                    dst_ref=buf.at[pl.ds((ranks - off) * rows, rows), :],
                    send_sem=kv_send.at[which, off - 1],
                    recv_sem=kv_recv.at[which, off - 1],
                    device_id={"cp": lax.rem(me + off, ranks)},
                    device_id_type=MESH,
                )
            )
    for copy in sent + later:
        copy.start()

    table.wait()
    row = lax.broadcasted_iota(jnp.int32, (rows, rows), 0)
    col = lax.broadcasted_iota(jnp.int32, (rows, rows), 1)
    q_pos = jnp.where(row < span, pairs[me, 0] * span, pairs[me, 1] * span - span) + row
    for r in range(ranks):
        rank = lax.rem(me + r, ranks)
        k_pos = jnp.where(col < span, pairs[rank, 0] * span, pairs[rank, 1] * span - span) + col
        bias[:, r * rows:(r + 1) * rows] = jnp.where(k_pos <= q_pos, 0.0, NEG)
    pair_acc[...] = jnp.zeros_like(pair_acc)

    for copy in own + begin:
        copy.wait()
    for copy in sent:
        copy.wait_recv()

    def dot(a, b, da, db):
        return lax.dot_general(a, b, (((da,), (db,)), ((), ())), preferred_element_type=jnp.float32)

    def lanes_of(h):
        return pl.ds(h * dim if isinstance(h, int) else pl.multiple_of(h * dim, dim), dim)

    def send_dq(h, lines, slot):
        return pltpu.make_async_remote_copy(
            src_ref=dq_buf.at[lines, lanes_of(h)],
            dst_ref=upstream.at[lines, lanes_of(h)],
            send_sem=dq_send.at[slot],
            recv_sem=dq_recv.at[slot],
            device_id={"pp": jnp.maximum(sec - 1, 0)},
            device_id_type=MESH,
        )

    def rows_of_head(h, lines, slot):
        lanes = lanes_of(h)
        q = q_buf[lines, lanes]
        g = g_buf[lines, lanes]
        delta = jnp.sum(
            g.astype(jnp.float32) * o_buf[lines, lanes].astype(jnp.float32), axis=1, keepdims=True
        )

        def scores(b):
            at = b * block_len if isinstance(b, int) else pl.multiple_of(b * block_len, block_len)
            part = pl.ds(at, block_len)
            return part, dot(q, k_buf[part, :], 1, 1) * (scale * LOG2E) + bias[lines, part]

        def terms(part, prob):
            dprob = dot(g, v_buf[part, :], 1, 1)
            dscore = (prob * (dprob - delta) * scale).astype(jnp.bfloat16)
            return prob.astype(jnp.bfloat16), dscore, dot(dscore, k_buf[part, :], 1, 0)

        def pair_terms(part, prob_low, dscore):
            pair_acc[part, :dim] += dot(dscore, q, 0, 0)
            pair_acc[part, dim:] += dot(prob_low, g, 0, 0)

        def start_dq(dq):
            dq_buf[lines, lanes] = dq.astype(jnp.bfloat16)

            @pl.when(sec > 0)
            def _():
                send_dq(h, lines, slot).start()

        if blocks == 1:
            part, score = scores(0)
            top = jnp.max(score, axis=1, keepdims=True)
            prob = jnp.exp2(score - top)
            prob = prob * (1.0 / jnp.sum(prob, axis=1, keepdims=True))
            prob_low, dscore, dq = terms(part, prob)
            start_dq(dq)
            pair_terms(part, prob_low, dscore)
        else:
            stats[0, lines] = jnp.full((lines.size, 1), NEG, jnp.float32)
            stats[1, lines] = jnp.zeros((lines.size, 1), jnp.float32)
            dq_acc[lines] = jnp.zeros((lines.size, dim), jnp.float32)

            def gather_stats(b, _):
                _, score = scores(b)
                before = stats[0, lines]
                top = jnp.maximum(before, jnp.max(score, axis=1, keepdims=True))
                mass = jnp.sum(jnp.exp2(score - top), axis=1, keepdims=True)
                stats[1, lines] = stats[1, lines] * jnp.exp2(before - top) + mass
                stats[0, lines] = top
                return 0

            def gather_terms(b, _):
                part, score = scores(b)
                prob = jnp.exp2(score - stats[0, lines]) * (1.0 / stats[1, lines])
                prob_low, dscore, dq = terms(part, prob)
                dq_acc[lines] += dq
                pair_terms(part, prob_low, dscore)
                return 0

            lax.fori_loop(0, blocks, gather_stats, 0)
            lax.fori_loop(0, blocks, gather_terms, 0)
            start_dq(dq_acc[lines])

    pieces = [(h, pl.ds(0, rows), h) for h in range(heads)]
    for piece in pieces[:1]:
        rows_of_head(*piece)

    @pl.when(sec == sections - 1)
    def _():
        upstream[...] = jnp.zeros_like(upstream)

    for copy in later:
        copy.wait()

    def one_head(h, _):
        rows_of_head(h, pl.ds(0, rows), h)
        return 0

    lax.fori_loop(1, heads, one_head, 0)

    pair_sent = []
    for off in range(1, ranks):
        dst = lax.rem(me + off, ranks)
        pair_sent.append(
            pltpu.make_async_remote_copy(
                src_ref=pair_acc.at[pl.ds(off * rows, rows), :],
                dst_ref=pair_recv.at[off - 1],
                send_sem=pair_send.at[off - 1],
                recv_sem=pair_got.at[off - 1],
                device_id={"cp": dst},
                device_id_type=MESH,
            )
        )
    for copy in pair_sent:
        copy.start()
    for copy in sent:
        copy.wait_send()
    for copy in pair_sent:
        copy.wait_recv()
    total = pair_acc[mine, :]
    for off in range(1, ranks):
        total = total + pair_recv[off - 1]
    key_grad[...] = total[:, :dim].astype(jnp.bfloat16)
    value_grad[...] = total[:, dim:].astype(jnp.bfloat16)
    for copy in pair_sent:
        copy.wait_send()

    @pl.when(sec > 0)
    def _():
        for piece in pieces:
            send_dq(*piece).wait_send()

    @pl.when(sec < sections - 1)
    def _():
        for piece in pieces:
            send_dq(*piece).wait_recv()


def pair_kernel(
    sections, first, last, roles,
    pairs_hbm, query, keys, values, attn_out, grad_out,
    key_grad, value_grad, upstream,
    q_buf, o_buf, g_buf, k_raw, v_raw, k_buf, v_buf, d_buf, y_got, s_buf, p_own, p_got, p_out,
    r_one, r_two, r_pack, key_low, key_wide, ds_buf, pr_buf, bias, pair_acc, pair_out, pair_recv, pairs,
    in_sem, kv_sem, low_send, low_recv, dq_sem, one_send, one_recv, block_send, pack_send, give_recv,
    two_recv, pack_recv, swap_sem, relay_buf, relay_sem, met, may_send, here_too, may_relay, may_detour,
):
    rows, width = q_buf.shape
    dim = k_buf.shape[1]
    heads = width // dim
    span = rows // 2
    seq = 2 * rows
    tile = span // 12
    bins = ((12, 4), (11, 5), (10, 6), (9, 7), (8, 3, 2, 1))
    packed = tile * len(bins)
    units = (last - first) // 2
    lag, held, relayed = 2, 2, 2
    scale = 1.0 / math.sqrt(dim)
    low, full = jnp.bfloat16, jnp.float32
    me = lax.axis_index("cp")
    sec = lax.axis_index("pp")
    peer = {"cp": 1 - me}
    below = {"pp": jnp.maximum(sec - 1, 0)}
    sends, gets = sec > 0, sec < sections - 1
    tp = lax.axis_index("tp")
    early = (sec == 0) & (tp == 0)
    relays = (sec == 0) & (tp == 1 + me)
    detours = (sec == 1) & (tp == 0)
    upper, lower, every = pl.ds(0, span), pl.ds(span, span), pl.ds(0, rows)

    def remote(src, dst, send, recv, device):
        return pltpu.make_async_remote_copy(
            src_ref=src, dst_ref=dst, send_sem=send, recv_sem=recv, device_id=device, device_id_type=MESH
        )

    def take(ref, sem):
        pltpu.make_async_copy(ref, ref, sem).wait()

    own = [
        pltpu.make_async_copy(keys, k_raw.at[every, :], in_sem.at[0]),
        pltpu.make_async_copy(values, v_raw.at[every, :], in_sem.at[0]),
    ]
    head, rest = pl.ds(0, dim), pl.ds(dim, width - dim)
    wide = ((query, q_buf), (grad_out, g_buf), (attn_out, o_buf))
    begin = [pltpu.make_async_copy(src.at[:, head], dst.at[:, head], in_sem.at[1]) for src, dst in wide]
    later = [pltpu.make_async_copy(src.at[:, rest], dst.at[:, rest], in_sem.at[2 + i]) for i, (src, dst) in enumerate(wide)]
    table = pltpu.make_async_copy(pairs_hbm, pairs, in_sem.at[5])
    other = pl.ds(rows, rows)

    barrier = pltpu.get_barrier_semaphore()

    @pl.when(me == 1)
    def _():
        pl.semaphore_signal(barrier, inc=1, device_id=peer, device_id_type=MESH)

    @pl.when(me == 0)
    def _():
        pl.semaphore_wait(barrier, 1)
        pl.semaphore_signal(met, inc=1, device_id=peer, device_id_type=MESH)
        for src, dst in ((keys, k_raw), (values, v_raw)):
            remote(src, dst.at[other, :], kv_sem.at[0], kv_sem.at[1], peer).start()

    for copy in own + [table] + begin:
        copy.start()

    @pl.when(me == 1)
    def _():
        take(k_raw, in_sem.at[0])
        pl.semaphore_wait(met, 1)
        for buf in (k_raw, v_raw):
            remote(buf.at[every, :], buf.at[other, :], kv_sem.at[0], kv_sem.at[1], peer).start()

        @pl.when(gets)
        def _():
            pl.semaphore_signal(barrier, inc=1, device_id={"pp": sec + 1}, device_id_type=MESH)

        @pl.when((sec == 0) & ((tp == 1) | (tp == 2)))
        def _():
            pl.semaphore_signal(barrier, inc=1, device_id={"tp": 0}, device_id_type=MESH)

    for copy in later:
        copy.start()

    table.wait()
    row = lax.broadcasted_iota(jnp.int32, (rows, seq), 0)
    col = lax.broadcasted_iota(jnp.int32, (rows, seq), 1)
    spans = [pairs[me, 0], pairs[me, 1], pairs[1 - me, 0], pairs[1 - me, 1]]
    q_pos = jnp.where(row < span, spans[0] * span, spans[1] * span - span) + row
    bias[...] = jnp.where(col <= q_pos, 0.0, NEG)
    pair_acc[...] = jnp.zeros_like(pair_acc)
    low_here = spans[0] == 0
    high_here = spans[1] == 0
    here = low_here | high_here

    def block_of(ref, n):
        return ref[n * span:(n + 1) * span, :]

    def of_span(ref, s):
        block = block_of(ref, 0)
        for n in range(1, 4):
            block = jnp.where(spans[n] == s, block_of(ref, n), block)
        return block

    def at_span(ref, s):
        block = block_of(ref, 0)
        for n in range(1, 4):
            block = jnp.where(s == n, block_of(ref, n), block)
        return block

    @pl.when(me == 0)
    def _():
        take(k_raw, in_sem.at[0])

    take(k_raw, kv_sem.at[1])
    for s in range(4):
        k_buf[pl.ds(s * span, span), :] = of_span(k_raw, s)

    half = pl.ds(pl.multiple_of(me * (span // 2), span // 2), span // 2)
    rest_half = pl.ds(pl.multiple_of((1 - me) * (span // 2), span // 2), span // 2)
    send_low = remote(k_buf.at[half, :], key_low.at[half, :], low_send.at[0], low_recv.at[0], below)
    pass_low = remote(key_low.at[half, :], key_low.at[half, :], low_send.at[1], low_recv.at[1], peer)

    @pl.when(sends)
    def _():
        @pl.when(me == 1)
        def _():
            pl.semaphore_wait(barrier, 1)
            pl.semaphore_signal(may_send, inc=1, device_id=peer, device_id_type=MESH)

            @pl.when(detours)
            def _():
                pl.semaphore_signal(here_too, inc=1, device_id=below, device_id_type=MESH)

        @pl.when(me == 0)
        def _():
            pl.semaphore_wait(may_send, 1)

        send_low.start()

    for s in range(4):
        v_buf[pl.ds(s * span, span), :] = of_span(v_raw, s)
    take(q_buf.at[:, pl.ds(0, 3 * dim)], in_sem.at[1])

    def dot(a, b, da, db):
        return lax.dot_general(a, b, (((da,), (db,)), ((), ())), preferred_element_type=full)

    def lanes_of(h, count=1):
        return pl.ds(h * dim if isinstance(h, int) else pl.multiple_of(h * dim, dim), count * dim)

    def lines_of(n, size, count=1):
        return pl.ds(n * size if isinstance(n, int) else pl.multiple_of(n * size, size), count * size)

    def two_blocks(group):
        role = jnp.int32(roles[0])
        for g in range(1, len(roles)):
            role = jnp.where(group >= g, roles[g], role)
        return me == role

    def by_role(group, if_two, if_one):
        pl.when(two_blocks(group))(if_two)
        pl.when(jnp.logical_not(two_blocks(group)))(if_one)

    def send_dq(h, lines):
        return remote(
            d_buf.at[lines, lanes_of(h)], upstream.at[lines, lanes_of(h)], dq_sem.at[0], dq_sem.at[1], below
        )

    def unit_lanes(i):
        return lanes_of(first + 2 * i, 2)

    def unit_lines(i):
        return lines_of(i, 2 * packed)

    def group_of(i):
        return i // 2 if isinstance(i, int) else lax.div(i, 2)

    def send_one(i):
        at = unit_lanes(i)
        return remote(d_buf.at[upper, at], r_one.at[:, at], one_send.at[0], one_recv.at[group_of(i)], below)

    def send_two(i):
        at = unit_lanes(i)
        return remote(s_buf.at[:, at], r_two.at[:, at], block_send.at[1], two_recv.at[group_of(i)], below)

    def send_pack(i):
        at = unit_lines(i)
        return remote(p_out.at[at, :], r_pack.at[at, :], pack_send.at[1], pack_recv.at[group_of(i)], below)

    def give_block(i):
        at = unit_lanes(i)
        return remote(d_buf.at[lower, at], y_got.at[:, at], block_send.at[0], give_recv.at[i], peer)

    def give_pack(i):
        at = unit_lines(i)
        return remote(p_own.at[at, :], p_got.at[at, :], pack_send.at[0], give_recv.at[i], peer)

    def heads_of(g):
        return range(first + 4 * g, min(first + 4 * g + 4, last))

    def group_lanes(g):
        return lanes_of(first + 4 * g, len(heads_of(g)))

    def group_lines(g):
        return pl.ds(4 * g * packed, len(heads_of(g)) * packed)

    def pass_two(g):
        at = group_lanes(g)
        return remote(r_two.at[:, at], r_two.at[:, at], block_send.at[2], two_recv.at[g], peer)

    def pass_pack(g):
        at = group_lines(g)
        return remote(r_pack.at[at, :], r_pack.at[at, :], pack_send.at[2], pack_recv.at[g], peer)

    def gradients(h, lines):
        lanes = lanes_of(h)
        q = q_buf[lines, lanes]
        g = g_buf[lines, lanes]
        delta = jnp.sum(g.astype(full) * o_buf[lines, lanes].astype(full), axis=1, keepdims=True)
        score = dot(q, k_buf[...], 1, 1) * (scale * LOG2E) + bias[lines, :]
        top = jnp.max(score, axis=1, keepdims=True)
        prob = jnp.exp2(score - top)
        prob = prob * (1.0 / jnp.sum(prob, axis=1, keepdims=True))
        dprob = dot(g, v_buf[...], 1, 1)
        dscore = (prob * (dprob - delta) * scale).astype(low)
        place = pl.ds(
            h * rows + lines.start if isinstance(h, int) else pl.multiple_of(h * rows + lines.start, span), lines.size
        )
        pr_buf[place, :] = prob.astype(low)
        ds_buf[place, :] = dscore
        return dscore, dot(dscore, k_buf[...], 1, 0)

    def pair_terms(h, _):
        place = lines_of(h, rows)
        pair_acc[:, :dim] += dot(ds_buf[place, :], q_buf[:, lanes_of(h)], 0, 0)
        pair_acc[:, dim:] += dot(pr_buf[place, :], g_buf[:, lanes_of(h)], 0, 0)
        return 0

    def plain_pieces(pieces, before=None):
        for h, lines in pieces:
            d_buf[lines, lanes_of(h)] = gradients(h, lines)[1].astype(low)

        @pl.when(sends)
        def _():
            if before is not None:
                before()
            for piece in pieces:
                send_dq(*piece).start()

    near, far = lanes_of(first + 2 * relayed), lanes_of(first + 2 * relayed + 1)
    relayed_recv = one_recv.at[group_of(relayed)]
    detour = remote(d_buf.at[upper, far], relay_buf, one_send.at[0], relay_sem.at[0], {"pp": 0, "tp": 1 + me})
    relay = remote(relay_buf, r_one.at[:, far], relay_sem.at[1], relayed_recv, {"tp": 0})

    def send_half():
        return remote(d_buf.at[upper, near], r_one.at[:, near], one_send.at[0], relayed_recv, below)

    def pack_head(h):
        lanes = lanes_of(h)
        dscore, dq = gradients(h, every)
        d_buf[upper, lanes] = jnp.where(low_here, dq[span:], dq[:span]).astype(low)
        d_buf[lower, lanes] = dq[span:].astype(low)
        block = jnp.where(high_here, dscore[span:, :dim].astype(full), dscore[:span, :dim].astype(full))
        lines = []
        for group in bins:
            line, at = 0.0, 0
            for n in group:
                entry = block[(n - 1) * tile:n * tile]
                line = line + (pltpu.roll(entry, at, 1) if at else entry)
                at += n * tile
            lines.append(line)
        return lines

    def unpack_head(lines):
        lane = lax.broadcasted_iota(jnp.int32, (tile, dim), 1)
        entries = {}
        for b, group in enumerate(bins):
            line, at = lines[b * tile:(b + 1) * tile], 0
            for n in group:
                entry = pltpu.roll(line, dim - at, 1) if at else line
                entries[n] = jnp.where(lane < n * tile, entry, 0.0)
                at += n * tile
        return [entries[n] for n in range(1, 13)]

    def gives(i):
        by_role(group_of(i), lambda: give_pack(i).start(), lambda: give_block(i).start())

    def second_sends(i):
        def two():
            at = unit_lanes(i)
            give_block(i).wait_recv()
            s_buf[:, at] = jnp.where(here, y_got[:, at], d_buf[lower, at])
            send_two(i).start()

        def one():
            at = unit_lines(i)
            give_pack(i).wait_recv()
            p_out[at, :] = jnp.where(here, p_own[at, :], p_got[at, :])
            send_pack(i).start()

        by_role(group_of(i), two, one)

    def packed_unit(i, _):
        lines = pack_head(first + 2 * i) + pack_head(first + 2 * i + 1)
        p_own[unit_lines(i), :] = jnp.concatenate(lines, axis=0).astype(low)

        @pl.when(sends)
        def _():
            gives(i)

            @pl.when((i < units - held) & jnp.logical_not(detours & (i == relayed)))
            def _():
                send_one(i).start()

            @pl.when(detours & (i == relayed))
            def _():
                send_half().start()
                pl.semaphore_wait(may_detour, 1)
                detour.start()

            @pl.when(i >= lag)
            def _():
                second_sends(i - lag)

        return 0

    plain_pieces([(0, every)])

    @pl.when(early & (me == 1))
    def _():
        pl.semaphore_wait(barrier, 2)
        pl.semaphore_wait(here_too, 1)
        for core in range(2):
            for sem, to in ((may_relay, {"tp": 1 + core, "cp": core}), (may_detour, {"pp": 1, "cp": core})):
                pl.semaphore_signal(sem, inc=1, device_id=to, device_id_type=MESH)

    for copy in later:
        copy.wait()
    lax.fori_loop(0, units, packed_unit, 0)

    def waiting():
        for i in range(units - lag, units):
            second_sends(i)
        for i in range(units - held, units):
            send_one(i).start()

    plain_pieces([(h, every) for h in range(last, heads)], waiting)

    @pl.when(relays)
    def _():
        take(relay_buf, relay_sem.at[0])
        pl.semaphore_wait(may_relay, 1)
        relay.start()

    lax.fori_loop(0, heads, pair_terms, 0, unroll=2)

    for n in range(2):
        pair_out[lines_of(n, span), :] = at_span(pair_acc, spans[2 + n])
    swap = remote(pair_out, pair_recv, swap_sem.at[0], swap_sem.at[1], peer)
    swap.start()

    def pass_on(g):
        def two():
            take(r_two.at[:, group_lanes(g)], two_recv.at[g])
            pass_two(g).start()

        def one():
            take(r_pack.at[group_lines(g), :], pack_recv.at[g])
            pass_pack(g).start()

        by_role(g, two, one)

    def assemble(g):
        take(r_one.at[:, group_lanes(g)], one_recv.at[g])
        by_role(g, lambda: pass_pack(g).wait_recv(), lambda: pass_two(g).wait_recv())
        for h in heads_of(g)[::2]:
            lines = r_pack[pl.ds((h - first) * packed, 2 * packed), :].astype(full)
            block = unpack_head(lines[:packed]) + unpack_head(lines[packed:])
            both = dot(jnp.concatenate(block, axis=0).astype(low), key_wide[...], 1, 0).astype(low)
            for n in range(2):
                lanes = lanes_of(h + n)
                opened = both[n * span:(n + 1) * span]
                one = r_one[:, lanes]
                upstream[upper, lanes] = jnp.where(low_here, opened, one)
                upstream[lower, lanes] = jnp.where(low_here, one, jnp.where(high_here, opened, r_two[:, lanes]))

    @pl.when(gets)
    def _():
        send_low.wait_recv()
        pass_low.start()
        pass_on(0)

    swap.wait_recv()
    for n in range(2):
        lines = lines_of(n, span)
        total = at_span(pair_acc, spans[n]) + pair_recv[lines, :]
        key_grad[lines, :] = total[:, :dim].astype(low)
        value_grad[lines, :] = total[:, dim:].astype(low)

    plain = heads - (last - first)

    @pl.when(gets)
    def _():
        take(key_low.at[rest_half, :], low_recv.at[1])
        key_wide[span:, :] = jnp.zeros((dim - span, dim), low)
        key_wide[:span, :] = key_low[...]
        for g in range(1, len(roles)):
            pass_on(g)
            assemble(g - 1)
        assemble(len(roles) - 1)
        pass_low.wait_send()

    @pl.when(jnp.logical_not(gets))
    def _():
        upstream[...] = jnp.zeros_like(upstream)

    take(k_raw, kv_sem.at[0])
    swap.wait_send()

    @pl.when(relays)
    def _():
        relay.wait_send()

    @pl.when(sends)
    def _():
        send_low.wait_send()
        take(d_buf.at[upper, lanes_of(first, last - first)], one_send.at[0])
        take(d_buf.at[:, lanes_of(0, plain)], dq_sem.at[0])

    def drain(core):
        double = sum(len(heads_of(g)) // 2 for g, role in enumerate(roles) if role == core)
        single = units - double

        def sent(step):
            def blocks(n, at):
                if n:
                    take(s_buf.at[:, lanes_of(0, 2 * n)], block_send.at[at])

            def packs(n, at):
                if n:
                    take(p_out.at[lines_of(0, 2 * packed, n), :], pack_send.at[at])

            blocks(single if step == 0 else double, step)
            packs(double if step == 0 else single, step)

        @pl.when(sends)
        def _():
            sent(0)
            sent(1)

        @pl.when(gets)
        def _():
            sent(2)

    pl.when(me == 0)(lambda: drain(0))
    pl.when(me == 1)(lambda: drain(1))

    @pl.when(gets)
    def _():
        take(upstream.at[:, lanes_of(0, plain)], dq_sem.at[1])


def store(key_grad, value_grad, upstream, key_out, value_out, upstream_out, sem):
    copies = [
        pltpu.make_async_copy(src, dst, sem.at[i])
        for i, (src, dst) in enumerate(
            ((upstream, upstream_out), (key_grad, key_out), (value_grad, value_out))
        )
    ]
    for copy in copies:
        copy.start()
    for copy in copies:
        copy.wait()


def body(query, keys, values, attn_out, grad_out, span_pairs):
    _, rows, width = query.shape
    dim = keys.shape[2]
    heads = width // dim
    ranks = lax.axis_size("cp")
    sections = lax.axis_size("pp")
    seq = ranks * rows
    low, full = jnp.bfloat16, jnp.float32
    dma = pltpu.SemaphoreType.DMA
    vmem = pl.BlockSpec(memory_space=pltpu.VMEM)
    hbm = pl.BlockSpec(memory_space=pltpu.HBM)

    def spaces(*shapes):
        return [pltpu.VMEM(shape, low) for shape in shapes]

    tall, flat, block = (rows, width), (seq, dim), (rows // 2, width)
    if ranks == 2 and lax.axis_size("tp") > 2 and sections > 1 and dim == 128 and rows == 192 and heads == 16:
        roles = (1, 1, 1, 1)
        groups, packs = len(roles), ((heads - 2) * (5 * rows // 24), dim)
        run = functools.partial(pair_kernel, sections, 1, heads - 1, roles)
        scratch = (
            spaces(tall, tall, tall, flat, flat, flat, flat, tall, block, block, packs, packs, packs)
            + spaces(block, block, packs, (rows // 2, dim), (dim, dim))
            + spaces((heads * rows, seq), (heads * rows, seq))
            + [
                pltpu.VMEM((rows, seq), full),
                pltpu.VMEM((seq, 2 * dim), full),
                pltpu.VMEM((rows, 2 * dim), full),
                pltpu.VMEM((rows, 2 * dim), full),
                pltpu.SMEM((ranks, 2), jnp.int32),
            ]
            + [dma((n,)) for n in (6, 2, 2, 2, 2, 1, groups, 3, 3, heads // 2, groups, groups, 2)]
            + [pltpu.VMEM((rows // 2, dim), low), dma((2,))]
            + [pltpu.SemaphoreType.REGULAR] * 5
        )
    else:
        others = max(ranks - 1, 1)
        run = functools.partial(kernel, ranks, sections, 2 * rows if ranks % 2 == 0 else rows)
        scratch = (
            spaces(tall, tall, tall, flat, flat, tall)
            + [
                pltpu.VMEM((rows, seq), full),
                pltpu.VMEM((2, rows, 1), full),
                pltpu.VMEM((rows, dim), full),
                pltpu.VMEM((seq, 2 * dim), full),
                pltpu.VMEM((others, rows, 2 * dim), full),
                pltpu.SMEM((ranks, 2), jnp.int32),
            ]
            + [dma((9,)), dma((2, others)), dma((2, others)), dma((heads + 1,)), dma((heads + 1,))]
            + [dma((others,)), dma((others,))]
        )
    key_grad, value_grad, upstream = pl.pallas_call(
        run,
        out_shape=(
            pltpu.VMEM((rows, dim), low),
            pltpu.VMEM((rows, dim), low),
            pltpu.VMEM((rows, width), low),
        ),
        in_specs=[hbm] * 6,
        out_specs=(vmem, vmem, vmem),
        scratch_shapes=scratch,
        compiler_params=pltpu.CompilerParams(
            collective_id=0, has_side_effects=True, vmem_limit_bytes=64 * 1024 * 1024 - 1200 * 1024
        ),
        name="backward",
    )(span_pairs, query[0], keys[0], values[0], attn_out[0], grad_out[0])
    anywhere = pl.BlockSpec(memory_space=pl.ANY)
    key_grad, value_grad, upstream = pl.pallas_call(
        store,
        out_shape=(
            jax.ShapeDtypeStruct((rows, dim), low),
            jax.ShapeDtypeStruct((rows, dim), low),
            jax.ShapeDtypeStruct((rows, width), low),
        ),
        in_specs=[anywhere] * 3,
        out_specs=(anywhere,) * 3,
        scratch_shapes=[dma((3,))],
        compiler_params=pltpu.CompilerParams(vmem_limit_bytes=1024 * 1024),
        name="store",
    )(key_grad, value_grad, upstream)
    return key_grad[None], value_grad[None], upstream[None]


def solution(mesh):
    spec = P("pp", "cp", "tp")
    return jax.shard_map(
        body,
        mesh=mesh,
        in_specs=(spec, spec, spec, spec, spec, P()),
        out_specs=(spec, spec, spec),
        check_vma=False,
    )
```

```python
import functools
import math

import jax
import jax.numpy as jnp
from jax import lax
from jax.experimental import pallas as pl
from jax.experimental.pallas import tpu as pltpu
from jax.sharding import PartitionSpec as P

MESH = pl.DeviceIdType.MESH
NEG = -1e30
LOG2E = math.log2(math.e)


def kernel(
    ranks, sections, block_len,
    pairs_hbm, query, keys, values, attn_out, grad_out,
    key_grad, value_grad, upstream,
    q_buf, o_buf, g_buf, k_buf, v_buf, dq_buf, bias, stats, dq_acc, pair_acc, pair_recv,
    pairs, in_sem, kv_send, kv_recv, dq_send, dq_recv, pair_send, pair_got,
):
    rows, width = q_buf.shape
    dim = k_buf.shape[1]
    heads = width // dim
    span = rows // 2
    seq = ranks * rows
    blocks = seq // block_len
    scale = 1.0 / math.sqrt(dim)
    me = lax.axis_index("cp")
    sec = lax.axis_index("pp")
    mine = pl.ds(0, rows)

    barrier = pltpu.get_barrier_semaphore()
    for off in range(1, ranks):
        pl.semaphore_signal(
            barrier, inc=1, device_id={"cp": lax.rem(me + off, ranks)}, device_id_type=MESH
        )

    @pl.when(sec < sections - 1)
    def _():
        pl.semaphore_signal(barrier, inc=1, device_id={"pp": sec + 1}, device_id_type=MESH)

    own = [
        pltpu.make_async_copy(keys, k_buf.at[mine, :], in_sem.at[0]),
        pltpu.make_async_copy(values, v_buf.at[mine, :], in_sem.at[1]),
    ]
    first, rest = pl.ds(0, dim), pl.ds(dim, width - dim)
    wide = ((query, q_buf), (grad_out, g_buf), (attn_out, o_buf))
    begin = [
        pltpu.make_async_copy(src.at[:, first], dst.at[:, first], in_sem.at[2 + i])
        for i, (src, dst) in enumerate(wide)
    ]
    later = [
        pltpu.make_async_copy(src.at[:, rest], dst.at[:, rest], in_sem.at[5 + i])
        for i, (src, dst) in enumerate(wide)
    ]
    table = pltpu.make_async_copy(pairs_hbm, pairs, in_sem.at[8])
    for copy in [table] + own + begin:
        copy.start()

    pl.semaphore_wait(barrier, ranks - 1 + (sec > 0).astype(jnp.int32))
    sent = []
    for off in range(1, ranks):
        for which, (src, buf) in enumerate(((keys, k_buf), (values, v_buf))):
            sent.append(
                pltpu.make_async_remote_copy(
                    src_ref=src,
                    dst_ref=buf.at[pl.ds((ranks - off) * rows, rows), :],
                    send_sem=kv_send.at[which, off - 1],
                    recv_sem=kv_recv.at[which, off - 1],
                    device_id={"cp": lax.rem(me + off, ranks)},
                    device_id_type=MESH,
                )
            )
    for copy in sent + later:
        copy.start()

    table.wait()
    row = lax.broadcasted_iota(jnp.int32, (rows, rows), 0)
    col = lax.broadcasted_iota(jnp.int32, (rows, rows), 1)
    q_pos = jnp.where(row < span, pairs[me, 0] * span, pairs[me, 1] * span - span) + row
    for r in range(ranks):
        rank = lax.rem(me + r, ranks)
        k_pos = jnp.where(col < span, pairs[rank, 0] * span, pairs[rank, 1] * span - span) + col
        bias[:, r * rows:(r + 1) * rows] = jnp.where(k_pos <= q_pos, 0.0, NEG)
    pair_acc[...] = jnp.zeros_like(pair_acc)

    for copy in own + begin:
        copy.wait()
    for copy in sent:
        copy.wait_recv()

    def dot(a, b, da, db):
        return lax.dot_general(a, b, (((da,), (db,)), ((), ())), preferred_element_type=jnp.float32)

    def lanes_of(h):
        return pl.ds(h * dim if isinstance(h, int) else pl.multiple_of(h * dim, dim), dim)

    def send_dq(h, lines, slot):
        return pltpu.make_async_remote_copy(
            src_ref=dq_buf.at[lines, lanes_of(h)],
            dst_ref=upstream.at[lines, lanes_of(h)],
            send_sem=dq_send.at[slot],
            recv_sem=dq_recv.at[slot],
            device_id={"pp": jnp.maximum(sec - 1, 0)},
            device_id_type=MESH,
        )

    def rows_of_head(h, lines, slot):
        lanes = lanes_of(h)
        q = q_buf[lines, lanes]
        g = g_buf[lines, lanes]
        delta = jnp.sum(
            g.astype(jnp.float32) * o_buf[lines, lanes].astype(jnp.float32), axis=1, keepdims=True
        )

        def scores(b):
            at = b * block_len if isinstance(b, int) else pl.multiple_of(b * block_len, block_len)
            part = pl.ds(at, block_len)
            return part, dot(q, k_buf[part, :], 1, 1) * (scale * LOG2E) + bias[lines, part]

        def terms(part, prob):
            dprob = dot(g, v_buf[part, :], 1, 1)
            dscore = (prob * (dprob - delta) * scale).astype(jnp.bfloat16)
            return prob.astype(jnp.bfloat16), dscore, dot(dscore, k_buf[part, :], 1, 0)

        def pair_terms(part, prob_low, dscore):
            pair_acc[part, :dim] += dot(dscore, q, 0, 0)
            pair_acc[part, dim:] += dot(prob_low, g, 0, 0)

        def start_dq(dq):
            dq_buf[lines, lanes] = dq.astype(jnp.bfloat16)

            @pl.when(sec > 0)
            def _():
                send_dq(h, lines, slot).start()

        if blocks == 1:
            part, score = scores(0)
            top = jnp.max(score, axis=1, keepdims=True)
            prob = jnp.exp2(score - top)
            prob = prob * (1.0 / jnp.sum(prob, axis=1, keepdims=True))
            prob_low, dscore, dq = terms(part, prob)
            start_dq(dq)
            pair_terms(part, prob_low, dscore)
        else:
            stats[0, lines] = jnp.full((lines.size, 1), NEG, jnp.float32)
            stats[1, lines] = jnp.zeros((lines.size, 1), jnp.float32)
            dq_acc[lines] = jnp.zeros((lines.size, dim), jnp.float32)

            def gather_stats(b, _):
                _, score = scores(b)
                before = stats[0, lines]
                top = jnp.maximum(before, jnp.max(score, axis=1, keepdims=True))
                mass = jnp.sum(jnp.exp2(score - top), axis=1, keepdims=True)
                stats[1, lines] = stats[1, lines] * jnp.exp2(before - top) + mass
                stats[0, lines] = top
                return 0

            def gather_terms(b, _):
                part, score = scores(b)
                prob = jnp.exp2(score - stats[0, lines]) * (1.0 / stats[1, lines])
                prob_low, dscore, dq = terms(part, prob)
                dq_acc[lines] += dq
                pair_terms(part, prob_low, dscore)
                return 0

            lax.fori_loop(0, blocks, gather_stats, 0)
            lax.fori_loop(0, blocks, gather_terms, 0)
            start_dq(dq_acc[lines])

    pieces = [(h, pl.ds(0, rows), h) for h in range(heads)]
    for piece in pieces[:1]:
        rows_of_head(*piece)

    @pl.when(sec == sections - 1)
    def _():
        upstream[...] = jnp.zeros_like(upstream)

    for copy in later:
        copy.wait()

    def one_head(h, _):
        rows_of_head(h, pl.ds(0, rows), h)
        return 0

    lax.fori_loop(1, heads, one_head, 0)

    pair_sent = []
    for off in range(1, ranks):
        dst = lax.rem(me + off, ranks)
        pair_sent.append(
            pltpu.make_async_remote_copy(
                src_ref=pair_acc.at[pl.ds(off * rows, rows), :],
                dst_ref=pair_recv.at[off - 1],
                send_sem=pair_send.at[off - 1],
                recv_sem=pair_got.at[off - 1],
                device_id={"cp": dst},
                device_id_type=MESH,
            )
        )
    for copy in pair_sent:
        copy.start()
    for copy in sent:
        copy.wait_send()
    for copy in pair_sent:
        copy.wait_recv()
    total = pair_acc[mine, :]
    for off in range(1, ranks):
        total = total + pair_recv[off - 1]
    key_grad[...] = total[:, :dim].astype(jnp.bfloat16)
    value_grad[...] = total[:, dim:].astype(jnp.bfloat16)
    for copy in pair_sent:
        copy.wait_send()

    @pl.when(sec > 0)
    def _():
        for piece in pieces:
            send_dq(*piece).wait_send()

    @pl.when(sec < sections - 1)
    def _():
        for piece in pieces:
            send_dq(*piece).wait_recv()


def pair_kernel(
    sections, first, last, per,
    pairs_hbm, query, keys, values, attn_out, grad_out,
    key_grad, value_grad, upstream,
    q_buf, o_buf, g_buf, k_raw, v_raw, k_buf, v_buf, d_buf, y_got, s_buf, p_own, p_got, p_out,
    r_one, r_two, r_pack, key_low, key_wide, ds_buf, pr_buf, relay_buf, tally, bias, pair_acc, pair_out, pair_recv,
    pairs, in_sem, kv_got, low_got, dq_got, one_got, two_got, pack_got, give_got, swap_got, relay_got, gone,
    met, may_send,
):
    rows, width = q_buf.shape
    dim = k_buf.shape[1]
    heads = width // dim
    span = rows // 2
    seq = 2 * rows
    tile = span // 12
    bins = ((12, 4), (11, 5), (10, 6), (9, 7), (8, 3, 2, 1))
    packed = tile * len(bins)
    units = (last - first) // 2
    held, relayed = 3, 2
    groups = -(-units // per)
    scale = 1.0 / math.sqrt(dim)
    low, full = jnp.bfloat16, jnp.float32
    me = lax.axis_index("cp")
    sec = lax.axis_index("pp")
    peer = {"cp": 1 - me}
    below = {"pp": jnp.maximum(sec - 1, 0)}
    sends, gets = sec > 0, sec < sections - 1
    tp = lax.axis_index("tp")
    early = (sec == 0) & (tp == 0)
    relays = (sec == 0) & (tp == 1 + me)
    detours = (sec == 1) & (tp == 0)
    upper, lower, every = pl.ds(0, span), pl.ds(span, span), pl.ds(0, rows)

    def remote(src, dst, recv, device):
        return pltpu.make_async_remote_copy(
            src_ref=src, dst_ref=dst, send_sem=gone.at[0], recv_sem=recv, device_id=device, device_id_type=MESH
        )

    def take(ref, sem):
        pltpu.make_async_copy(ref, ref, sem).wait()

    own = [
        pltpu.make_async_copy(keys, k_raw.at[every, :], in_sem.at[0]),
        pltpu.make_async_copy(values, v_raw.at[every, :], in_sem.at[0]),
    ]
    head, rest = pl.ds(0, dim), pl.ds(dim, width - dim)
    wide = ((query, q_buf), (grad_out, g_buf), (attn_out, o_buf))
    begin = [pltpu.make_async_copy(src.at[:, head], dst.at[:, head], in_sem.at[1]) for src, dst in wide]
    later = [pltpu.make_async_copy(src.at[:, rest], dst.at[:, rest], in_sem.at[2]) for src, dst in wide]
    table = pltpu.make_async_copy(pairs_hbm, pairs, in_sem.at[3])
    other = pl.ds(rows, rows)

    barrier = pltpu.get_barrier_semaphore()

    @pl.when(me == 1)
    def _():
        pl.semaphore_signal(barrier, inc=1, device_id=peer, device_id_type=MESH)

    @pl.when(me == 0)
    def _():
        pl.semaphore_wait(barrier, 1)
        pl.semaphore_signal(met, inc=1, device_id=peer, device_id_type=MESH)
        for src, dst in ((keys, k_raw), (values, v_raw)):
            remote(src, dst.at[other, :], kv_got.at[0], peer).start()

    for copy in own + [table] + begin:
        copy.start()

    @pl.when(me == 1)
    def _():
        take(k_raw, in_sem.at[0])
        pl.semaphore_wait(met, 1)
        for buf in (k_raw, v_raw):
            remote(buf.at[every, :], buf.at[other, :], kv_got.at[0], peer).start()

        @pl.when(gets)
        def _():
            pl.semaphore_signal(barrier, inc=1, device_id={"pp": sec + 1}, device_id_type=MESH)

        @pl.when((sec == 0) & ((tp == 1) | (tp == 2)))
        def _():
            pl.semaphore_signal(barrier, inc=1, device_id={"tp": 0}, device_id_type=MESH)

    for copy in later:
        copy.start()

    table.wait()
    row = lax.broadcasted_iota(jnp.int32, (rows, seq), 0)
    col = lax.broadcasted_iota(jnp.int32, (rows, seq), 1)
    spans = [pairs[me, 0], pairs[me, 1], pairs[1 - me, 0], pairs[1 - me, 1]]
    q_pos = jnp.where(row < span, spans[0] * span, spans[1] * span - span) + row
    bias[...] = jnp.where(col <= q_pos, 0.0, NEG)
    pair_acc[...] = jnp.zeros_like(pair_acc)
    low_here = spans[0] == 0
    high_here = spans[1] == 0
    here = low_here | high_here

    def block_of(ref, n):
        return ref[n * span:(n + 1) * span, :]

    def of_span(ref, s):
        block = block_of(ref, 0)
        for n in range(1, 4):
            block = jnp.where(spans[n] == s, block_of(ref, n), block)
        return block

    def at_span(ref, s):
        block = block_of(ref, 0)
        for n in range(1, 4):
            block = jnp.where(s == n, block_of(ref, n), block)
        return block

    @pl.when(me == 0)
    def _():
        take(k_raw, in_sem.at[0])

    take(k_raw, kv_got.at[0])
    for s in range(4):
        k_buf[pl.ds(s * span, span), :] = of_span(k_raw, s)

    half = pl.ds(pl.multiple_of(me * (span // 2), span // 2), span // 2)
    rest_half = pl.ds(pl.multiple_of((1 - me) * (span // 2), span // 2), span // 2)
    send_low = remote(k_buf.at[half, :], key_low.at[half, :], low_got.at[0], below)
    pass_low = remote(key_low.at[half, :], key_low.at[half, :], low_got.at[1], peer)

    @pl.when(sends)
    def _():
        @pl.when(me == 1)
        def _():
            pl.semaphore_wait(barrier, 1)
            pl.semaphore_signal(may_send, inc=1, device_id=peer, device_id_type=MESH)

            @pl.when(detours)
            def _():
                pl.semaphore_signal(barrier, inc=1, device_id=below, device_id_type=MESH)

        @pl.when(me == 0)
        def _():
            pl.semaphore_wait(may_send, 1)

        send_low.start()

    for s in range(4):
        v_buf[pl.ds(s * span, span), :] = of_span(v_raw, s)
    take(q_buf.at[:, pl.ds(0, 3 * dim)], in_sem.at[1])

    def dot(a, b, da, db):
        return lax.dot_general(a, b, (((da,), (db,)), ((), ())), preferred_element_type=full)

    def lanes_of(h, count=1):
        return pl.ds(h * dim if isinstance(h, int) else pl.multiple_of(h * dim, dim), count * dim)

    def lines_of(n, size, count=1):
        return pl.ds(n * size if isinstance(n, int) else pl.multiple_of(n * size, size), count * size)

    def by_core(if_one, if_zero):
        pl.when(me == 1)(if_one)
        pl.when(me == 0)(if_zero)

    def send_dq(h, lines):
        return remote(
            d_buf.at[lines, lanes_of(h)], upstream.at[lines, lanes_of(h)], dq_got.at[0], below
        )

    def unit_lanes(i):
        return lanes_of(first + 2 * i, 2)

    def unit_lines(i):
        return lines_of(i, 2 * packed)

    def group_of(i):
        return i // per if isinstance(i, int) else lax.div(i, per)

    def units_of(g):
        return min(per, units - per * g) if isinstance(g, int) else per

    def heads_of(g):
        return range(first + 2 * per * g, first + 2 * (per * g + units_of(g)))

    def group_lanes(g):
        return lanes_of(first + 2 * per * g, 2 * units_of(g))

    def group_lines(g):
        return lines_of(per * g, 2 * packed, units_of(g))

    def send_one(i):
        at = unit_lanes(i)
        return remote(d_buf.at[upper, at], r_one.at[:, at], one_got.at[group_of(i)], below)

    def send_two(g):
        return remote(s_buf.at[:, group_lanes(g)], r_two.at[:, group_lanes(g)], two_got.at[g], below)

    def send_pack(g):
        return remote(p_out.at[group_lines(g), :], r_pack.at[group_lines(g), :], pack_got.at[g], below)

    def give_block(i):
        at = unit_lanes(i)
        return remote(d_buf.at[lower, at], y_got.at[:, at], give_got.at[group_of(i)], peer)

    def give_pack(i):
        at = unit_lines(i)
        return remote(p_own.at[at, :], p_got.at[at, :], give_got.at[group_of(i)], peer)

    def pass_two(g):
        return remote(r_two.at[:, group_lanes(g)], r_two.at[:, group_lanes(g)], two_got.at[g], peer)

    def pass_pack(g):
        return remote(r_pack.at[group_lines(g), :], r_pack.at[group_lines(g), :], pack_got.at[g], peer)

    def gradients(h, lines):
        lanes = lanes_of(h)
        q = q_buf[lines, lanes]
        g = g_buf[lines, lanes]
        delta = jnp.sum(g.astype(full) * o_buf[lines, lanes].astype(full), axis=1, keepdims=True)
        score = dot(q, k_buf[...], 1, 1) * (scale * LOG2E) + bias[lines, :]
        top = jnp.max(score, axis=1, keepdims=True)
        prob = jnp.exp2(score - top)
        prob = prob * (1.0 / jnp.sum(prob, axis=1, keepdims=True))
        dprob = dot(g, v_buf[...], 1, 1)
        dscore = (prob * (dprob - delta) * scale).astype(low)
        place = pl.ds(
            h * rows + lines.start if isinstance(h, int) else pl.multiple_of(h * rows + lines.start, span), lines.size
        )
        pr_buf[place, :] = prob.astype(low)
        ds_buf[place, :] = dscore
        return dscore, dot(dscore, k_buf[...], 1, 0)

    def pair_terms(h, _):
        place = lines_of(h, rows)
        pair_acc[:, :dim] += dot(ds_buf[place, :], q_buf[:, lanes_of(h)], 0, 0)
        pair_acc[:, dim:] += dot(pr_buf[place, :], g_buf[:, lanes_of(h)], 0, 0)
        return 0

    def plain_pieces(pieces, before=None):
        for h, lines in pieces:
            d_buf[lines, lanes_of(h)] = gradients(h, lines)[1].astype(low)

        @pl.when(sends)
        def _():
            if before is not None:
                before()
            for piece in pieces:
                send_dq(*piece).start()

    near, far = lanes_of(first + 2 * relayed), lanes_of(first + 2 * relayed + 1)
    at_last = one_got.at[group_of(relayed)]
    half_unit = remote(d_buf.at[upper, near], r_one.at[:, near], at_last, below)
    detour = remote(d_buf.at[upper, far], relay_buf, relay_got.at[0], {"pp": 0, "tp": 1 + me})
    relay = remote(relay_buf, r_one.at[:, far], at_last, {"tp": 0})

    def pack_head(h):
        lanes = lanes_of(h)
        dscore, dq = gradients(h, every)
        d_buf[upper, lanes] = jnp.where(low_here, dq[span:], dq[:span]).astype(low)
        d_buf[lower, lanes] = dq[span:].astype(low)
        block = jnp.where(high_here, dscore[span:, :dim].astype(full), dscore[:span, :dim].astype(full))
        lines = []
        for group in bins:
            line, at = 0.0, 0
            for n in group:
                entry = block[(n - 1) * tile:n * tile]
                line = line + (pltpu.roll(entry, at, 1) if at else entry)
                at += n * tile
            lines.append(line)
        return lines

    def unpack_head(lines):
        lane = lax.broadcasted_iota(jnp.int32, (tile, dim), 1)
        entries = {}
        for b, group in enumerate(bins):
            line, at = lines[b * tile:(b + 1) * tile], 0
            for n in group:
                entry = pltpu.roll(line, dim - at, 1) if at else line
                entries[n] = jnp.where(lane < n * tile, entry, 0.0)
                at += n * tile
        return [entries[n] for n in range(1, 13)]

    def gives(i):
        by_core(lambda: give_pack(i).start(), lambda: give_block(i).start())

    def second_sends(g):
        def two():
            at = group_lanes(g)
            take(y_got.at[:, at], give_got.at[g])
            s_buf[:, at] = jnp.where(here, y_got[:, at], d_buf[lower, at])
            send_two(g).start()

        def one():
            at = group_lines(g)
            take(p_got.at[at, :], give_got.at[g])
            p_out[at, :] = jnp.where(here, p_own[at, :], p_got[at, :])
            send_pack(g).start()

        by_core(two, one)

    def packed_unit(i, _):
        lines = pack_head(first + 2 * i) + pack_head(first + 2 * i + 1)
        p_own[unit_lines(i), :] = jnp.concatenate(lines, axis=0).astype(low)

        @pl.when(sends)
        def _():
            gives(i)

            @pl.when((i < units - held) & jnp.logical_not(detours & (i == relayed)))
            def _():
                send_one(i).start()

            @pl.when(detours & (i == relayed))
            def _():
                half_unit.start()
                pl.semaphore_wait(met, 1)
                detour.start()

            @pl.when((i > 0) & (lax.rem(i, per) == 0))
            def _():
                second_sends(group_of(i) - 1)

        return 0

    plain_pieces([(0, every)])

    @pl.when(early & (me == 1))
    def _():
        pl.semaphore_wait(barrier, 3)
        for core in range(2):
            for to in ({"tp": 1 + core, "cp": core}, {"pp": 1, "cp": core}):
                pl.semaphore_signal(met, inc=1, device_id=to, device_id_type=MESH)

    take(tally.at[pl.ds(0, 3 * rows * (heads - 1)), :], in_sem.at[2])
    lax.fori_loop(0, units, packed_unit, 0)

    def waiting():
        second_sends(groups - 1)
        for i in range(units - held, units):
            send_one(i).start()

    plain_pieces([(h, every) for h in range(last, heads)], waiting)

    @pl.when(relays)
    def _():
        take(relay_buf, relay_got.at[0])
        pl.semaphore_wait(met, 1)
        relay.start()

    lax.fori_loop(0, heads, pair_terms, 0, unroll=2)

    for n in range(2):
        pair_out[lines_of(n, span), :] = at_span(pair_acc, spans[2 + n])
    swap = remote(pair_out, pair_recv, swap_got.at[0], peer)
    swap.start()

    def pass_on(g):
        def two():
            take(r_two.at[:, group_lanes(g)], two_got.at[g])
            pass_two(g).start()

        def one():
            take(r_pack.at[group_lines(g), :], pack_got.at[g])
            pass_pack(g).start()

        by_core(two, one)

    def assemble(g):
        by_core(
            lambda: take(r_pack.at[group_lines(g), :], pack_got.at[g]),
            lambda: take(r_two.at[:, group_lanes(g)], two_got.at[g]),
        )
        take(r_one.at[:, group_lanes(g)], one_got.at[g])
        for h in heads_of(g)[::2]:
            lines = r_pack[pl.ds((h - first) * packed, 2 * packed), :].astype(full)
            block = unpack_head(lines[:packed]) + unpack_head(lines[packed:])
            both = dot(jnp.concatenate(block, axis=0).astype(low), key_wide[...], 1, 0).astype(low)
            for n in range(2):
                lanes = lanes_of(h + n)
                opened = both[n * span:(n + 1) * span]
                one = r_one[:, lanes]
                upstream[upper, lanes] = jnp.where(low_here, opened, one)
                upstream[lower, lanes] = jnp.where(low_here, one, jnp.where(high_here, opened, r_two[:, lanes]))

    @pl.when(gets)
    def _():
        send_low.wait_recv()
        pass_low.start()
        pass_on(0)

    swap.wait_recv()
    for n in range(2):
        lines = lines_of(n, span)
        total = at_span(pair_acc, spans[n]) + pair_recv[lines, :]
        key_grad[lines, :] = total[:, :dim].astype(low)
        value_grad[lines, :] = total[:, dim:].astype(low)

    plain = heads - (last - first)

    @pl.when(gets)
    def _():
        take(key_low.at[rest_half, :], low_got.at[1])
        key_wide[span:, :] = jnp.zeros((dim - span, dim), low)
        key_wide[:span, :] = key_low[...]
        for g in range(1, groups):
            pass_on(g)
            assemble(g - 1)
        assemble(groups - 1)

    @pl.when(jnp.logical_not(gets))
    def _():
        upstream[...] = jnp.zeros_like(upstream)

    @pl.when(gets)
    def _():
        take(upstream.at[:, lanes_of(0, plain)], dq_got.at[0])

    def drain(core, sending, getting, relaying):
        two, pack = 2 * units * span, 2 * units * packed
        lines = 2 * rows + 4 * rows + (span if relaying else 0)
        if sending:
            lines += span // 2 + plain * rows + 2 * units * span + two + pack
        if getting:
            lines += span // 2 + (two if core else pack)
        take(tally.at[pl.ds(0, lines), :], gone.at[0])

    for core in range(2):
        mine = me == core
        pl.when(mine & sends & gets)(functools.partial(drain, core, True, True, False))
        pl.when(mine & jnp.logical_not(gets))(functools.partial(drain, core, True, False, False))
        pl.when(mine & relays)(functools.partial(drain, core, False, True, True))
        pl.when(mine & jnp.logical_not(sends | relays))(functools.partial(drain, core, False, True, False))


def store(key_grad, value_grad, upstream, key_out, value_out, upstream_out, sem):
    copies = [
        pltpu.make_async_copy(src, dst, sem.at[i])
        for i, (src, dst) in enumerate(
            ((upstream, upstream_out), (key_grad, key_out), (value_grad, value_out))
        )
    ]
    for copy in copies:
        copy.start()
    for copy in copies:
        copy.wait()


def body(query, keys, values, attn_out, grad_out, span_pairs):
    _, rows, width = query.shape
    dim = keys.shape[2]
    heads = width // dim
    ranks = lax.axis_size("cp")
    sections = lax.axis_size("pp")
    seq = ranks * rows
    low, full = jnp.bfloat16, jnp.float32
    dma = pltpu.SemaphoreType.DMA
    vmem = pl.BlockSpec(memory_space=pltpu.VMEM)
    hbm = pl.BlockSpec(memory_space=pltpu.HBM)

    def spaces(*shapes):
        return [pltpu.VMEM(shape, low) for shape in shapes]

    tall, flat, block = (rows, width), (seq, dim), (rows // 2, width)
    if ranks == 2 and lax.axis_size("tp") > 2 and sections > 1 and dim == 128 and rows == 192 and heads == 16:
        groups, packs = 3, ((heads - 2) * (5 * rows // 24), dim)
        run = functools.partial(pair_kernel, sections, 1, heads - 1, groups)
        scratch = (
            spaces(tall, tall, tall, flat, flat, flat, flat, tall, block, block, packs, packs, packs)
            + spaces(block, block, packs, (rows // 2, dim), (dim, dim))
            + spaces((heads * rows, seq), (heads * rows, seq), (rows // 2, dim), (3 * heads * rows, dim))
            + [
                pltpu.VMEM((rows, seq), full),
                pltpu.VMEM((seq, 2 * dim), full),
                pltpu.VMEM((rows, 2 * dim), full),
                pltpu.VMEM((rows, 2 * dim), full),
                pltpu.SMEM((ranks, 2), jnp.int32),
            ]
            + [dma((n,)) for n in (4, 1, 2, 1, groups, groups, groups, groups, 1, 1, 1)]
            + [pltpu.SemaphoreType.REGULAR] * 2
        )
    else:
        others = max(ranks - 1, 1)
        run = functools.partial(kernel, ranks, sections, 2 * rows if ranks % 2 == 0 else rows)
        scratch = (
            spaces(tall, tall, tall, flat, flat, tall)
            + [
                pltpu.VMEM((rows, seq), full),
                pltpu.VMEM((2, rows, 1), full),
                pltpu.VMEM((rows, dim), full),
                pltpu.VMEM((seq, 2 * dim), full),
                pltpu.VMEM((others, rows, 2 * dim), full),
                pltpu.SMEM((ranks, 2), jnp.int32),
            ]
            + [dma((9,)), dma((2, others)), dma((2, others)), dma((heads + 1,)), dma((heads + 1,))]
            + [dma((others,)), dma((others,))]
        )
    key_grad, value_grad, upstream = pl.pallas_call(
        run,
        out_shape=(
            pltpu.VMEM((rows, dim), low),
            pltpu.VMEM((rows, dim), low),
            pltpu.VMEM((rows, width), low),
        ),
        in_specs=[hbm] * 6,
        out_specs=(vmem, vmem, vmem),
        scratch_shapes=scratch,
        compiler_params=pltpu.CompilerParams(
            collective_id=0, has_side_effects=True, vmem_limit_bytes=64 * 1024 * 1024 - 1200 * 1024
        ),
        name="backward",
    )(span_pairs, query[0], keys[0], values[0], attn_out[0], grad_out[0])
    anywhere = pl.BlockSpec(memory_space=pl.ANY)
    key_grad, value_grad, upstream = pl.pallas_call(
        store,
        out_shape=(
            jax.ShapeDtypeStruct((rows, dim), low),
            jax.ShapeDtypeStruct((rows, dim), low),
            jax.ShapeDtypeStruct((rows, width), low),
        ),
        in_specs=[anywhere] * 3,
        out_specs=(anywhere,) * 3,
        scratch_shapes=[dma((3,))],
        compiler_params=pltpu.CompilerParams(vmem_limit_bytes=1024 * 1024),
        name="store",
    )(key_grad, value_grad, upstream)
    return key_grad[None], value_grad[None], upstream[None]


def solution(mesh):
    spec = P("pp", "cp", "tp")
    return jax.shard_map(
        body,
        mesh=mesh,
        in_specs=(spec, spec, spec, spec, spec, P()),
        out_specs=(spec, spec, spec),
        check_vma=False,
    )
```

```python
import functools
import math

import jax
import jax.numpy as jnp
from jax import lax
from jax.experimental import pallas as pl
from jax.experimental.pallas import tpu as pltpu
from jax.sharding import PartitionSpec as P

MESH = pl.DeviceIdType.MESH
NEG = -1e30
LOG2E = math.log2(math.e)


def kernel(
    ranks, sections, block_len,
    pairs_hbm, query, keys, values, attn_out, grad_out,
    key_grad, value_grad, upstream,
    q_buf, o_buf, g_buf, k_buf, v_buf, dq_buf, bias, stats, dq_acc, pair_acc, pair_recv,
    pairs, in_sem, kv_send, kv_recv, dq_send, dq_recv, pair_send, pair_got,
):
    rows, width = q_buf.shape
    dim = k_buf.shape[1]
    heads = width // dim
    span = rows // 2
    seq = ranks * rows
    blocks = seq // block_len
    scale = 1.0 / math.sqrt(dim)
    me = lax.axis_index("cp")
    sec = lax.axis_index("pp")
    mine = pl.ds(0, rows)

    barrier = pltpu.get_barrier_semaphore()
    for off in range(1, ranks):
        pl.semaphore_signal(
            barrier, inc=1, device_id={"cp": lax.rem(me + off, ranks)}, device_id_type=MESH
        )

    @pl.when(sec < sections - 1)
    def _():
        pl.semaphore_signal(barrier, inc=1, device_id={"pp": sec + 1}, device_id_type=MESH)

    own = [
        pltpu.make_async_copy(keys, k_buf.at[mine, :], in_sem.at[0]),
        pltpu.make_async_copy(values, v_buf.at[mine, :], in_sem.at[1]),
    ]
    first, rest = pl.ds(0, dim), pl.ds(dim, width - dim)
    wide = ((query, q_buf), (grad_out, g_buf), (attn_out, o_buf))
    begin = [
        pltpu.make_async_copy(src.at[:, first], dst.at[:, first], in_sem.at[2 + i])
        for i, (src, dst) in enumerate(wide)
    ]
    later = [
        pltpu.make_async_copy(src.at[:, rest], dst.at[:, rest], in_sem.at[5 + i])
        for i, (src, dst) in enumerate(wide)
    ]
    table = pltpu.make_async_copy(pairs_hbm, pairs, in_sem.at[8])
    for copy in [table] + own + begin:
        copy.start()

    pl.semaphore_wait(barrier, ranks - 1 + (sec > 0).astype(jnp.int32))
    sent = []
    for off in range(1, ranks):
        for which, (src, buf) in enumerate(((keys, k_buf), (values, v_buf))):
            sent.append(
                pltpu.make_async_remote_copy(
                    src_ref=src,
                    dst_ref=buf.at[pl.ds((ranks - off) * rows, rows), :],
                    send_sem=kv_send.at[which, off - 1],
                    recv_sem=kv_recv.at[which, off - 1],
                    device_id={"cp": lax.rem(me + off, ranks)},
                    device_id_type=MESH,
                )
            )
    for copy in sent + later:
        copy.start()

    table.wait()
    row = lax.broadcasted_iota(jnp.int32, (rows, rows), 0)
    col = lax.broadcasted_iota(jnp.int32, (rows, rows), 1)
    q_pos = jnp.where(row < span, pairs[me, 0] * span, pairs[me, 1] * span - span) + row
    for r in range(ranks):
        rank = lax.rem(me + r, ranks)
        k_pos = jnp.where(col < span, pairs[rank, 0] * span, pairs[rank, 1] * span - span) + col
        bias[:, r * rows:(r + 1) * rows] = jnp.where(k_pos <= q_pos, 0.0, NEG)
    pair_acc[...] = jnp.zeros_like(pair_acc)

    for copy in own + begin:
        copy.wait()
    for copy in sent:
        copy.wait_recv()

    def dot(a, b, da, db):
        return lax.dot_general(a, b, (((da,), (db,)), ((), ())), preferred_element_type=jnp.float32)

    def lanes_of(h):
        return pl.ds(h * dim if isinstance(h, int) else pl.multiple_of(h * dim, dim), dim)

    def send_dq(h, lines, slot):
        return pltpu.make_async_remote_copy(
            src_ref=dq_buf.at[lines, lanes_of(h)],
            dst_ref=upstream.at[lines, lanes_of(h)],
            send_sem=dq_send.at[slot],
            recv_sem=dq_recv.at[slot],
            device_id={"pp": jnp.maximum(sec - 1, 0)},
            device_id_type=MESH,
        )

    def rows_of_head(h, lines, slot):
        lanes = lanes_of(h)
        q = q_buf[lines, lanes]
        g = g_buf[lines, lanes]
        delta = jnp.sum(
            g.astype(jnp.float32) * o_buf[lines, lanes].astype(jnp.float32), axis=1, keepdims=True
        )

        def scores(b):
            at = b * block_len if isinstance(b, int) else pl.multiple_of(b * block_len, block_len)
            part = pl.ds(at, block_len)
            return part, dot(q, k_buf[part, :], 1, 1) * (scale * LOG2E) + bias[lines, part]

        def terms(part, prob):
            dprob = dot(g, v_buf[part, :], 1, 1)
            dscore = (prob * (dprob - delta) * scale).astype(jnp.bfloat16)
            return prob.astype(jnp.bfloat16), dscore, dot(dscore, k_buf[part, :], 1, 0)

        def pair_terms(part, prob_low, dscore):
            pair_acc[part, :dim] += dot(dscore, q, 0, 0)
            pair_acc[part, dim:] += dot(prob_low, g, 0, 0)

        def start_dq(dq):
            dq_buf[lines, lanes] = dq.astype(jnp.bfloat16)

            @pl.when(sec > 0)
            def _():
                send_dq(h, lines, slot).start()

        if blocks == 1:
            part, score = scores(0)
            top = jnp.max(score, axis=1, keepdims=True)
            prob = jnp.exp2(score - top)
            prob = prob * (1.0 / jnp.sum(prob, axis=1, keepdims=True))
            prob_low, dscore, dq = terms(part, prob)
            start_dq(dq)
            pair_terms(part, prob_low, dscore)
        else:
            stats[0, lines] = jnp.full((lines.size, 1), NEG, jnp.float32)
            stats[1, lines] = jnp.zeros((lines.size, 1), jnp.float32)
            dq_acc[lines] = jnp.zeros((lines.size, dim), jnp.float32)

            def gather_stats(b, _):
                _, score = scores(b)
                before = stats[0, lines]
                top = jnp.maximum(before, jnp.max(score, axis=1, keepdims=True))
                mass = jnp.sum(jnp.exp2(score - top), axis=1, keepdims=True)
                stats[1, lines] = stats[1, lines] * jnp.exp2(before - top) + mass
                stats[0, lines] = top
                return 0

            def gather_terms(b, _):
                part, score = scores(b)
                prob = jnp.exp2(score - stats[0, lines]) * (1.0 / stats[1, lines])
                prob_low, dscore, dq = terms(part, prob)
                dq_acc[lines] += dq
                pair_terms(part, prob_low, dscore)
                return 0

            lax.fori_loop(0, blocks, gather_stats, 0)
            lax.fori_loop(0, blocks, gather_terms, 0)
            start_dq(dq_acc[lines])

    pieces = [(h, pl.ds(0, rows), h) for h in range(heads)]
    for piece in pieces[:1]:
        rows_of_head(*piece)

    @pl.when(sec == sections - 1)
    def _():
        upstream[...] = jnp.zeros_like(upstream)

    for copy in later:
        copy.wait()

    def one_head(h, _):
        rows_of_head(h, pl.ds(0, rows), h)
        return 0

    lax.fori_loop(1, heads, one_head, 0)

    pair_sent = []
    for off in range(1, ranks):
        dst = lax.rem(me + off, ranks)
        pair_sent.append(
            pltpu.make_async_remote_copy(
                src_ref=pair_acc.at[pl.ds(off * rows, rows), :],
                dst_ref=pair_recv.at[off - 1],
                send_sem=pair_send.at[off - 1],
                recv_sem=pair_got.at[off - 1],
                device_id={"cp": dst},
                device_id_type=MESH,
            )
        )
    for copy in pair_sent:
        copy.start()
    for copy in sent:
        copy.wait_send()
    for copy in pair_sent:
        copy.wait_recv()
    total = pair_acc[mine, :]
    for off in range(1, ranks):
        total = total + pair_recv[off - 1]
    key_grad[...] = total[:, :dim].astype(jnp.bfloat16)
    value_grad[...] = total[:, dim:].astype(jnp.bfloat16)
    for copy in pair_sent:
        copy.wait_send()

    @pl.when(sec > 0)
    def _():
        for piece in pieces:
            send_dq(*piece).wait_send()

    @pl.when(sec < sections - 1)
    def _():
        for piece in pieces:
            send_dq(*piece).wait_recv()


def pair_kernel(
    sections, first, last, per,
    pairs_hbm, query, keys, values, attn_out, grad_out,
    key_grad, value_grad, upstream,
    q_buf, o_buf, g_buf, k_raw, v_raw, k_buf, v_buf, d_buf, y_got, s_buf, p_own, p_got, p_out,
    r_one, r_two, r_pack, r_open, key_low, key_wide, ds_buf, pr_buf, relay_buf, tally, bias, pair_acc, pair_out, pair_recv,
    pairs, in_sem, kv_got, low_got, dq_got, one_got, two_got, pack_got, give_got, swap_got, relay_got, gone,
    met, may_send,
):
    rows, width = q_buf.shape
    dim = k_buf.shape[1]
    heads = width // dim
    span = rows // 2
    seq = 2 * rows
    tile = span // 12
    bins = ((12, 4), (11, 5), (10, 6), (9, 7), (8, 3, 2, 1))
    packed = tile * len(bins)
    single = packed + tile
    units = (last - first) // 2
    held, relayed = 3, 2
    groups = -(-units // per)
    scale = 1.0 / math.sqrt(dim)
    low, full = jnp.bfloat16, jnp.float32
    me = lax.axis_index("cp")
    sec = lax.axis_index("pp")
    peer = {"cp": 1 - me}
    below = {"pp": jnp.maximum(sec - 1, 0)}
    sends, gets = sec > 0, sec < sections - 1
    tp = lax.axis_index("tp")
    early = (sec == 0) & (tp == 0)
    relays = (sec == 0) & (tp == 1 + me)
    detours = (sec == 1) & (tp == 0)
    upper, lower, every = pl.ds(0, span), pl.ds(span, span), pl.ds(0, rows)

    def remote(src, dst, recv, device):
        return pltpu.make_async_remote_copy(
            src_ref=src, dst_ref=dst, send_sem=gone.at[0], recv_sem=recv, device_id=device, device_id_type=MESH
        )

    def take(ref, sem):
        pltpu.make_async_copy(ref, ref, sem).wait()

    own = [
        pltpu.make_async_copy(keys, k_raw.at[every, :], in_sem.at[0]),
        pltpu.make_async_copy(values, v_raw.at[every, :], in_sem.at[0]),
    ]
    head, rest = pl.ds(0, dim), pl.ds(dim, width - dim)
    wide = ((query, q_buf), (grad_out, g_buf), (attn_out, o_buf))
    begin = [pltpu.make_async_copy(src.at[:, head], dst.at[:, head], in_sem.at[1]) for src, dst in wide]
    later = [pltpu.make_async_copy(src.at[:, rest], dst.at[:, rest], in_sem.at[2]) for src, dst in wide]
    table = pltpu.make_async_copy(pairs_hbm, pairs, in_sem.at[3])
    other = pl.ds(rows, rows)

    barrier = pltpu.get_barrier_semaphore()

    @pl.when(me == 1)
    def _():
        pl.semaphore_signal(barrier, inc=1, device_id=peer, device_id_type=MESH)

    @pl.when(me == 0)
    def _():
        pl.semaphore_wait(barrier, 1)
        pl.semaphore_signal(met, inc=1, device_id=peer, device_id_type=MESH)
        for src, dst in ((keys, k_raw), (values, v_raw)):
            remote(src, dst.at[other, :], kv_got.at[0], peer).start()

    for copy in own + [table] + begin:
        copy.start()

    @pl.when(me == 1)
    def _():
        take(k_raw, in_sem.at[0])
        pl.semaphore_wait(met, 1)
        for buf in (k_raw, v_raw):
            remote(buf.at[every, :], buf.at[other, :], kv_got.at[0], peer).start()

        @pl.when(gets)
        def _():
            pl.semaphore_signal(barrier, inc=1, device_id={"pp": sec + 1}, device_id_type=MESH)

        @pl.when((sec == 0) & ((tp == 1) | (tp == 2)))
        def _():
            pl.semaphore_signal(barrier, inc=1, device_id={"tp": 0}, device_id_type=MESH)

    for copy in later:
        copy.start()

    table.wait()
    row = lax.broadcasted_iota(jnp.int32, (rows, seq), 0)
    col = lax.broadcasted_iota(jnp.int32, (rows, seq), 1)
    spans = [pairs[me, 0], pairs[me, 1], pairs[1 - me, 0], pairs[1 - me, 1]]
    q_pos = jnp.where(row < span, spans[0] * span, spans[1] * span - span) + row
    bias[...] = jnp.where(col <= q_pos, 0.0, NEG)
    pair_acc[...] = jnp.zeros_like(pair_acc)
    low_here = spans[0] == 0
    high_here = spans[1] == 0
    here = low_here | high_here

    def block_of(ref, n):
        return ref[n * span:(n + 1) * span, :]

    def of_span(ref, s):
        block = block_of(ref, 0)
        for n in range(1, 4):
            block = jnp.where(spans[n] == s, block_of(ref, n), block)
        return block

    def at_span(ref, s):
        block = block_of(ref, 0)
        for n in range(1, 4):
            block = jnp.where(s == n, block_of(ref, n), block)
        return block

    @pl.when(me == 0)
    def _():
        take(k_raw, in_sem.at[0])

    take(k_raw, kv_got.at[0])
    for s in range(4):
        k_buf[pl.ds(s * span, span), :] = of_span(k_raw, s)

    half = pl.ds(pl.multiple_of(me * (span // 2), span // 2), span // 2)
    rest_half = pl.ds(pl.multiple_of((1 - me) * (span // 2), span // 2), span // 2)
    send_low = remote(k_buf.at[half, :], key_low.at[half, :], low_got.at[0], below)
    pass_low = remote(key_low.at[half, :], key_low.at[half, :], low_got.at[1], peer)

    @pl.when(sends)
    def _():
        @pl.when(me == 1)
        def _():
            pl.semaphore_wait(barrier, 1)
            pl.semaphore_signal(may_send, inc=1, device_id=peer, device_id_type=MESH)

            @pl.when(detours)
            def _():
                pl.semaphore_signal(barrier, inc=1, device_id=below, device_id_type=MESH)

        @pl.when(me == 0)
        def _():
            pl.semaphore_wait(may_send, 1)

        send_low.start()

    for s in range(4):
        v_buf[pl.ds(s * span, span), :] = of_span(v_raw, s)
    take(q_buf.at[:, pl.ds(0, 3 * dim)], in_sem.at[1])

    def dot(a, b, da, db):
        return lax.dot_general(a, b, (((da,), (db,)), ((), ())), preferred_element_type=full)

    def lanes_of(h, count=1):
        return pl.ds(h * dim if isinstance(h, int) else pl.multiple_of(h * dim, dim), count * dim)

    def lines_of(n, size, count=1):
        return pl.ds(n * size if isinstance(n, int) else pl.multiple_of(n * size, size), count * size)

    def by_core(if_one, if_zero):
        pl.when(me == 1)(if_one)
        pl.when(me == 0)(if_zero)

    def send_dq(h, lines):
        return remote(
            d_buf.at[lines, lanes_of(h)], upstream.at[lines, lanes_of(h)], dq_got.at[0], below
        )

    def unit_lanes(i):
        return lanes_of(first + 2 * i, 2)

    def unit_lines(i):
        return lines_of(i, 2 * packed)

    def group_of(i):
        return i // per if isinstance(i, int) else lax.div(i, per)

    def units_of(g):
        return min(per, units - per * g) if isinstance(g, int) else per

    def extra(g):
        return 1 if isinstance(g, int) and g == groups - 1 else 0

    def heads_of(g):
        return range(first + 2 * per * g, first + 2 * (per * g + units_of(g)))

    def group_lanes(g):
        return lanes_of(first + 2 * per * g, 2 * units_of(g) + extra(g))

    def group_lines(g):
        if extra(g):
            return pl.ds(2 * per * g * packed, 2 * units_of(g) * packed + single)
        return lines_of(per * g, 2 * packed, units_of(g))

    def send_one(i):
        at = unit_lanes(i)
        return remote(d_buf.at[upper, at], r_one.at[:, at], one_got.at[group_of(i)], below)

    alone = pl.ds(2 * units * packed, single)
    last_lanes = lanes_of(last)
    send_last = remote(d_buf.at[upper, last_lanes], r_one.at[:, last_lanes], one_got.at[groups - 1], below)
    give_last_block = remote(d_buf.at[lower, last_lanes], y_got.at[:, last_lanes], give_got.at[groups - 1], peer)
    give_last_pack = remote(p_own.at[alone, :], p_got.at[alone, :], give_got.at[groups - 1], peer)

    def send_two(g):
        return remote(s_buf.at[:, group_lanes(g)], r_two.at[:, group_lanes(g)], two_got.at[g], below)

    def send_pack(g):
        return remote(p_out.at[group_lines(g), :], r_pack.at[group_lines(g), :], pack_got.at[g], below)

    def give_block(i):
        at = unit_lanes(i)
        return remote(d_buf.at[lower, at], y_got.at[:, at], give_got.at[group_of(i)], peer)

    def give_pack(i):
        at = unit_lines(i)
        return remote(p_own.at[at, :], p_got.at[at, :], give_got.at[group_of(i)], peer)

    def pass_two(g):
        return remote(r_two.at[:, group_lanes(g)], r_two.at[:, group_lanes(g)], two_got.at[g], peer)

    def pass_pack(g):
        return remote(r_pack.at[group_lines(g), :], r_pack.at[group_lines(g), :], pack_got.at[g], peer)

    def gradients(h, lines, plain=False):
        lanes = lanes_of(h)
        q = q_buf[lines, lanes]
        g = g_buf[lines, lanes]
        delta = jnp.sum(g.astype(full) * o_buf[lines, lanes].astype(full), axis=1, keepdims=True)
        score = dot(q, k_buf[...], 1, 1) * (scale * LOG2E) + bias[lines, :]
        top = jnp.max(score, axis=1, keepdims=True)
        power = jnp.exp2(score - top)
        dprob = (dot(g, v_buf[...], 1, 1) - delta) * scale
        inverse = 1.0 / jnp.sum(power, axis=1, keepdims=True)
        prob = power * inverse
        dscore = (prob * dprob).astype(low)
        place = pl.ds(
            h * rows + lines.start if isinstance(h, int) else pl.multiple_of(h * rows + lines.start, span), lines.size
        )
        pr_buf[place, :] = prob.astype(low)
        ds_buf[place, :] = dscore
        if plain:
            return dscore, dot((power * dprob).astype(low), k_buf[...], 1, 0) * inverse
        return dscore, dot(dscore, k_buf[...], 1, 0)

    def pair_terms(h, _):
        place = lines_of(h, rows)
        pair_acc[:, :dim] += dot(ds_buf[place, :], q_buf[:, lanes_of(h)], 0, 0)
        pair_acc[:, dim:] += dot(pr_buf[place, :], g_buf[:, lanes_of(h)], 0, 0)
        return 0

    def plain_pieces(pieces, before=None):
        for h, lines in pieces:
            d_buf[lines, lanes_of(h)] = gradients(h, lines, h == 0)[1].astype(low)

        @pl.when(sends)
        def _():
            if before is not None:
                before()
            for piece in pieces:
                send_dq(*piece).start()

    near, far = lanes_of(first + 2 * relayed), lanes_of(first + 2 * relayed + 1)
    at_last = one_got.at[group_of(relayed)]
    half_unit = remote(d_buf.at[upper, near], r_one.at[:, near], at_last, below)
    detour = remote(d_buf.at[upper, far], relay_buf, relay_got.at[0], {"pp": 0, "tp": 1 + me})
    relay = remote(relay_buf, r_one.at[:, far], at_last, {"tp": 0})

    def pack_head(h):
        lanes = lanes_of(h)
        dscore, dq = gradients(h, every)
        d_buf[upper, lanes] = jnp.where(low_here, dq[span:], dq[:span]).astype(low)
        d_buf[lower, lanes] = dq[span:].astype(low)
        block = jnp.where(high_here, dscore[span:, :dim].astype(full), dscore[:span, :dim].astype(full))
        lines = []
        for group in bins:
            line, at = 0.0, 0
            for n in group:
                entry = block[(n - 1) * tile:n * tile]
                line = line + (pltpu.roll(entry, at, 1) if at else entry)
                at += n * tile
            lines.append(line)
        return lines

    def unpack_head(lines):
        lane = lax.broadcasted_iota(jnp.int32, (tile, dim), 1)
        entries = {}
        for b, group in enumerate(bins):
            line, at = lines[b * tile:(b + 1) * tile], 0
            for n in group:
                entry = pltpu.roll(line, dim - at, 1) if at else line
                entries[n] = jnp.where(lane < n * tile, entry, 0.0)
                at += n * tile
        return [entries[n] for n in range(1, 13)]

    def gives(i):
        by_core(lambda: give_pack(i).start(), lambda: give_block(i).start())

    def second_sends(g):
        def two():
            at = group_lanes(g)
            take(y_got.at[:, at], give_got.at[g])
            s_buf[:, at] = jnp.where(here, y_got[:, at], d_buf[lower, at])
            send_two(g).start()

        def one():
            at = group_lines(g)
            take(p_got.at[at, :], give_got.at[g])
            p_out[at, :] = jnp.where(here, p_own[at, :], p_got[at, :])
            send_pack(g).start()

        by_core(two, one)

    def packed_unit(i, _):
        lines = pack_head(first + 2 * i) + pack_head(first + 2 * i + 1)
        p_own[unit_lines(i), :] = jnp.concatenate(lines, axis=0).astype(low)

        @pl.when(sends)
        def _():
            gives(i)

            @pl.when((i < units - held) & jnp.logical_not(detours & (i == relayed)))
            def _():
                send_one(i).start()

            @pl.when(detours & (i == relayed))
            def _():
                half_unit.start()
                pl.semaphore_wait(met, 1)
                detour.start()

            @pl.when((i > 0) & (lax.rem(i, per) == 0))
            def _():
                second_sends(group_of(i) - 1)

        return 0

    plain_pieces([(0, every)])

    @pl.when(early & (me == 1))
    def _():
        pl.semaphore_wait(barrier, 3)
        for core in range(2):
            for to in ({"tp": 1 + core, "cp": core}, {"pp": 1, "cp": core}):
                pl.semaphore_signal(met, inc=1, device_id=to, device_id_type=MESH)

    take(tally.at[pl.ds(0, 3 * rows * (heads - 1)), :], in_sem.at[2])
    lax.fori_loop(0, units, packed_unit, 0)

    lines = pack_head(last)
    p_own[alone, :] = jnp.concatenate(lines + [jnp.zeros((tile, dim), full)], axis=0).astype(low)

    @pl.when(sends)
    def _():
        by_core(give_last_pack.start, give_last_block.start)

    @pl.when(relays)
    def _():
        take(relay_buf, relay_got.at[0])
        pl.semaphore_wait(met, 1)
        relay.start()

    lax.fori_loop(0, 4, pair_terms, 0, unroll=2)

    @pl.when(sends)
    def _():
        second_sends(groups - 1)
        for i in range(units - held, units):
            send_one(i).start()
        send_last.start()

    lax.fori_loop(4, heads, pair_terms, 0, unroll=2)

    for n in range(2):
        pair_out[lines_of(n, span), :] = at_span(pair_acc, spans[2 + n])
    swap = remote(pair_out, pair_recv, swap_got.at[0], peer)
    swap.start()

    def pass_on(g):
        def two():
            take(r_two.at[:, group_lanes(g)], two_got.at[g])
            pass_two(g).start()

        def one():
            take(r_pack.at[group_lines(g), :], pack_got.at[g])
            pass_pack(g).start()

        by_core(two, one)

    def assemble(g):
        by_core(
            lambda: take(r_pack.at[group_lines(g), :], pack_got.at[g]),
            lambda: take(r_two.at[:, group_lanes(g)], two_got.at[g]),
        )
        def open_heads(h, count, size):
            lines = r_pack[pl.ds((h - first) * packed, size), :].astype(full)
            block = []
            for n in range(count):
                block += unpack_head(lines[n * packed:(n + 1) * packed])
            both = dot(jnp.concatenate(block, axis=0).astype(low), key_wide[...], 1, 0).astype(low)
            for n in range(count):
                r_open[:, lanes_of(h + n)] = both[n * span:(n + 1) * span]

        for h in heads_of(g)[::2]:
            open_heads(h, 2, 2 * packed)
        if extra(g):
            open_heads(last, 1, single)
        at = group_lanes(g)
        take(r_one.at[:, at], one_got.at[g])
        upstream[upper, at] = jnp.where(low_here, r_open[:, at], r_one[:, at])
        upstream[lower, at] = jnp.where(low_here, r_one[:, at], jnp.where(high_here, r_open[:, at], r_two[:, at]))

    @pl.when(gets)
    def _():
        send_low.wait_recv()
        pass_low.start()
        pass_on(0)

    swap.wait_recv()
    for n in range(2):
        lines = lines_of(n, span)
        total = at_span(pair_acc, spans[n]) + pair_recv[lines, :]
        key_grad[lines, :] = total[:, :dim].astype(low)
        value_grad[lines, :] = total[:, dim:].astype(low)

    plain = first

    @pl.when(gets)
    def _():
        take(key_low.at[rest_half, :], low_got.at[1])
        key_wide[span:, :] = jnp.zeros((dim - span, dim), low)
        key_wide[:span, :] = key_low[...]
        for g in range(1, groups):
            pass_on(g)
            assemble(g - 1)
        assemble(groups - 1)

    @pl.when(jnp.logical_not(gets))
    def _():
        upstream[...] = jnp.zeros_like(upstream)

    def drain(core, sending, getting, relaying):
        two, pack = (last + 1 - first) * span, 2 * units * packed + single
        lines = 2 * rows + 4 * rows + (span if relaying else 0)
        if sending:
            lines += span // 2 + plain * rows + two + two + pack
        if getting:
            lines += span // 2 + (two if core else pack)
        take(tally.at[pl.ds(0, lines), :], gone.at[0])

    for core in range(2):
        mine = me == core
        pl.when(mine & sends & gets)(functools.partial(drain, core, True, True, False))
        pl.when(mine & jnp.logical_not(gets))(functools.partial(drain, core, True, False, False))
        pl.when(mine & relays)(functools.partial(drain, core, False, True, True))
        pl.when(mine & jnp.logical_not(sends | relays))(functools.partial(drain, core, False, True, False))

    @pl.when(gets)
    def _():
        take(upstream.at[:, lanes_of(0, plain)], dq_got.at[0])


def store(key_grad, value_grad, upstream, key_out, value_out, upstream_out, sem):
    copies = [
        pltpu.make_async_copy(src, dst, sem.at[i])
        for i, (src, dst) in enumerate(
            ((upstream, upstream_out), (key_grad, key_out), (value_grad, value_out))
        )
    ]
    for copy in copies:
        copy.start()
    for copy in copies:
        copy.wait()


def body(query, keys, values, attn_out, grad_out, span_pairs):
    _, rows, width = query.shape
    dim = keys.shape[2]
    heads = width // dim
    ranks = lax.axis_size("cp")
    sections = lax.axis_size("pp")
    seq = ranks * rows
    low, full = jnp.bfloat16, jnp.float32
    dma = pltpu.SemaphoreType.DMA
    vmem = pl.BlockSpec(memory_space=pltpu.VMEM)
    hbm = pl.BlockSpec(memory_space=pltpu.HBM)

    def spaces(*shapes):
        return [pltpu.VMEM(shape, low) for shape in shapes]

    tall, flat, block = (rows, width), (seq, dim), (rows // 2, width)
    if ranks == 2 and lax.axis_size("tp") > 2 and sections > 1 and dim == 128 and rows == 192 and heads == 16:
        groups, packs = 3, ((heads - 2) * (5 * rows // 24) + rows // 4, dim)
        run = functools.partial(pair_kernel, sections, 1, heads - 1, groups)
        scratch = (
            spaces(tall, tall, tall, flat, flat, flat, flat, tall, block, block, packs, packs, packs)
            + spaces(block, block, packs, block, (rows // 2, dim), (dim, dim))
            + spaces((heads * rows, seq), (heads * rows, seq), (rows // 2, dim), (3 * heads * rows, dim))
            + [
                pltpu.VMEM((rows, seq), full),
                pltpu.VMEM((seq, 2 * dim), full),
                pltpu.VMEM((rows, 2 * dim), full),
                pltpu.VMEM((rows, 2 * dim), full),
                pltpu.SMEM((ranks, 2), jnp.int32),
            ]
            + [dma((n,)) for n in (4, 1, 2, 1, groups, groups, groups, groups, 1, 1, 1)]
            + [pltpu.SemaphoreType.REGULAR] * 2
        )
    else:
        others = max(ranks - 1, 1)
        run = functools.partial(kernel, ranks, sections, 2 * rows if ranks % 2 == 0 else rows)
        scratch = (
            spaces(tall, tall, tall, flat, flat, tall)
            + [
                pltpu.VMEM((rows, seq), full),
                pltpu.VMEM((2, rows, 1), full),
                pltpu.VMEM((rows, dim), full),
                pltpu.VMEM((seq, 2 * dim), full),
                pltpu.VMEM((others, rows, 2 * dim), full),
                pltpu.SMEM((ranks, 2), jnp.int32),
            ]
            + [dma((9,)), dma((2, others)), dma((2, others)), dma((heads + 1,)), dma((heads + 1,))]
            + [dma((others,)), dma((others,))]
        )
    key_grad, value_grad, upstream = pl.pallas_call(
        run,
        out_shape=(
            pltpu.VMEM((rows, dim), low),
            pltpu.VMEM((rows, dim), low),
            pltpu.VMEM((rows, width), low),
        ),
        in_specs=[hbm] * 6,
        out_specs=(vmem, vmem, vmem),
        scratch_shapes=scratch,
        compiler_params=pltpu.CompilerParams(
            collective_id=0, has_side_effects=True, vmem_limit_bytes=64 * 1024 * 1024 - 1200 * 1024
        ),
        name="backward",
    )(span_pairs, query[0], keys[0], values[0], attn_out[0], grad_out[0])
    anywhere = pl.BlockSpec(memory_space=pl.ANY)
    key_grad, value_grad, upstream = pl.pallas_call(
        store,
        out_shape=(
            jax.ShapeDtypeStruct((rows, dim), low),
            jax.ShapeDtypeStruct((rows, dim), low),
            jax.ShapeDtypeStruct((rows, width), low),
        ),
        in_specs=[anywhere] * 3,
        out_specs=(anywhere,) * 3,
        scratch_shapes=[dma((3,))],
        compiler_params=pltpu.CompilerParams(vmem_limit_bytes=1024 * 1024),
        name="store",
    )(key_grad, value_grad, upstream)
    return key_grad[None], value_grad[None], upstream[None]


def solution(mesh):
    spec = P("pp", "cp", "tp")
    return jax.shard_map(
        body,
        mesh=mesh,
        in_specs=(spec, spec, spec, spec, spec, P()),
        out_specs=(spec, spec, spec),
        check_vma=False,
    )
```

```python
import functools
import math

import jax
import jax.numpy as jnp
from jax import lax
from jax.experimental import pallas as pl
from jax.experimental.pallas import tpu as pltpu
from jax.sharding import PartitionSpec as P

MESH = pl.DeviceIdType.MESH
NEG = -1e30
LOG2E = math.log2(math.e)


def kernel(
    ranks, sections, block_len,
    pairs_hbm, query, keys, values, attn_out, grad_out,
    key_grad, value_grad, upstream,
    q_buf, o_buf, g_buf, k_buf, v_buf, dq_buf, bias, stats, dq_acc, pair_acc, pair_recv,
    pairs, in_sem, kv_send, kv_recv, dq_send, dq_recv, pair_send, pair_got,
):
    rows, width = q_buf.shape
    dim = k_buf.shape[1]
    heads = width // dim
    span = rows // 2
    seq = ranks * rows
    blocks = seq // block_len
    scale = 1.0 / math.sqrt(dim)
    me = lax.axis_index("cp")
    sec = lax.axis_index("pp")
    mine = pl.ds(0, rows)

    barrier = pltpu.get_barrier_semaphore()
    for off in range(1, ranks):
        pl.semaphore_signal(
            barrier, inc=1, device_id={"cp": lax.rem(me + off, ranks)}, device_id_type=MESH
        )

    @pl.when(sec < sections - 1)
    def _():
        pl.semaphore_signal(barrier, inc=1, device_id={"pp": sec + 1}, device_id_type=MESH)

    own = [
        pltpu.make_async_copy(keys, k_buf.at[mine, :], in_sem.at[0]),
        pltpu.make_async_copy(values, v_buf.at[mine, :], in_sem.at[1]),
    ]
    first, rest = pl.ds(0, dim), pl.ds(dim, width - dim)
    wide = ((query, q_buf), (grad_out, g_buf), (attn_out, o_buf))
    begin = [
        pltpu.make_async_copy(src.at[:, first], dst.at[:, first], in_sem.at[2 + i])
        for i, (src, dst) in enumerate(wide)
    ]
    later = [
        pltpu.make_async_copy(src.at[:, rest], dst.at[:, rest], in_sem.at[5 + i])
        for i, (src, dst) in enumerate(wide)
    ]
    table = pltpu.make_async_copy(pairs_hbm, pairs, in_sem.at[8])
    for copy in [table] + own + begin:
        copy.start()

    pl.semaphore_wait(barrier, ranks - 1 + (sec > 0).astype(jnp.int32))
    sent = []
    for off in range(1, ranks):
        for which, (src, buf) in enumerate(((keys, k_buf), (values, v_buf))):
            sent.append(
                pltpu.make_async_remote_copy(
                    src_ref=src,
                    dst_ref=buf.at[pl.ds((ranks - off) * rows, rows), :],
                    send_sem=kv_send.at[which, off - 1],
                    recv_sem=kv_recv.at[which, off - 1],
                    device_id={"cp": lax.rem(me + off, ranks)},
                    device_id_type=MESH,
                )
            )
    for copy in sent + later:
        copy.start()

    table.wait()
    row = lax.broadcasted_iota(jnp.int32, (rows, rows), 0)
    col = lax.broadcasted_iota(jnp.int32, (rows, rows), 1)
    q_pos = jnp.where(row < span, pairs[me, 0] * span, pairs[me, 1] * span - span) + row
    for r in range(ranks):
        rank = lax.rem(me + r, ranks)
        k_pos = jnp.where(col < span, pairs[rank, 0] * span, pairs[rank, 1] * span - span) + col
        bias[:, r * rows:(r + 1) * rows] = jnp.where(k_pos <= q_pos, 0.0, NEG)
    pair_acc[...] = jnp.zeros_like(pair_acc)

    for copy in own + begin:
        copy.wait()
    for copy in sent:
        copy.wait_recv()

    def dot(a, b, da, db):
        return lax.dot_general(a, b, (((da,), (db,)), ((), ())), preferred_element_type=jnp.float32)

    def lanes_of(h):
        return pl.ds(h * dim if isinstance(h, int) else pl.multiple_of(h * dim, dim), dim)

    def send_dq(h, lines, slot):
        return pltpu.make_async_remote_copy(
            src_ref=dq_buf.at[lines, lanes_of(h)],
            dst_ref=upstream.at[lines, lanes_of(h)],
            send_sem=dq_send.at[slot],
            recv_sem=dq_recv.at[slot],
            device_id={"pp": jnp.maximum(sec - 1, 0)},
            device_id_type=MESH,
        )

    def rows_of_head(h, lines, slot):
        lanes = lanes_of(h)
        q = q_buf[lines, lanes]
        g = g_buf[lines, lanes]
        delta = jnp.sum(
            g.astype(jnp.float32) * o_buf[lines, lanes].astype(jnp.float32), axis=1, keepdims=True
        )

        def scores(b):
            at = b * block_len if isinstance(b, int) else pl.multiple_of(b * block_len, block_len)
            part = pl.ds(at, block_len)
            return part, dot(q, k_buf[part, :], 1, 1) * (scale * LOG2E) + bias[lines, part]

        def terms(part, prob):
            dprob = dot(g, v_buf[part, :], 1, 1)
            dscore = (prob * (dprob - delta) * scale).astype(jnp.bfloat16)
            return prob.astype(jnp.bfloat16), dscore, dot(dscore, k_buf[part, :], 1, 0)

        def pair_terms(part, prob_low, dscore):
            pair_acc[part, :dim] += dot(dscore, q, 0, 0)
            pair_acc[part, dim:] += dot(prob_low, g, 0, 0)

        def start_dq(dq):
            dq_buf[lines, lanes] = dq.astype(jnp.bfloat16)

            @pl.when(sec > 0)
            def _():
                send_dq(h, lines, slot).start()

        if blocks == 1:
            part, score = scores(0)
            top = jnp.max(score, axis=1, keepdims=True)
            prob = jnp.exp2(score - top)
            prob = prob * (1.0 / jnp.sum(prob, axis=1, keepdims=True))
            prob_low, dscore, dq = terms(part, prob)
            start_dq(dq)
            pair_terms(part, prob_low, dscore)
        else:
            stats[0, lines] = jnp.full((lines.size, 1), NEG, jnp.float32)
            stats[1, lines] = jnp.zeros((lines.size, 1), jnp.float32)
            dq_acc[lines] = jnp.zeros((lines.size, dim), jnp.float32)

            def gather_stats(b, _):
                _, score = scores(b)
                before = stats[0, lines]
                top = jnp.maximum(before, jnp.max(score, axis=1, keepdims=True))
                mass = jnp.sum(jnp.exp2(score - top), axis=1, keepdims=True)
                stats[1, lines] = stats[1, lines] * jnp.exp2(before - top) + mass
                stats[0, lines] = top
                return 0

            def gather_terms(b, _):
                part, score = scores(b)
                prob = jnp.exp2(score - stats[0, lines]) * (1.0 / stats[1, lines])
                prob_low, dscore, dq = terms(part, prob)
                dq_acc[lines] += dq
                pair_terms(part, prob_low, dscore)
                return 0

            lax.fori_loop(0, blocks, gather_stats, 0)
            lax.fori_loop(0, blocks, gather_terms, 0)
            start_dq(dq_acc[lines])

    pieces = [(h, pl.ds(0, rows), h) for h in range(heads)]
    for piece in pieces[:1]:
        rows_of_head(*piece)

    @pl.when(sec == sections - 1)
    def _():
        upstream[...] = jnp.zeros_like(upstream)

    for copy in later:
        copy.wait()

    def one_head(h, _):
        rows_of_head(h, pl.ds(0, rows), h)
        return 0

    lax.fori_loop(1, heads, one_head, 0)

    pair_sent = []
    for off in range(1, ranks):
        dst = lax.rem(me + off, ranks)
        pair_sent.append(
            pltpu.make_async_remote_copy(
                src_ref=pair_acc.at[pl.ds(off * rows, rows), :],
                dst_ref=pair_recv.at[off - 1],
                send_sem=pair_send.at[off - 1],
                recv_sem=pair_got.at[off - 1],
                device_id={"cp": dst},
                device_id_type=MESH,
            )
        )
    for copy in pair_sent:
        copy.start()
    for copy in sent:
        copy.wait_send()
    for copy in pair_sent:
        copy.wait_recv()
    total = pair_acc[mine, :]
    for off in range(1, ranks):
        total = total + pair_recv[off - 1]
    key_grad[...] = total[:, :dim].astype(jnp.bfloat16)
    value_grad[...] = total[:, dim:].astype(jnp.bfloat16)
    for copy in pair_sent:
        copy.wait_send()

    @pl.when(sec > 0)
    def _():
        for piece in pieces:
            send_dq(*piece).wait_send()

    @pl.when(sec < sections - 1)
    def _():
        for piece in pieces:
            send_dq(*piece).wait_recv()


def pair_kernel(
    sections, first, last, per,
    pairs_hbm, query, keys, values, attn_out, grad_out,
    key_grad, value_grad, upstream,
    q_buf, o_buf, g_buf, k_raw, v_raw, k_buf, v_buf, d_buf, y_got, s_buf, p_own, p_got, p_out,
    r_one, r_two, r_pack, r_open, key_low, key_wide, ds_buf, pr_buf, relay_buf, tally, bias, pair_acc, pair_out, pair_recv,
    pairs, in_sem, kv_got, low_got, dq_got, one_got, two_got, pack_got, give_got, swap_got, relay_got, gone,
    met, may_send,
):
    rows, width = q_buf.shape
    dim = k_buf.shape[1]
    heads = width // dim
    span = rows // 2
    seq = 2 * rows
    tile = span // 12
    bins = ((12, 4), (11, 5), (10, 6), (9, 7), (8, 3, 2, 1))
    packed = tile * len(bins)
    single = packed + tile
    units = (last - first) // 2
    held, relayed = 3, 3
    groups = -(-units // per)
    scale = 1.0 / math.sqrt(dim)
    low, full = jnp.bfloat16, jnp.float32
    me = lax.axis_index("cp")
    sec = lax.axis_index("pp")
    peer = {"cp": 1 - me}
    below = {"pp": jnp.maximum(sec - 1, 0)}
    sends, gets = sec > 0, sec < sections - 1
    tp = lax.axis_index("tp")
    early = (sec == 0) & (tp == 0)
    relays = (sec == 0) & (tp == 1 + me)
    detours = (sec == 1) & (tp == 0)
    upper, lower, every = pl.ds(0, span), pl.ds(span, span), pl.ds(0, rows)

    def remote(src, dst, recv, device):
        return pltpu.make_async_remote_copy(
            src_ref=src, dst_ref=dst, send_sem=gone.at[0], recv_sem=recv, device_id=device, device_id_type=MESH
        )

    def take(ref, sem):
        pltpu.make_async_copy(ref, ref, sem).wait()

    own = [
        pltpu.make_async_copy(keys, k_raw.at[every, :], in_sem.at[0]),
        pltpu.make_async_copy(values, v_raw.at[every, :], in_sem.at[0]),
    ]
    head, rest = pl.ds(0, dim), pl.ds(dim, width - dim)
    wide = ((query, q_buf), (grad_out, g_buf), (attn_out, o_buf))
    begin = [pltpu.make_async_copy(src.at[:, head], dst.at[:, head], in_sem.at[1]) for src, dst in wide]
    later = [pltpu.make_async_copy(src.at[:, rest], dst.at[:, rest], in_sem.at[2]) for src, dst in wide]
    table = pltpu.make_async_copy(pairs_hbm, pairs, in_sem.at[3])
    other = pl.ds(rows, rows)

    barrier = pltpu.get_barrier_semaphore()

    @pl.when(me == 1)
    def _():
        pl.semaphore_signal(barrier, inc=1, device_id=peer, device_id_type=MESH)

    @pl.when(me == 0)
    def _():
        pl.semaphore_wait(barrier, 1)
        pl.semaphore_signal(met, inc=1, device_id=peer, device_id_type=MESH)
        for src, dst in ((keys, k_raw), (values, v_raw)):
            remote(src, dst.at[other, :], kv_got.at[0], peer).start()

    for copy in own + [table] + begin:
        copy.start()

    @pl.when(me == 1)
    def _():
        take(k_raw, in_sem.at[0])
        pl.semaphore_wait(met, 1)
        for buf in (k_raw, v_raw):
            remote(buf.at[every, :], buf.at[other, :], kv_got.at[0], peer).start()

        @pl.when(gets)
        def _():
            pl.semaphore_signal(barrier, inc=1, device_id={"pp": sec + 1}, device_id_type=MESH)

        @pl.when((sec == 0) & ((tp == 1) | (tp == 2)))
        def _():
            pl.semaphore_signal(barrier, inc=1, device_id={"tp": 0}, device_id_type=MESH)

    for copy in later:
        copy.start()

    table.wait()
    row = lax.broadcasted_iota(jnp.int32, (rows, seq), 0)
    col = lax.broadcasted_iota(jnp.int32, (rows, seq), 1)
    spans = [pairs[me, 0], pairs[me, 1], pairs[1 - me, 0], pairs[1 - me, 1]]
    q_pos = jnp.where(row < span, spans[0] * span, spans[1] * span - span) + row
    bias[...] = jnp.where(col <= q_pos, 0.0, NEG)
    pair_acc[...] = jnp.zeros_like(pair_acc)
    low_here = spans[0] == 0
    high_here = spans[1] == 0
    here = low_here | high_here

    def block_of(ref, n):
        return ref[n * span:(n + 1) * span, :]

    def of_span(ref, s):
        block = block_of(ref, 0)
        for n in range(1, 4):
            block = jnp.where(spans[n] == s, block_of(ref, n), block)
        return block

    def at_span(ref, s):
        block = block_of(ref, 0)
        for n in range(1, 4):
            block = jnp.where(s == n, block_of(ref, n), block)
        return block

    @pl.when(me == 0)
    def _():
        take(k_raw, in_sem.at[0])

    take(k_raw, kv_got.at[0])
    for s in range(4):
        k_buf[pl.ds(s * span, span), :] = of_span(k_raw, s)

    half = pl.ds(pl.multiple_of(me * (span // 2), span // 2), span // 2)
    rest_half = pl.ds(pl.multiple_of((1 - me) * (span // 2), span // 2), span // 2)
    send_low = remote(k_buf.at[half, :], key_low.at[half, :], low_got.at[0], below)
    pass_low = remote(key_low.at[half, :], key_low.at[half, :], low_got.at[1], peer)

    @pl.when(sends)
    def _():
        @pl.when(me == 1)
        def _():
            pl.semaphore_wait(barrier, 1)
            pl.semaphore_signal(may_send, inc=1, device_id=peer, device_id_type=MESH)

            @pl.when(detours)
            def _():
                pl.semaphore_signal(barrier, inc=1, device_id=below, device_id_type=MESH)

        @pl.when(me == 0)
        def _():
            pl.semaphore_wait(may_send, 1)

        send_low.start()

    for s in range(4):
        v_buf[pl.ds(s * span, span), :] = of_span(v_raw, s)
    take(q_buf.at[:, pl.ds(0, 3 * dim)], in_sem.at[1])

    def dot(a, b, da, db):
        return lax.dot_general(a, b, (((da,), (db,)), ((), ())), preferred_element_type=full)

    def lanes_of(h, count=1):
        return pl.ds(h * dim if isinstance(h, int) else pl.multiple_of(h * dim, dim), count * dim)

    def lines_of(n, size, count=1):
        return pl.ds(n * size if isinstance(n, int) else pl.multiple_of(n * size, size), count * size)

    def by_core(if_one, if_zero):
        pl.when(me == 1)(if_one)
        pl.when(me == 0)(if_zero)

    def send_dq(h, lines):
        return remote(
            d_buf.at[lines, lanes_of(h)], upstream.at[lines, lanes_of(h)], dq_got.at[0], below
        )

    def unit_lanes(i):
        return lanes_of(first + 2 * i, 2)

    def unit_lines(i):
        return lines_of(i, 2 * packed)

    def group_of(i):
        return i // per if isinstance(i, int) else lax.div(i, per)

    def units_of(g):
        return min(per, units - per * g) if isinstance(g, int) else per

    def extra(g):
        return 1 if isinstance(g, int) and g == groups - 1 else 0

    def heads_of(g):
        return range(first + 2 * per * g, first + 2 * (per * g + units_of(g)))

    def group_lanes(g):
        return lanes_of(first + 2 * per * g, 2 * units_of(g) + extra(g))

    def group_lines(g):
        if extra(g):
            return pl.ds(2 * per * g * packed, 2 * units_of(g) * packed + single)
        return lines_of(per * g, 2 * packed, units_of(g))

    def send_one(i):
        at = unit_lanes(i)
        return remote(d_buf.at[upper, at], r_one.at[:, at], one_got.at[group_of(i)], below)

    alone = pl.ds(2 * units * packed, single)
    last_lanes = lanes_of(last)
    send_last = remote(d_buf.at[upper, last_lanes], r_one.at[:, last_lanes], one_got.at[groups - 1], below)
    give_last_block = remote(d_buf.at[lower, last_lanes], y_got.at[:, last_lanes], give_got.at[groups - 1], peer)
    give_last_pack = remote(p_own.at[alone, :], p_got.at[alone, :], give_got.at[groups - 1], peer)

    def send_two(g):
        return remote(s_buf.at[:, group_lanes(g)], r_two.at[:, group_lanes(g)], two_got.at[g], below)

    def send_pack(g):
        return remote(p_out.at[group_lines(g), :], r_pack.at[group_lines(g), :], pack_got.at[g], below)

    def give_block(i):
        at = unit_lanes(i)
        return remote(d_buf.at[lower, at], y_got.at[:, at], give_got.at[group_of(i)], peer)

    def give_pack(i):
        at = unit_lines(i)
        return remote(p_own.at[at, :], p_got.at[at, :], give_got.at[group_of(i)], peer)

    def pass_two(g):
        return remote(r_two.at[:, group_lanes(g)], r_two.at[:, group_lanes(g)], two_got.at[g], peer)

    def pass_pack(g):
        return remote(r_pack.at[group_lines(g), :], r_pack.at[group_lines(g), :], pack_got.at[g], peer)

    def gradients(h, lines, plain=False):
        lanes = lanes_of(h)
        q = q_buf[lines, lanes]
        g = g_buf[lines, lanes]
        delta = jnp.sum(g.astype(full) * o_buf[lines, lanes].astype(full), axis=1, keepdims=True)
        score = dot(q, k_buf[...], 1, 1) * (scale * LOG2E) + bias[lines, :]
        top = jnp.max(score, axis=1, keepdims=True)
        power = jnp.exp2(score - top)
        dprob = (dot(g, v_buf[...], 1, 1) - delta) * scale
        inverse = 1.0 / jnp.sum(power, axis=1, keepdims=True)
        prob = power * inverse
        dscore = (prob * dprob).astype(low)
        place = pl.ds(
            h * rows + lines.start if isinstance(h, int) else pl.multiple_of(h * rows + lines.start, span), lines.size
        )
        pr_buf[place, :] = prob.astype(low)
        ds_buf[place, :] = dscore
        if plain:
            return dscore, dot((power * dprob).astype(low), k_buf[...], 1, 0) * inverse
        return dscore, dot(dscore, k_buf[...], 1, 0)

    def pair_terms(h, _):
        place = lines_of(h, rows)
        pair_acc[:, :dim] += dot(ds_buf[place, :], q_buf[:, lanes_of(h)], 0, 0)
        pair_acc[:, dim:] += dot(pr_buf[place, :], g_buf[:, lanes_of(h)], 0, 0)
        return 0

    def plain_pieces(pieces, before=None):
        for h, lines in pieces:
            d_buf[lines, lanes_of(h)] = gradients(h, lines, h == 0)[1].astype(low)

        @pl.when(sends)
        def _():
            if before is not None:
                before()
            for piece in pieces:
                send_dq(*piece).start()

    near, far = lanes_of(first + 2 * relayed), lanes_of(first + 2 * relayed + 1)
    at_last = one_got.at[group_of(relayed)]
    half_unit = remote(d_buf.at[upper, near], r_one.at[:, near], at_last, below)
    detour = remote(d_buf.at[upper, far], relay_buf, relay_got.at[0], {"pp": 0, "tp": 1 + me})
    relay = remote(relay_buf, r_one.at[:, far], at_last, {"tp": 0})

    def pack_head(h):
        lanes = lanes_of(h)
        dscore, dq = gradients(h, every)
        d_buf[upper, lanes] = jnp.where(low_here, dq[span:], dq[:span]).astype(low)
        d_buf[lower, lanes] = dq[span:].astype(low)
        block = jnp.where(high_here, dscore[span:, :dim].astype(full), dscore[:span, :dim].astype(full))
        lines = []
        for group in bins:
            line, at = 0.0, 0
            for n in group:
                entry = block[(n - 1) * tile:n * tile]
                line = line + (pltpu.roll(entry, at, 1) if at else entry)
                at += n * tile
            lines.append(line)
        return lines

    def unpack_head(lines):
        lane = lax.broadcasted_iota(jnp.int32, (tile, dim), 1)
        entries = {}
        for b, group in enumerate(bins):
            line, at = lines[b * tile:(b + 1) * tile], 0
            for n in group:
                entry = pltpu.roll(line, dim - at, 1) if at else line
                entries[n] = jnp.where(lane < n * tile, entry, 0.0)
                at += n * tile
        return [entries[n] for n in range(1, 13)]

    def gives(i):
        by_core(lambda: give_pack(i).start(), lambda: give_block(i).start())

    def second_sends(g):
        def two():
            at = group_lanes(g)
            take(y_got.at[:, at], give_got.at[g])
            s_buf[:, at] = jnp.where(here, y_got[:, at], d_buf[lower, at])
            send_two(g).start()

        def one():
            at = group_lines(g)
            take(p_got.at[at, :], give_got.at[g])
            p_out[at, :] = jnp.where(here, p_own[at, :], p_got[at, :])
            send_pack(g).start()

        by_core(two, one)

    def packed_unit(i, _):
        lines = pack_head(first + 2 * i) + pack_head(first + 2 * i + 1)
        p_own[unit_lines(i), :] = jnp.concatenate(lines, axis=0).astype(low)

        @pl.when(sends)
        def _():
            gives(i)

            @pl.when((i < units - held) & jnp.logical_not(detours & (i == relayed)))
            def _():
                send_one(i).start()

            @pl.when(detours & (i == relayed))
            def _():
                half_unit.start()
                pl.semaphore_wait(met, 1)
                detour.start()

            @pl.when((i > 0) & (lax.rem(i, per) == 0))
            def _():
                second_sends(group_of(i) - 1)

        return 0

    plain_pieces([(0, every)])

    @pl.when(early & (me == 1))
    def _():
        pl.semaphore_wait(barrier, 3)
        for core in range(2):
            for to in ({"tp": 1 + core, "cp": core}, {"pp": 1, "cp": core}):
                pl.semaphore_signal(met, inc=1, device_id=to, device_id_type=MESH)

    take(tally.at[pl.ds(0, 3 * rows * (heads - 1)), :], in_sem.at[2])
    lax.fori_loop(0, units, packed_unit, 0)

    lines = pack_head(last)
    p_own[alone, :] = jnp.concatenate(lines + [jnp.zeros((tile, dim), full)], axis=0).astype(low)

    @pl.when(sends)
    def _():
        by_core(give_last_pack.start, give_last_block.start)

    @pl.when(relays)
    def _():
        take(relay_buf, relay_got.at[0])
        pl.semaphore_wait(met, 1)
        relay.start()

    lax.fori_loop(0, 4, pair_terms, 0, unroll=2)

    @pl.when(sends)
    def _():
        second_sends(groups - 1)
        for i in range(units - held, units):
            send_one(i).start()
        send_last.start()

    lax.fori_loop(4, heads, pair_terms, 0, unroll=2)

    for n in range(2):
        pair_out[lines_of(n, span), :] = at_span(pair_acc, spans[2 + n])
    swap = remote(pair_out, pair_recv, swap_got.at[0], peer)
    swap.start()

    def pass_on(g):
        def two():
            take(r_two.at[:, group_lanes(g)], two_got.at[g])
            pass_two(g).start()

        def one():
            take(r_pack.at[group_lines(g), :], pack_got.at[g])
            pass_pack(g).start()

        by_core(two, one)

    def assemble(g):
        by_core(
            lambda: take(r_pack.at[group_lines(g), :], pack_got.at[g]),
            lambda: take(r_two.at[:, group_lanes(g)], two_got.at[g]),
        )
        def open_heads(h, count, size):
            lines = r_pack[pl.ds((h - first) * packed, size), :].astype(full)
            block = []
            for n in range(count):
                block += unpack_head(lines[n * packed:(n + 1) * packed])
            both = dot(jnp.concatenate(block, axis=0).astype(low), key_wide[...], 1, 0).astype(low)
            for n in range(count):
                r_open[:, lanes_of(h + n)] = both[n * span:(n + 1) * span]

        for h in heads_of(g)[::2]:
            open_heads(h, 2, 2 * packed)
        if extra(g):
            open_heads(last, 1, single)
        at = group_lanes(g)
        take(r_one.at[:, at], one_got.at[g])
        upstream[upper, at] = jnp.where(low_here, r_open[:, at], r_one[:, at])
        upstream[lower, at] = jnp.where(low_here, r_one[:, at], jnp.where(high_here, r_open[:, at], r_two[:, at]))

    @pl.when(gets)
    def _():
        send_low.wait_recv()
        pass_low.start()
        pass_on(0)

    swap.wait_recv()
    for n in range(2):
        lines = lines_of(n, span)
        total = at_span(pair_acc, spans[n]) + pair_recv[lines, :]
        key_grad[lines, :] = total[:, :dim].astype(low)
        value_grad[lines, :] = total[:, dim:].astype(low)

    plain = first

    @pl.when(gets)
    def _():
        take(key_low.at[rest_half, :], low_got.at[1])
        key_wide[span:, :] = jnp.zeros((dim - span, dim), low)
        key_wide[:span, :] = key_low[...]
        for g in range(1, groups):
            pass_on(g)
            assemble(g - 1)
        assemble(groups - 1)

    @pl.when(jnp.logical_not(gets))
    def _():
        upstream[...] = jnp.zeros_like(upstream)

    def drain(core, sending, getting, relaying):
        two, pack = (last + 1 - first) * span, 2 * units * packed + single
        lines = 2 * rows + 4 * rows + (span if relaying else 0)
        if sending:
            lines += span // 2 + plain * rows + two + two + pack
        if getting:
            lines += span // 2 + (two if core else pack)
        take(tally.at[pl.ds(0, lines), :], gone.at[0])

    for core in range(2):
        mine = me == core
        pl.when(mine & sends & gets)(functools.partial(drain, core, True, True, False))
        pl.when(mine & jnp.logical_not(gets))(functools.partial(drain, core, True, False, False))
        pl.when(mine & relays)(functools.partial(drain, core, False, True, True))
        pl.when(mine & jnp.logical_not(sends | relays))(functools.partial(drain, core, False, True, False))

    @pl.when(gets)
    def _():
        take(upstream.at[:, lanes_of(0, plain)], dq_got.at[0])


def store(key_grad, value_grad, upstream, key_out, value_out, upstream_out, sem):
    copies = [
        pltpu.make_async_copy(src, dst, sem.at[i])
        for i, (src, dst) in enumerate(
            ((upstream, upstream_out), (key_grad, key_out), (value_grad, value_out))
        )
    ]
    for copy in copies:
        copy.start()
    for copy in copies:
        copy.wait()


def body(query, keys, values, attn_out, grad_out, span_pairs):
    _, rows, width = query.shape
    dim = keys.shape[2]
    heads = width // dim
    ranks = lax.axis_size("cp")
    sections = lax.axis_size("pp")
    seq = ranks * rows
    low, full = jnp.bfloat16, jnp.float32
    dma = pltpu.SemaphoreType.DMA
    vmem = pl.BlockSpec(memory_space=pltpu.VMEM)
    hbm = pl.BlockSpec(memory_space=pltpu.HBM)

    def spaces(*shapes):
        return [pltpu.VMEM(shape, low) for shape in shapes]

    tall, flat, block = (rows, width), (seq, dim), (rows // 2, width)
    if ranks == 2 and lax.axis_size("tp") > 2 and sections > 1 and dim == 128 and rows == 192 and heads == 16:
        groups, packs = 3, ((heads - 2) * (5 * rows // 24) + rows // 4, dim)
        run = functools.partial(pair_kernel, sections, 1, heads - 1, groups)
        scratch = (
            spaces(tall, tall, tall, flat, flat, flat, flat, tall, block, block, packs, packs, packs)
            + spaces(block, block, packs, block, (rows // 2, dim), (dim, dim))
            + spaces((heads * rows, seq), (heads * rows, seq), (rows // 2, dim), (3 * heads * rows, dim))
            + [
                pltpu.VMEM((rows, seq), full),
                pltpu.VMEM((seq, 2 * dim), full),
                pltpu.VMEM((rows, 2 * dim), full),
                pltpu.VMEM((rows, 2 * dim), full),
                pltpu.SMEM((ranks, 2), jnp.int32),
            ]
            + [dma((n,)) for n in (4, 1, 2, 1, groups, groups, groups, groups, 1, 1, 1)]
            + [pltpu.SemaphoreType.REGULAR] * 2
        )
    else:
        others = max(ranks - 1, 1)
        run = functools.partial(kernel, ranks, sections, 2 * rows if ranks % 2 == 0 else rows)
        scratch = (
            spaces(tall, tall, tall, flat, flat, tall)
            + [
                pltpu.VMEM((rows, seq), full),
                pltpu.VMEM((2, rows, 1), full),
                pltpu.VMEM((rows, dim), full),
                pltpu.VMEM((seq, 2 * dim), full),
                pltpu.VMEM((others, rows, 2 * dim), full),
                pltpu.SMEM((ranks, 2), jnp.int32),
            ]
            + [dma((9,)), dma((2, others)), dma((2, others)), dma((heads + 1,)), dma((heads + 1,))]
            + [dma((others,)), dma((others,))]
        )
    key_grad, value_grad, upstream = pl.pallas_call(
        run,
        out_shape=(
            pltpu.VMEM((rows, dim), low),
            pltpu.VMEM((rows, dim), low),
            pltpu.VMEM((rows, width), low),
        ),
        in_specs=[hbm] * 6,
        out_specs=(vmem, vmem, vmem),
        scratch_shapes=scratch,
        compiler_params=pltpu.CompilerParams(
            collective_id=0, has_side_effects=True, vmem_limit_bytes=64 * 1024 * 1024 - 1200 * 1024
        ),
        name="backward",
    )(span_pairs, query[0], keys[0], values[0], attn_out[0], grad_out[0])
    anywhere = pl.BlockSpec(memory_space=pl.ANY)
    key_grad, value_grad, upstream = pl.pallas_call(
        store,
        out_shape=(
            jax.ShapeDtypeStruct((rows, dim), low),
            jax.ShapeDtypeStruct((rows, dim), low),
            jax.ShapeDtypeStruct((rows, width), low),
        ),
        in_specs=[anywhere] * 3,
        out_specs=(anywhere,) * 3,
        scratch_shapes=[dma((3,))],
        compiler_params=pltpu.CompilerParams(vmem_limit_bytes=1024 * 1024),
        name="store",
    )(key_grad, value_grad, upstream)
    return key_grad[None], value_grad[None], upstream[None]


def solution(mesh):
    spec = P("pp", "cp", "tp")
    return jax.shard_map(
        body,
        mesh=mesh,
        in_specs=(spec, spec, spec, spec, spec, P()),
        out_specs=(spec, spec, spec),
        check_vma=False,
    )
```

```python
import functools
import math

import jax
import jax.numpy as jnp
from jax import lax
from jax.experimental import pallas as pl
from jax.experimental.pallas import tpu as pltpu
from jax.sharding import PartitionSpec as P

MESH = pl.DeviceIdType.MESH
NEG = -1e30
LOG2E = math.log2(math.e)


def kernel(
    ranks, sections, block_len,
    pairs_hbm, query, keys, values, attn_out, grad_out,
    key_grad, value_grad, upstream,
    q_buf, o_buf, g_buf, k_buf, v_buf, dq_buf, bias, stats, dq_acc, pair_acc, pair_recv,
    pairs, in_sem, kv_send, kv_recv, dq_send, dq_recv, pair_send, pair_got,
):
    rows, width = q_buf.shape
    dim = k_buf.shape[1]
    heads = width // dim
    span = rows // 2
    seq = ranks * rows
    blocks = seq // block_len
    scale = 1.0 / math.sqrt(dim)
    me = lax.axis_index("cp")
    sec = lax.axis_index("pp")
    mine = pl.ds(0, rows)

    barrier = pltpu.get_barrier_semaphore()
    for off in range(1, ranks):
        pl.semaphore_signal(
            barrier, inc=1, device_id={"cp": lax.rem(me + off, ranks)}, device_id_type=MESH
        )

    @pl.when(sec < sections - 1)
    def _():
        pl.semaphore_signal(barrier, inc=1, device_id={"pp": sec + 1}, device_id_type=MESH)

    own = [
        pltpu.make_async_copy(keys, k_buf.at[mine, :], in_sem.at[0]),
        pltpu.make_async_copy(values, v_buf.at[mine, :], in_sem.at[1]),
    ]
    first, rest = pl.ds(0, dim), pl.ds(dim, width - dim)
    wide = ((query, q_buf), (grad_out, g_buf), (attn_out, o_buf))
    begin = [
        pltpu.make_async_copy(src.at[:, first], dst.at[:, first], in_sem.at[2 + i])
        for i, (src, dst) in enumerate(wide)
    ]
    later = [
        pltpu.make_async_copy(src.at[:, rest], dst.at[:, rest], in_sem.at[5 + i])
        for i, (src, dst) in enumerate(wide)
    ]
    table = pltpu.make_async_copy(pairs_hbm, pairs, in_sem.at[8])
    for copy in [table] + own + begin:
        copy.start()

    pl.semaphore_wait(barrier, ranks - 1 + (sec > 0).astype(jnp.int32))
    sent = []
    for off in range(1, ranks):
        for which, (src, buf) in enumerate(((keys, k_buf), (values, v_buf))):
            sent.append(
                pltpu.make_async_remote_copy(
                    src_ref=src,
                    dst_ref=buf.at[pl.ds((ranks - off) * rows, rows), :],
                    send_sem=kv_send.at[which, off - 1],
                    recv_sem=kv_recv.at[which, off - 1],
                    device_id={"cp": lax.rem(me + off, ranks)},
                    device_id_type=MESH,
                )
            )
    for copy in sent + later:
        copy.start()

    table.wait()
    row = lax.broadcasted_iota(jnp.int32, (rows, rows), 0)
    col = lax.broadcasted_iota(jnp.int32, (rows, rows), 1)
    q_pos = jnp.where(row < span, pairs[me, 0] * span, pairs[me, 1] * span - span) + row
    for r in range(ranks):
        rank = lax.rem(me + r, ranks)
        k_pos = jnp.where(col < span, pairs[rank, 0] * span, pairs[rank, 1] * span - span) + col
        bias[:, r * rows:(r + 1) * rows] = jnp.where(k_pos <= q_pos, 0.0, NEG)
    pair_acc[...] = jnp.zeros_like(pair_acc)

    for copy in own + begin:
        copy.wait()
    for copy in sent:
        copy.wait_recv()

    def dot(a, b, da, db):
        return lax.dot_general(a, b, (((da,), (db,)), ((), ())), preferred_element_type=jnp.float32)

    def lanes_of(h):
        return pl.ds(h * dim if isinstance(h, int) else pl.multiple_of(h * dim, dim), dim)

    def send_dq(h, lines, slot):
        return pltpu.make_async_remote_copy(
            src_ref=dq_buf.at[lines, lanes_of(h)],
            dst_ref=upstream.at[lines, lanes_of(h)],
            send_sem=dq_send.at[slot],
            recv_sem=dq_recv.at[slot],
            device_id={"pp": jnp.maximum(sec - 1, 0)},
            device_id_type=MESH,
        )

    def rows_of_head(h, lines, slot):
        lanes = lanes_of(h)
        q = q_buf[lines, lanes]
        g = g_buf[lines, lanes]
        delta = jnp.sum(
            g.astype(jnp.float32) * o_buf[lines, lanes].astype(jnp.float32), axis=1, keepdims=True
        )

        def scores(b):
            at = b * block_len if isinstance(b, int) else pl.multiple_of(b * block_len, block_len)
            part = pl.ds(at, block_len)
            return part, dot(q, k_buf[part, :], 1, 1) * (scale * LOG2E) + bias[lines, part]

        def terms(part, prob):
            dprob = dot(g, v_buf[part, :], 1, 1)
            dscore = (prob * (dprob - delta) * scale).astype(jnp.bfloat16)
            return prob.astype(jnp.bfloat16), dscore, dot(dscore, k_buf[part, :], 1, 0)

        def pair_terms(part, prob_low, dscore):
            pair_acc[part, :dim] += dot(dscore, q, 0, 0)
            pair_acc[part, dim:] += dot(prob_low, g, 0, 0)

        def start_dq(dq):
            dq_buf[lines, lanes] = dq.astype(jnp.bfloat16)

            @pl.when(sec > 0)
            def _():
                send_dq(h, lines, slot).start()

        if blocks == 1:
            part, score = scores(0)
            top = jnp.max(score, axis=1, keepdims=True)
            prob = jnp.exp2(score - top)
            prob = prob * (1.0 / jnp.sum(prob, axis=1, keepdims=True))
            prob_low, dscore, dq = terms(part, prob)
            start_dq(dq)
            pair_terms(part, prob_low, dscore)
        else:
            stats[0, lines] = jnp.full((lines.size, 1), NEG, jnp.float32)
            stats[1, lines] = jnp.zeros((lines.size, 1), jnp.float32)
            dq_acc[lines] = jnp.zeros((lines.size, dim), jnp.float32)

            def gather_stats(b, _):
                _, score = scores(b)
                before = stats[0, lines]
                top = jnp.maximum(before, jnp.max(score, axis=1, keepdims=True))
                mass = jnp.sum(jnp.exp2(score - top), axis=1, keepdims=True)
                stats[1, lines] = stats[1, lines] * jnp.exp2(before - top) + mass
                stats[0, lines] = top
                return 0

            def gather_terms(b, _):
                part, score = scores(b)
                prob = jnp.exp2(score - stats[0, lines]) * (1.0 / stats[1, lines])
                prob_low, dscore, dq = terms(part, prob)
                dq_acc[lines] += dq
                pair_terms(part, prob_low, dscore)
                return 0

            lax.fori_loop(0, blocks, gather_stats, 0)
            lax.fori_loop(0, blocks, gather_terms, 0)
            start_dq(dq_acc[lines])

    pieces = [(h, pl.ds(0, rows), h) for h in range(heads)]
    for piece in pieces[:1]:
        rows_of_head(*piece)

    @pl.when(sec == sections - 1)
    def _():
        upstream[...] = jnp.zeros_like(upstream)

    for copy in later:
        copy.wait()

    def one_head(h, _):
        rows_of_head(h, pl.ds(0, rows), h)
        return 0

    lax.fori_loop(1, heads, one_head, 0)

    pair_sent = []
    for off in range(1, ranks):
        dst = lax.rem(me + off, ranks)
        pair_sent.append(
            pltpu.make_async_remote_copy(
                src_ref=pair_acc.at[pl.ds(off * rows, rows), :],
                dst_ref=pair_recv.at[off - 1],
                send_sem=pair_send.at[off - 1],
                recv_sem=pair_got.at[off - 1],
                device_id={"cp": dst},
                device_id_type=MESH,
            )
        )
    for copy in pair_sent:
        copy.start()
    for copy in sent:
        copy.wait_send()
    for copy in pair_sent:
        copy.wait_recv()
    total = pair_acc[mine, :]
    for off in range(1, ranks):
        total = total + pair_recv[off - 1]
    key_grad[...] = total[:, :dim].astype(jnp.bfloat16)
    value_grad[...] = total[:, dim:].astype(jnp.bfloat16)
    for copy in pair_sent:
        copy.wait_send()

    @pl.when(sec > 0)
    def _():
        for piece in pieces:
            send_dq(*piece).wait_send()

    @pl.when(sec < sections - 1)
    def _():
        for piece in pieces:
            send_dq(*piece).wait_recv()


def pair_kernel(
    sections, first, last, per,
    pairs_hbm, query, keys, values, attn_out, grad_out,
    key_grad, value_grad, upstream,
    q_buf, o_buf, g_buf, k_raw, v_raw, k_buf, v_buf, d_buf, y_got, s_buf, p_own, p_got, p_out,
    r_one, r_two, r_pack, r_open, key_low, key_wide, ds_buf, pr_buf, relay_buf, tally, bias, pair_acc, pair_out, pair_recv,
    pairs, in_sem, kv_got, low_got, dq_got, one_got, two_got, pack_got, give_got, swap_got, relay_got, gone,
    met, may_send,
):
    rows, width = q_buf.shape
    dim = k_buf.shape[1]
    heads = width // dim
    span = rows // 2
    seq = 2 * rows
    tile = span // 12
    bins = ((12, 4), (11, 5), (10, 6), (9, 7), (8, 3, 2, 1))
    packed = tile * len(bins)
    single = packed + tile
    units = (last - first) // 2
    held, relayed = 3, 3
    groups = -(-units // per)
    scale = 1.0 / math.sqrt(dim)
    low, full = jnp.bfloat16, jnp.float32
    me = lax.axis_index("cp")
    sec = lax.axis_index("pp")
    peer = {"cp": 1 - me}
    below = {"pp": jnp.maximum(sec - 1, 0)}
    sends, gets = sec > 0, sec < sections - 1
    tp = lax.axis_index("tp")
    early = (sec == 0) & (tp == 0)
    relays = (sec == 0) & (tp == 1 + me)
    detours = (sec == 1) & (tp == 0)
    upper, lower, every = pl.ds(0, span), pl.ds(span, span), pl.ds(0, rows)

    def remote(src, dst, recv, device):
        return pltpu.make_async_remote_copy(
            src_ref=src, dst_ref=dst, send_sem=gone.at[0], recv_sem=recv, device_id=device, device_id_type=MESH
        )

    def take(ref, sem):
        pltpu.make_async_copy(ref, ref, sem).wait()

    own = [
        pltpu.make_async_copy(keys, k_raw.at[every, :], in_sem.at[0]),
        pltpu.make_async_copy(values, v_raw.at[every, :], in_sem.at[0]),
    ]
    head, rest = pl.ds(0, dim), pl.ds(dim, width - dim)
    wide = ((query, q_buf), (grad_out, g_buf), (attn_out, o_buf))
    begin = [pltpu.make_async_copy(src.at[:, head], dst.at[:, head], in_sem.at[1]) for src, dst in wide]
    later = [pltpu.make_async_copy(src.at[:, rest], dst.at[:, rest], in_sem.at[2]) for src, dst in wide]
    table = pltpu.make_async_copy(pairs_hbm, pairs, in_sem.at[3])
    other = pl.ds(rows, rows)

    barrier = pltpu.get_barrier_semaphore()

    @pl.when(me == 1)
    def _():
        pl.semaphore_signal(barrier, inc=1, device_id=peer, device_id_type=MESH)

    @pl.when(me == 0)
    def _():
        pl.semaphore_wait(barrier, 1)
        pl.semaphore_signal(met, inc=1, device_id=peer, device_id_type=MESH)
        for src, dst in ((keys, k_raw), (values, v_raw)):
            remote(src, dst.at[other, :], kv_got.at[0], peer).start()

    for copy in own + [table] + begin:
        copy.start()

    @pl.when(me == 1)
    def _():
        take(k_raw, in_sem.at[0])
        pl.semaphore_wait(met, 1)
        for buf in (k_raw, v_raw):
            remote(buf.at[every, :], buf.at[other, :], kv_got.at[0], peer).start()

        @pl.when(gets)
        def _():
            pl.semaphore_signal(barrier, inc=1, device_id={"pp": sec + 1}, device_id_type=MESH)

        @pl.when((sec == 0) & ((tp == 1) | (tp == 2)))
        def _():
            pl.semaphore_signal(barrier, inc=1, device_id={"tp": 0}, device_id_type=MESH)

    for copy in later:
        copy.start()

    table.wait()
    row = lax.broadcasted_iota(jnp.int32, (rows, seq), 0)
    col = lax.broadcasted_iota(jnp.int32, (rows, seq), 1)
    spans = [pairs[me, 0], pairs[me, 1], pairs[1 - me, 0], pairs[1 - me, 1]]
    q_pos = jnp.where(row < span, spans[0] * span, spans[1] * span - span) + row
    bias[...] = jnp.where(col <= q_pos, 0.0, NEG)
    pair_acc[...] = jnp.zeros_like(pair_acc)
    low_here = spans[0] == 0
    high_here = spans[1] == 0
    here = low_here | high_here

    def block_of(ref, n):
        return ref[n * span:(n + 1) * span, :]

    def of_span(ref, s):
        block = block_of(ref, 0)
        for n in range(1, 4):
            block = jnp.where(spans[n] == s, block_of(ref, n), block)
        return block

    def at_span(ref, s):
        block = block_of(ref, 0)
        for n in range(1, 4):
            block = jnp.where(s == n, block_of(ref, n), block)
        return block

    @pl.when(me == 0)
    def _():
        take(k_raw, in_sem.at[0])

    take(k_raw, kv_got.at[0])
    for s in range(4):
        k_buf[pl.ds(s * span, span), :] = of_span(k_raw, s)

    half = pl.ds(pl.multiple_of(me * (span // 2), span // 2), span // 2)
    rest_half = pl.ds(pl.multiple_of((1 - me) * (span // 2), span // 2), span // 2)
    send_low = remote(k_buf.at[half, :], key_low.at[half, :], low_got.at[0], below)
    pass_low = remote(key_low.at[half, :], key_low.at[half, :], low_got.at[1], peer)

    @pl.when(sends)
    def _():
        @pl.when(me == 1)
        def _():
            pl.semaphore_wait(barrier, 1)
            pl.semaphore_signal(may_send, inc=1, device_id=peer, device_id_type=MESH)

            @pl.when(detours)
            def _():
                pl.semaphore_signal(barrier, inc=1, device_id=below, device_id_type=MESH)

        @pl.when(me == 0)
        def _():
            pl.semaphore_wait(may_send, 1)

        send_low.start()

    for s in range(4):
        v_buf[pl.ds(s * span, span), :] = of_span(v_raw, s)
    take(q_buf.at[:, pl.ds(0, 3 * dim)], in_sem.at[1])

    def dot(a, b, da, db):
        return lax.dot_general(a, b, (((da,), (db,)), ((), ())), preferred_element_type=full)

    def lanes_of(h, count=1):
        return pl.ds(h * dim if isinstance(h, int) else pl.multiple_of(h * dim, dim), count * dim)

    def lines_of(n, size, count=1):
        return pl.ds(n * size if isinstance(n, int) else pl.multiple_of(n * size, size), count * size)

    def by_core(if_one, if_zero):
        pl.when(me == 1)(if_one)
        pl.when(me == 0)(if_zero)

    def send_dq(h, lines):
        return remote(
            d_buf.at[lines, lanes_of(h)], upstream.at[lines, lanes_of(h)], dq_got.at[0], below
        )

    def unit_lanes(i):
        return lanes_of(first + 2 * i, 2)

    def unit_lines(i):
        return lines_of(i, 2 * packed)

    def group_of(i):
        return i // per if isinstance(i, int) else lax.div(i, per)

    def units_of(g):
        return min(per, units - per * g) if isinstance(g, int) else per

    def extra(g):
        return 1 if isinstance(g, int) and g == groups - 1 else 0

    def heads_of(g):
        return range(first + 2 * per * g, first + 2 * (per * g + units_of(g)))

    def group_lanes(g):
        return lanes_of(first + 2 * per * g, 2 * units_of(g) + extra(g))

    def group_lines(g):
        if extra(g):
            return pl.ds(2 * per * g * packed, 2 * units_of(g) * packed + single)
        return lines_of(per * g, 2 * packed, units_of(g))

    def send_one(i):
        at = unit_lanes(i)
        return remote(d_buf.at[upper, at], r_one.at[:, at], one_got.at[group_of(i)], below)

    alone = pl.ds(2 * units * packed, single)
    last_lanes = lanes_of(last)
    give_last_block = remote(d_buf.at[lower, last_lanes], y_got.at[:, last_lanes], give_got.at[groups - 1], peer)
    give_last_pack = remote(p_own.at[alone, :], p_got.at[alone, :], give_got.at[groups - 1], peer)

    def send_two(g):
        return remote(s_buf.at[:, group_lanes(g)], r_two.at[:, group_lanes(g)], two_got.at[g], below)

    def send_pack(g):
        return remote(p_out.at[group_lines(g), :], r_pack.at[group_lines(g), :], pack_got.at[g], below)

    def give_block(i):
        at = unit_lanes(i)
        return remote(d_buf.at[lower, at], y_got.at[:, at], give_got.at[group_of(i)], peer)

    def give_pack(i):
        at = unit_lines(i)
        return remote(p_own.at[at, :], p_got.at[at, :], give_got.at[group_of(i)], peer)

    def pass_two(g):
        return remote(r_two.at[:, group_lanes(g)], r_two.at[:, group_lanes(g)], two_got.at[g], peer)

    def pass_pack(g):
        return remote(r_pack.at[group_lines(g), :], r_pack.at[group_lines(g), :], pack_got.at[g], peer)

    def gradients(h, lines, plain=False):
        lanes = lanes_of(h)
        q = q_buf[lines, lanes]
        g = g_buf[lines, lanes]
        delta = jnp.sum(g.astype(full) * o_buf[lines, lanes].astype(full), axis=1, keepdims=True)
        score = dot(q, k_buf[...], 1, 1) * (scale * LOG2E) + bias[lines, :]
        top = jnp.max(score, axis=1, keepdims=True)
        power = jnp.exp2(score - top)
        dprob = (dot(g, v_buf[...], 1, 1) - delta) * scale
        inverse = 1.0 / jnp.sum(power, axis=1, keepdims=True)
        prob = power * inverse
        dscore = (prob * dprob).astype(low)
        place = pl.ds(
            h * rows + lines.start if isinstance(h, int) else pl.multiple_of(h * rows + lines.start, span), lines.size
        )
        pr_buf[place, :] = prob.astype(low)
        ds_buf[place, :] = dscore
        if plain:
            return dscore, dot((power * dprob).astype(low), k_buf[...], 1, 0) * inverse
        return dscore, dot(dscore, k_buf[...], 1, 0)

    def pair_terms(h, _):
        place = lines_of(h, rows)
        pair_acc[:, :dim] += dot(ds_buf[place, :], q_buf[:, lanes_of(h)], 0, 0)
        pair_acc[:, dim:] += dot(pr_buf[place, :], g_buf[:, lanes_of(h)], 0, 0)
        return 0

    def plain_pieces(pieces, before=None):
        for h, lines in pieces:
            d_buf[lines, lanes_of(h)] = gradients(h, lines, h == 0)[1].astype(low)

        @pl.when(sends)
        def _():
            if before is not None:
                before()
            for piece in pieces:
                send_dq(*piece).start()

    near, far = lanes_of(first + 2 * relayed), lanes_of(first + 2 * relayed + 1)
    at_last = one_got.at[group_of(relayed)]
    half_unit = remote(d_buf.at[upper, near], r_one.at[:, near], at_last, below)
    detour = remote(d_buf.at[upper, far], relay_buf, relay_got.at[0], {"pp": 0, "tp": 1 + me})
    relay = remote(relay_buf, r_one.at[:, far], at_last, {"tp": 0})

    def pack_head(h):
        lanes = lanes_of(h)
        dscore, dq = gradients(h, every)
        d_buf[upper, lanes] = jnp.where(low_here, dq[span:], dq[:span]).astype(low)
        d_buf[lower, lanes] = dq[span:].astype(low)
        block = jnp.where(high_here, dscore[span:, :dim].astype(full), dscore[:span, :dim].astype(full))
        lines = []
        for group in bins:
            line, at = 0.0, 0
            for n in group:
                entry = block[(n - 1) * tile:n * tile]
                line = line + (pltpu.roll(entry, at, 1) if at else entry)
                at += n * tile
            lines.append(line)
        return lines

    def unpack_head(lines):
        lane = lax.broadcasted_iota(jnp.int32, (tile, dim), 1)
        entries = {}
        for b, group in enumerate(bins):
            line, at = lines[b * tile:(b + 1) * tile], 0
            for n in group:
                entry = pltpu.roll(line, dim - at, 1) if at else line
                entries[n] = jnp.where(lane < n * tile, entry, 0.0)
                at += n * tile
        return [entries[n] for n in range(1, 13)]

    def gives(i):
        by_core(lambda: give_pack(i).start(), lambda: give_block(i).start())

    def second_sends(g):
        def two():
            at = group_lanes(g)
            take(y_got.at[:, at], give_got.at[g])
            s_buf[:, at] = jnp.where(here, y_got[:, at], d_buf[lower, at])
            send_two(g).start()

        def one():
            at = group_lines(g)
            take(p_got.at[at, :], give_got.at[g])
            p_out[at, :] = jnp.where(here, p_own[at, :], p_got[at, :])
            send_pack(g).start()

        by_core(two, one)

    def packed_unit(i, _):
        lines = pack_head(first + 2 * i) + pack_head(first + 2 * i + 1)
        p_own[unit_lines(i), :] = jnp.concatenate(lines, axis=0).astype(low)

        @pl.when(sends)
        def _():
            gives(i)

            @pl.when((i < units - held) & jnp.logical_not(detours & (i == relayed)))
            def _():
                send_one(i).start()

            @pl.when(detours & (i == relayed))
            def _():
                half_unit.start()
                pl.semaphore_wait(met, 1)
                detour.start()

            @pl.when((i > 0) & (lax.rem(i, per) == 0))
            def _():
                second_sends(group_of(i) - 1)

        return 0

    plain_pieces([(0, every)])

    @pl.when(early & (me == 1))
    def _():
        pl.semaphore_wait(barrier, 3)
        for core in range(2):
            for to in ({"tp": 1 + core, "cp": core}, {"pp": 1, "cp": core}):
                pl.semaphore_signal(met, inc=1, device_id=to, device_id_type=MESH)

    take(tally.at[pl.ds(0, 3 * rows * (heads - 1)), :], in_sem.at[2])
    lax.fori_loop(0, units, packed_unit, 0)

    lines = pack_head(last)
    p_own[alone, :] = jnp.concatenate(lines + [jnp.zeros((tile, dim), full)], axis=0).astype(low)

    @pl.when(sends)
    def _():
        by_core(give_last_pack.start, give_last_block.start)

    @pl.when(relays)
    def _():
        take(relay_buf, relay_got.at[0])
        pl.semaphore_wait(met, 1)
        relay.start()

    lax.fori_loop(0, 4, pair_terms, 0, unroll=2)

    @pl.when(sends)
    def _():
        second_sends(groups - 1)
        for g in range(group_of(units - held), groups):
            begins = max(first + 2 * per * g, last - 2 * held)
            at = lanes_of(begins, heads_of(g)[-1] + 1 + extra(g) - begins)
            remote(d_buf.at[upper, at], r_one.at[:, at], one_got.at[g], below).start()

    lax.fori_loop(4, heads, pair_terms, 0, unroll=2)

    for n in range(2):
        pair_out[lines_of(n, span), :] = at_span(pair_acc, spans[2 + n])
    swap = remote(pair_out, pair_recv, swap_got.at[0], peer)
    swap.start()

    def pass_on(g):
        def two():
            take(r_two.at[:, group_lanes(g)], two_got.at[g])
            pass_two(g).start()

        def one():
            take(r_pack.at[group_lines(g), :], pack_got.at[g])
            pass_pack(g).start()

        by_core(two, one)

    def assemble(g):
        by_core(
            lambda: take(r_pack.at[group_lines(g), :], pack_got.at[g]),
            lambda: take(r_two.at[:, group_lanes(g)], two_got.at[g]),
        )
        def open_heads(h, count, size):
            lines = r_pack[pl.ds((h - first) * packed, size), :].astype(full)
            block = []
            for n in range(count):
                block += unpack_head(lines[n * packed:(n + 1) * packed])
            both = dot(jnp.concatenate(block, axis=0).astype(low), key_wide[...], 1, 0).astype(low)
            for n in range(count):
                r_open[:, lanes_of(h + n)] = both[n * span:(n + 1) * span]

        for h in heads_of(g)[::2]:
            open_heads(h, 2, 2 * packed)
        if extra(g):
            open_heads(last, 1, single)
        at = group_lanes(g)
        take(r_one.at[:, at], one_got.at[g])
        upstream[upper, at] = jnp.where(low_here, r_open[:, at], r_one[:, at])
        upstream[lower, at] = jnp.where(low_here, r_one[:, at], jnp.where(high_here, r_open[:, at], r_two[:, at]))

    @pl.when(gets)
    def _():
        send_low.wait_recv()
        pass_low.start()
        pass_on(0)

    swap.wait_recv()
    for n in range(2):
        lines = lines_of(n, span)
        total = at_span(pair_acc, spans[n]) + pair_recv[lines, :]
        key_grad[lines, :] = total[:, :dim].astype(low)
        value_grad[lines, :] = total[:, dim:].astype(low)

    plain = first

    @pl.when(gets)
    def _():
        take(key_low.at[rest_half, :], low_got.at[1])
        key_wide[span:, :] = jnp.zeros((dim - span, dim), low)
        key_wide[:span, :] = key_low[...]
        for g in range(1, groups):
            pass_on(g)
            assemble(g - 1)
        assemble(groups - 1)

    @pl.when(jnp.logical_not(gets))
    def _():
        upstream[...] = jnp.zeros_like(upstream)

    def drain(core, sending, getting, relaying):
        two, pack = (last + 1 - first) * span, 2 * units * packed + single
        lines = 2 * rows + 4 * rows + (span if relaying else 0)
        if sending:
            lines += span // 2 + plain * rows + two + two + pack
        if getting:
            lines += span // 2 + (two if core else pack)
        take(tally.at[pl.ds(0, lines), :], gone.at[0])

    for core in range(2):
        mine = me == core
        pl.when(mine & sends & gets)(functools.partial(drain, core, True, True, False))
        pl.when(mine & jnp.logical_not(gets))(functools.partial(drain, core, True, False, False))
        pl.when(mine & relays)(functools.partial(drain, core, False, True, True))
        pl.when(mine & jnp.logical_not(sends | relays))(functools.partial(drain, core, False, True, False))

    @pl.when(gets)
    def _():
        take(upstream.at[:, lanes_of(0, plain)], dq_got.at[0])


def store(key_grad, value_grad, upstream, key_out, value_out, upstream_out, sem):
    copies = [
        pltpu.make_async_copy(src, dst, sem.at[i])
        for i, (src, dst) in enumerate(
            ((upstream, upstream_out), (key_grad, key_out), (value_grad, value_out))
        )
    ]
    for copy in copies:
        copy.start()
    for copy in copies:
        copy.wait()


def body(query, keys, values, attn_out, grad_out, span_pairs):
    _, rows, width = query.shape
    dim = keys.shape[2]
    heads = width // dim
    ranks = lax.axis_size("cp")
    sections = lax.axis_size("pp")
    seq = ranks * rows
    low, full = jnp.bfloat16, jnp.float32
    dma = pltpu.SemaphoreType.DMA
    vmem = pl.BlockSpec(memory_space=pltpu.VMEM)
    hbm = pl.BlockSpec(memory_space=pltpu.HBM)

    def spaces(*shapes):
        return [pltpu.VMEM(shape, low) for shape in shapes]

    tall, flat, block = (rows, width), (seq, dim), (rows // 2, width)
    if ranks == 2 and lax.axis_size("tp") > 2 and sections > 1 and dim == 128 and rows == 192 and heads == 16:
        groups, packs = 3, ((heads - 2) * (5 * rows // 24) + rows // 4, dim)
        run = functools.partial(pair_kernel, sections, 1, heads - 1, groups)
        scratch = (
            spaces(tall, tall, tall, flat, flat, flat, flat, tall, block, block, packs, packs, packs)
            + spaces(block, block, packs, block, (rows // 2, dim), (dim, dim))
            + spaces((heads * rows, seq), (heads * rows, seq), (rows // 2, dim), (3 * heads * rows, dim))
            + [
                pltpu.VMEM((rows, seq), full),
                pltpu.VMEM((seq, 2 * dim), full),
                pltpu.VMEM((rows, 2 * dim), full),
                pltpu.VMEM((rows, 2 * dim), full),
                pltpu.SMEM((ranks, 2), jnp.int32),
            ]
            + [dma((n,)) for n in (4, 1, 2, 1, groups, groups, groups, groups, 1, 1, 1)]
            + [pltpu.SemaphoreType.REGULAR] * 2
        )
    else:
        others = max(ranks - 1, 1)
        run = functools.partial(kernel, ranks, sections, 2 * rows if ranks % 2 == 0 else rows)
        scratch = (
            spaces(tall, tall, tall, flat, flat, tall)
            + [
                pltpu.VMEM((rows, seq), full),
                pltpu.VMEM((2, rows, 1), full),
                pltpu.VMEM((rows, dim), full),
                pltpu.VMEM((seq, 2 * dim), full),
                pltpu.VMEM((others, rows, 2 * dim), full),
                pltpu.SMEM((ranks, 2), jnp.int32),
            ]
            + [dma((9,)), dma((2, others)), dma((2, others)), dma((heads + 1,)), dma((heads + 1,))]
            + [dma((others,)), dma((others,))]
        )
    key_grad, value_grad, upstream = pl.pallas_call(
        run,
        out_shape=(
            pltpu.VMEM((rows, dim), low),
            pltpu.VMEM((rows, dim), low),
            pltpu.VMEM((rows, width), low),
        ),
        in_specs=[hbm] * 6,
        out_specs=(vmem, vmem, vmem),
        scratch_shapes=scratch,
        compiler_params=pltpu.CompilerParams(
            collective_id=0, has_side_effects=True, vmem_limit_bytes=64 * 1024 * 1024 - 1200 * 1024
        ),
        name="backward",
    )(span_pairs, query[0], keys[0], values[0], attn_out[0], grad_out[0])
    anywhere = pl.BlockSpec(memory_space=pl.ANY)
    key_grad, value_grad, upstream = pl.pallas_call(
        store,
        out_shape=(
            jax.ShapeDtypeStruct((rows, dim), low),
            jax.ShapeDtypeStruct((rows, dim), low),
            jax.ShapeDtypeStruct((rows, width), low),
        ),
        in_specs=[anywhere] * 3,
        out_specs=(anywhere,) * 3,
        scratch_shapes=[dma((3,))],
        compiler_params=pltpu.CompilerParams(vmem_limit_bytes=1024 * 1024),
        name="store",
    )(key_grad, value_grad, upstream)
    return key_grad[None], value_grad[None], upstream[None]


def solution(mesh):
    spec = P("pp", "cp", "tp")
    return jax.shard_map(
        body,
        mesh=mesh,
        in_specs=(spec, spec, spec, spec, spec, P()),
        out_specs=(spec, spec, spec),
        check_vma=False,
    )
```
